32 devices in a mesh: batch: 16 (over z, y, core), head: 2 (over x).
Axes of the slice: x: 2, y: 2, z: 4, core: 2. Of those that a mesh axis runs over, the one named last changes fastest.
Arguments:
- tokens: bfloat16 [14336, 1024], P('batch', 'head'), may hold values from -6 to 6
- ln_gain: float32 [1024], replicated, may hold values from 0.5 to 1.5
- w_qkv: bfloat16 [1024, 3072], P(None, 'head'), may hold values from -0.1875 to 0.1875
- qk_gain: float32 [2, 64], replicated, may hold values from 1 to 1.7
- w_out: bfloat16 [1024, 1024], P('head'), may hold values from -1 to 1
- w_up: bfloat16 [1024, 4096], P(None, 'head'), may hold values from -0.1875 to 0.1875
- b_up: float32 [4096], P('head'), may hold values from -3 to 3
- w_down: bfloat16 [4096, 1024], P('head'), may hold values from -0.09375 to 0.09375
- b_out: float32 [1024], P('head'), may hold values from -3 to 3
- cotangent: bfloat16 [14336, 1024], P('batch', 'head'), may hold values from -6 to 6
- slot_image: int32 [64], P('batch'), may hold values from 0 to 3, as said below
- token_valid: int32 [14336], P('batch'), may hold values from 0 to 1, as said below
Outputs:
- output: bfloat16 [14336, 1024], P('batch', 'head')
- grad_tokens: bfloat16 [14336, 1024], P('batch', 'head')
- grad_ln_gain: float32 [1024], P('head')
- grad_w_qkv: float32 [1024, 3072], P(None, 'head')
- grad_qk_gain: float32 [2, 64], replicated
- grad_w_out: float32 [1024, 1024], P('head')
- grad_w_up: float32 [1024, 4096], P(None, 'head')
- grad_b_up: float32 [4096], P('head')
- grad_w_down: float32 [4096, 1024], P('head')
- grad_b_out: float32 [1024], P('head')
The draws below stay inside these ranges and needn't reach their ends.
Inputs may be any that keep to these rules, and one draw needn't show every extreme that they name: `slot_image`: within each group of 4 slots the image numbers start at 0, never fall, and rise by one from slot to slot, except that a long image takes the first 3 slots of some groups (at least one group in every draw); every other image takes one slot. `token_valid`: in each slot the valid rows come first; a long image has all of its 672 rows valid; a one-slot image has 112 to 196 valid rows, and the first one-slot image of every group has exactly 196.
All inputs are finite; a program needn't handle non-finite values.
Results may differ from the reference program's by a relative error of at most 0.012.
Values may be sent and summed in bfloat16 or wider, within the bound.
No kernel may reach another device: no remote copies, remote signals or barrier semaphores. Data moves between devices by JAX's collectives and lax.ppermute only.
A program may use at most 192 MiB of HBM per device.

```python
import jax
import jax.numpy as jnp
from jax import lax

D = 1024
HEADS = 16
HD = 64
FF = 4096
SLOT = 224
LONG_SLOTS = 3
SLOTS_DEV = 4
TOK_DEV = 896
TOKENS = 14336
KEY_BLOCKS = 1
SHORT_MOST = 196
N_BATCH = 16


def slot_layout(key):
    base = jax.random.fold_in(key, 11)
    key_forced, key_choose, key_length = jax.random.split(base, 3)
    forced = jax.random.randint(key_forced, (), 0, N_BATCH)
    long_draw = jax.random.randint(key_choose, (N_BATCH,), 0, 8)
    devices = jnp.arange(N_BATCH)
    has_long = (long_draw == 0) | (devices == forced)
    slot_index = jnp.arange(SLOTS_DEV)[None, :]
    image_ids = jnp.where(has_long[:, None], jnp.where(slot_index < LONG_SLOTS, 0, slot_index - LONG_SLOTS + 1), slot_index)
    lengths = jax.random.randint(key_length, (N_BATCH, SLOTS_DEV), SLOT // 2, SHORT_MOST + 1)
    first_short = jnp.where(has_long, LONG_SLOTS, 0)
    lengths = jnp.where(slot_index == first_short[:, None], SHORT_MOST, lengths)
    lengths = jnp.where(has_long[:, None] & (slot_index < LONG_SLOTS), SLOT, lengths)
    return (image_ids.astype(jnp.int32), lengths.astype(jnp.int32))


def draw_slot_image(key, part):
    image_ids, lengths = slot_layout(key)
    return image_ids.reshape(-1)


def draw_token_valid(key, part):
    image_ids, lengths = slot_layout(key)
    position = jnp.arange(SLOT)
    return (position[None, None, :] < lengths[:, :, None]).astype(jnp.int32).reshape(-1)


def block_levels(stream_key, dims, cuts, least, top_value):
    level, own = 1.0, jax.random.fold_in(stream_key, 6)
    for dim, blocks in cuts:
        heights = jnp.exp(jax.random.uniform(jax.random.fold_in(own, dim), (blocks,), jnp.float32, least / len(cuts), top_value / len(cuts)))
        level = level * jnp.repeat(heights, dims[dim] // blocks).reshape([-1 if axis == dim else 1 for axis in range(len(dims))])
    return level


def noise(key, dims, deviation, reach, pieces=(), held_as=jnp.bfloat16):
    level = block_levels(key, dims, pieces, -0.22, 0.18) if pieces else 1.0
    values = jax.random.normal(key, dims, jnp.float32) * deviation * level
    return jnp.minimum(jnp.maximum(values, -reach), reach).astype(held_as)


def setup_inputs(seed: int = 0) -> dict:
    arg_keys = jax.random.split(jax.random.key(seed), 13)
    return {
        "tokens": noise(arg_keys[0], (TOKENS, D), 1.0, 6.0, ((0, 16), (1, 2))),
        "ln_gain": jnp.clip(1.0 + 0.1 * jax.random.normal(arg_keys[1], (D,), jnp.float32), 0.5, 1.5),
        "w_qkv": noise(arg_keys[2], (D, 3 * D), D ** -0.5, 0.1875, ((1, 2),)),
        "qk_gain": jnp.clip(jax.random.uniform(arg_keys[3], (2, HD), jnp.float32, 1.0, 1.7), 1.0, 1.7),
        "w_out": noise(arg_keys[4], (D, D), (D // 32) ** -0.5, 1.0, ((0, 2),)),
        "w_up": noise(arg_keys[5], (D, FF), D ** -0.5, 0.1875, ((1, 2),)),
        "b_up": noise(arg_keys[6], (FF,), 0.5, 3.0, ((0, 2),), jnp.float32),
        "w_down": noise(arg_keys[7], (FF, D), FF ** -0.5, 0.09375, ((0, 2),)),
        "b_out": noise(arg_keys[8], (D,), 0.5, 3.0, ((0, 2),), jnp.float32),
        "cotangent": noise(arg_keys[9], (TOKENS, D), 1.0, 6.0, ((0, 16), (1, 2))),
        "slot_image": draw_slot_image(jax.random.fold_in(arg_keys[12], 71), 0),
        "token_valid": draw_token_valid(jax.random.fold_in(arg_keys[12], 71), 0),
    }


EPSILON = 1e-06

@jax.custom_vjp
def low(v):
    return lax.optimization_barrier(v.astype(jnp.bfloat16)).astype(jnp.float32)

@jax.custom_vjp
def low_back(v):
    return v

def low_keep(v):
    return (low(v), None)

def low_pass(kept, grad):
    return (grad,)

def back_keep(v):
    return (v, None)

def back_low(kept, grad):
    return (low(grad),)
low.defvjp(low_keep, low_pass)
low_back.defvjp(back_keep, back_low)

def product(left, right):
    return jnp.dot(left, right, precision=lax.Precision.HIGHEST, preferred_element_type=jnp.float32)

def layer_norm(values, gain):
    center = lax.optimization_barrier(jnp.mean(values, axis=-1, keepdims=True))
    shifted = values - center
    spread = lax.optimization_barrier(jnp.mean(shifted * shifted, axis=-1, keepdims=True))
    return shifted * lax.rsqrt(spread + EPSILON) * gain

def attention(query, key_rows, value_rows, token_image, usable_key):
    block_rows = 4 * SLOT
    window = KEY_BLOCKS * block_rows
    block_count = TOK_DEV // block_rows
    factor = float(HD) ** (-0.5)
    query_groups = query.reshape(N_BATCH, TOK_DEV, HEADS, HD)
    key_groups = key_rows.reshape(N_BATCH, TOK_DEV, HEADS, HD)
    value_groups = value_rows.reshape(N_BATCH, TOK_DEV, HEADS, HD)
    image_groups = token_image.reshape(N_BATCH, TOK_DEV)
    usable_groups = usable_key.reshape(N_BATCH, TOK_DEV)

    def one_group(operands):
        group_query, group_key, group_value, group_image, group_usable = operands

        def one_block(block_index):
            row_start = block_index * block_rows
            key_start = jnp.maximum(block_index - KEY_BLOCKS + 1, 0) * block_rows
            query_block = lax.dynamic_slice_in_dim(group_query, row_start, block_rows, 0)
            key_block = lax.dynamic_slice_in_dim(group_key, key_start, window, 0)
            value_block = lax.dynamic_slice_in_dim(group_value, key_start, window, 0)
            query_image = lax.dynamic_slice_in_dim(group_image, row_start, block_rows, 0)
            key_image = lax.dynamic_slice_in_dim(group_image, key_start, window, 0)
            key_usable = lax.dynamic_slice_in_dim(group_usable, key_start, window, 0)
            scores = low_back(jnp.einsum('qhe,khe->hqk', query_block, key_block, precision=lax.Precision.HIGHEST) * factor)
            allowed = (query_image[:, None] == key_image[None, :]) & key_usable[None, :]
            scores = jnp.where(allowed[None], scores, -1e+30)
            weights = jax.nn.softmax(scores, axis=-1)
            return jnp.einsum('hqk,khe->qhe', low(weights), value_block, precision=lax.Precision.HIGHEST)
        blocks = lax.map(jax.checkpoint(one_block), jnp.arange(block_count, dtype=jnp.int32))
        return blocks.reshape(TOK_DEV, HEADS, HD)
    result = lax.map(one_group, (query_groups, key_groups, value_groups, image_groups, usable_groups))
    return result.reshape(TOKENS, HEADS, HD)

def forward(tokens, ln_gain, w_qkv, qk_gain, w_out, w_up, b_up, w_down, b_out, token_image, usable_key):
    normed = low(layer_norm(tokens, ln_gain))
    joined = low_back(product(normed, w_qkv)).reshape(TOKENS, HEADS, 3, HD)
    query = low(layer_norm(joined[:, :, 0], qk_gain[0]))
    key_rows = low(layer_norm(joined[:, :, 1], qk_gain[1]))
    value_rows = low(joined[:, :, 2])
    attended = attention(query, key_rows, value_rows, token_image, usable_key).reshape(TOKENS, D)
    attended_low = low_back(low(attended))
    pre_gate = low_back(product(normed, w_up) + b_up)
    hidden = low(jax.nn.gelu(pre_gate, approximate=False))
    return tokens + product(attended_low, w_out) + product(hidden, w_down) + b_out

def reference(tokens, ln_gain, w_qkv, qk_gain, w_out, w_up, b_up, w_down, b_out, cotangent, slot_image, token_valid):
    token_image = jnp.repeat(slot_image, SLOT, total_repeat_length=TOKENS)
    usable_key = token_valid == 1
    floats = tuple((item.astype(jnp.float32) for item in (tokens, ln_gain, w_qkv, qk_gain, w_out, w_up, b_up, w_down, b_out)))

    def apply_block(*operands):
        return forward(*operands, token_image, usable_key)
    result, backward = jax.vjp(apply_block, *floats)
    grads = backward(cotangent.astype(jnp.float32))
    return (result.astype(jnp.bfloat16), grads[0].astype(jnp.bfloat16), grads[1], grads[2], grads[3], grads[4], grads[5], grads[6], grads[7], grads[8])
```

```python
import functools

import jax
import jax.numpy as jnp
from jax import lax
from jax.experimental import pallas as pl
from jax.experimental.pallas import tpu as pltpu
from jax.sharding import PartitionSpec as P

HD = 64
EPSILON = 1e-06
FAR = -16384.0
LOW = jnp.bfloat16
WIDE = jnp.float32
MIB = 1024 * 1024


def contract(left, right, left_dim, right_dim):
    return lax.dot_general(
        left, right, (((left_dim,), (right_dim,)), ((), ())), preferred_element_type=WIDE
    )


def swap(values, axis):
    return lax.ppermute(values, axis, [(0, 1), (1, 0)])


def both_halves(mine, other, first, dim):
    return jnp.where(
        first,
        jnp.concatenate([mine, other], axis=dim),
        jnp.concatenate([other, mine], axis=dim),
    )


def mlp_body(normed_ref, w_ref, b_ref, hidden_ref, slope_ref):
    pre = jnp.dot(normed_ref[...], w_ref[...], preferred_element_type=WIDE) + b_ref[...]
    cdf = 0.5 * (1.0 + lax.erf(pre * (0.5**0.5)))
    density = jnp.exp(-0.5 * pre * pre) * 0.3989422804014327
    hidden_ref[...] = (pre * cdf).astype(LOW)
    slope_ref[...] = (cdf + pre * density).astype(LOW)


def mlp_forward(normed, w_up, b_up):
    rows, width = normed.shape
    units = w_up.shape[1]
    block = 256
    return pl.pallas_call(
        mlp_body,
        grid=(units // block,),
        in_specs=[
            pl.BlockSpec((rows, width), lambda i: (0, 0)),
            pl.BlockSpec((width, block), lambda i: (0, i)),
            pl.BlockSpec((1, block), lambda i: (0, i)),
        ],
        out_specs=[
            pl.BlockSpec((rows, block), lambda i: (0, i)),
            pl.BlockSpec((rows, block), lambda i: (0, i)),
        ],
        out_shape=[
            jax.ShapeDtypeStruct((rows, units), LOW),
            jax.ShapeDtypeStruct((rows, units), LOW),
        ],
        compiler_params=pltpu.CompilerParams(vmem_limit_bytes=16 * MIB),
        cost_estimate=pl.CostEstimate(
            flops=2 * rows * width * units,
            bytes_accessed=2 * (rows * width + width * units + 2 * rows * units),
            transcendentals=2 * rows * units,
        ),
        name="mlp_forward",
    )(normed, w_up, b_up.reshape(1, units))


def norm_body(side_ref, mine_ref, other_ref, gain_ref, normed_ref, stats_ref):
    mine = mine_ref[...].astype(WIDE)
    other = other_ref[...].astype(WIDE)
    width = 2 * mine.shape[1]
    half = mine.shape[1]
    center = (
        jnp.sum(mine, axis=1, keepdims=True) + jnp.sum(other, axis=1, keepdims=True)
    ) / width
    mine = mine - center
    other = other - center
    spread = (
        jnp.sum(mine * mine, axis=1, keepdims=True)
        + jnp.sum(other * other, axis=1, keepdims=True)
    ) / width
    scaled = lax.rsqrt(spread + EPSILON)
    first = side_ref[0] == 0
    left = jnp.where(first, mine, other)
    right = jnp.where(first, other, mine)
    normed_ref[:, 0:half] = (left * scaled * gain_ref[:, 0:half]).astype(LOW)
    normed_ref[:, half:width] = (right * scaled * gain_ref[:, half:width]).astype(LOW)
    lane = lax.broadcasted_iota(jnp.int32, stats_ref.shape, 1)
    stats_ref[...] = jnp.where(lane == 0, center, scaled)


def input_norm(side, mine, other, gain):
    rows, half = mine.shape
    block = 224
    return pl.pallas_call(
        norm_body,
        grid_spec=pltpu.PrefetchScalarGridSpec(
            num_scalar_prefetch=1,
            grid=(rows // block,),
            in_specs=[
                pl.BlockSpec((block, half), lambda i, s: (i, 0)),
                pl.BlockSpec((block, half), lambda i, s: (i, 0)),
                pl.BlockSpec((1, 2 * half), lambda i, s: (0, 0)),
            ],
            out_specs=[
                pl.BlockSpec((block, 2 * half), lambda i, s: (i, 0)),
                pl.BlockSpec((block, 128), lambda i, s: (i, 0)),
            ],
        ),
        out_shape=[
            jax.ShapeDtypeStruct((rows, 2 * half), LOW),
            jax.ShapeDtypeStruct((rows, 128), WIDE),
        ],
        cost_estimate=pl.CostEstimate(
            flops=20 * rows * half, bytes_accessed=10 * rows * half, transcendentals=rows
        ),
        name="input_norm",
    )(side, mine, other, gain.reshape(1, 2 * half))


def slope_body(piece_ref, w_ref, slope_ref, grad_pre_ref, bias_ref):
    back = lax.dot_general(
        piece_ref[...], w_ref[...], (((1,), (1,)), ((), ())), preferred_element_type=WIDE
    )
    low = (back * slope_ref[...].astype(WIDE)).astype(LOW)
    grad_pre_ref[...] = low
    bias_ref[...] = jnp.sum(low.astype(WIDE), axis=0, keepdims=True)


def mlp_slope(piece, w_down, slope):
    rows, width = piece.shape
    units = w_down.shape[0]
    block = 256
    return pl.pallas_call(
        slope_body,
        grid=(units // block,),
        in_specs=[
            pl.BlockSpec((rows, width), lambda i: (0, 0)),
            pl.BlockSpec((block, width), lambda i: (i, 0)),
            pl.BlockSpec((rows, block), lambda i: (0, i)),
        ],
        out_specs=[
            pl.BlockSpec((rows, block), lambda i: (0, i)),
            pl.BlockSpec((1, block), lambda i: (0, i)),
        ],
        out_shape=[
            jax.ShapeDtypeStruct((rows, units), LOW),
            jax.ShapeDtypeStruct((1, units), WIDE),
        ],
        compiler_params=pltpu.CompilerParams(vmem_limit_bytes=16 * MIB),
        cost_estimate=pl.CostEstimate(
            flops=2 * rows * width * units,
            bytes_accessed=2 * (rows * width + width * units + 2 * rows * units),
            transcendentals=0,
        ),
        name="mlp_slope",
    )(piece, w_down, slope)


def first_dims(left, right):
    return lax.dot_general(left, right, (((0,), (0,)), ((), ())), preferred_element_type=WIDE)


def mlp_weights_body(down_steps, hidden_ref, piece_ref, normed_ref, grad_pre_ref, out_ref):
    step = pl.program_id(0)

    @pl.when(step < down_steps)
    def _():
        out_ref[...] = first_dims(hidden_ref[...], piece_ref[...]).astype(LOW)

    @pl.when(step >= down_steps)
    def _():
        out_ref[...] = first_dims(normed_ref[...], grad_pre_ref[...]).astype(LOW)


def mlp_weights(hidden, piece, normed, grad_pre):
    rows, units = hidden.shape
    width = piece.shape[1]
    block = 512
    down = units // block
    across = width // block
    halves = units // width

    def later(i):
        return jnp.maximum(i - down, 0)

    return pl.pallas_call(
        functools.partial(mlp_weights_body, down),
        grid=(down + halves * across,),
        in_specs=[
            pl.BlockSpec((rows, block), lambda i: (0, jnp.minimum(i, down - 1))),
            pl.BlockSpec((rows, width), lambda i: (0, 0)),
            pl.BlockSpec((rows, block), lambda i: (0, later(i) % across)),
            pl.BlockSpec((rows, width), lambda i: (0, later(i) // across)),
        ],
        out_specs=pl.BlockSpec((block, width), lambda i: (i, 0)),
        out_shape=pltpu.HBM((2 * units, width), LOW),
        compiler_params=pltpu.CompilerParams(vmem_limit_bytes=24 * MIB),
        cost_estimate=pl.CostEstimate(
            flops=4 * rows * width * units,
            bytes_accessed=2 * (2 * rows * width + 2 * rows * units + 2 * width * units),
            transcendentals=0,
        ),
        name="mlp_weights",
    )(hidden, piece, normed, grad_pre)


def heads_weights_body(normed_ref, grad_joined_ref, piece_ref, attended_ref, out_ref):
    columns = grad_joined_ref.shape[1]
    out_ref[:, 0:columns] = first_dims(normed_ref[...], grad_joined_ref[...]).astype(LOW)
    out_ref[:, columns:] = lax.dot_general(
        piece_ref[...], attended_ref[...], (((0,), (1,)), ((), ())), preferred_element_type=WIDE
    ).astype(LOW)


def heads_weights(normed, grad_joined, piece, attended_t):
    rows, width = normed.shape
    columns, inner = grad_joined.shape[1], attended_t.shape[0]
    block = 256
    return pl.pallas_call(
        heads_weights_body,
        grid=(width // block,),
        in_specs=[
            pl.BlockSpec((rows, block), lambda i: (0, i)),
            pl.BlockSpec((rows, columns), lambda i: (0, 0)),
            pl.BlockSpec((rows, block), lambda i: (0, i)),
            pl.BlockSpec((inner, rows), lambda i: (0, 0)),
        ],
        out_specs=pl.BlockSpec((block, columns + inner), lambda i: (i, 0)),
        out_shape=jax.ShapeDtypeStruct((width, columns + inner), LOW),
        compiler_params=pltpu.CompilerParams(vmem_limit_bytes=16 * MIB),
        cost_estimate=pl.CostEstimate(
            flops=2 * rows * width * (columns + inner),
            bytes_accessed=2 * (2 * rows * width + (rows + width) * (columns + inner)),
            transcendentals=0,
        ),
        name="heads_weights",
    )(normed, grad_joined, piece, attended_t)


def spread_body(columns, mlp_ref, *refs):
    heads_refs, (down_ref, up_ref, qkv_ref, out_ref) = refs[:-4], refs[-4:]
    step = pl.program_id(0)
    steps = pl.num_programs(0)

    @pl.when(step < steps // 2)
    def _():
        down_ref[...] = mlp_ref[...].astype(WIDE).reshape(down_ref.shape)

    @pl.when(step >= steps // 2)
    def _():
        up_ref[...] = mlp_ref[...].astype(WIDE).reshape(up_ref.shape)

    for number, ref in enumerate(heads_refs):
        value = ref[...].astype(WIDE).reshape(qkv_ref.shape[0], -1)
        inner = value.shape[1] - columns
        qkv_ref[:, columns * number : columns * (number + 1)] = value[:, 0:columns]
        out_ref[inner * number : inner * (number + 1), :] = jnp.transpose(value[:, columns:])


def spread(whole, n, units, columns, count):
    width = whole.shape[1]
    mlp_rows, heads_rows = 2 * units // n, width // n
    assert whole.shape[0] == n * (mlp_rows + count * heads_rows)
    steps = width // 128
    block = 2 * units // steps
    inner = width - columns
    across = 2 * width // block // 2

    def later(i):
        return jnp.maximum(i - steps // 2, 0)

    def heads_spec(number):
        skip = mlp_rows // heads_rows + number
        return pl.BlockSpec((n // steps, 1, heads_rows, width), lambda i: (i, skip, 0, 0))

    by_rows = whole.reshape(n, -1, width)
    by_parts = whole.reshape(n, -1, heads_rows, width)
    return pl.pallas_call(
        functools.partial(spread_body, columns),
        grid=(steps,),
        in_specs=[pl.BlockSpec((n // steps, mlp_rows, width), lambda i: (i, 0, 0))]
        + [heads_spec(number) for number in range(count)],
        out_specs=[
            pl.BlockSpec((block, width), lambda i: (jnp.minimum(i, steps // 2 - 1), 0)),
            pl.BlockSpec((block, width), lambda i: (later(i) % across, later(i) // across)),
            pl.BlockSpec((128, columns * count), lambda i: (i, 0)),
            pl.BlockSpec((inner * count, 128), lambda i: (0, i)),
        ],
        out_shape=[
            jax.ShapeDtypeStruct((units, width), WIDE),
            jax.ShapeDtypeStruct((width, units), WIDE),
            jax.ShapeDtypeStruct((width, columns * count), WIDE),
            jax.ShapeDtypeStruct((inner * count, width), WIDE),
        ],
        compiler_params=pltpu.CompilerParams(vmem_limit_bytes=32 * MIB),
        cost_estimate=pl.CostEstimate(
            flops=whole.size, bytes_accessed=6 * whole.size, transcendentals=0
        ),
        name="spread",
    )(by_rows, *[by_parts] * count)


def output_body(mine, side_ref, attended_ref, w_out_ref, hidden_ref, w_down_ref, *refs):
    total = jnp.dot(hidden_ref[...], w_down_ref[...], preferred_element_type=WIDE) + first_dims(
        attended_ref[...], w_out_ref[...]
    )
    if mine:
        tokens_ref, arrived_ref, bias_ref, out_ref = refs
        total = (
            tokens_ref[...].astype(WIDE) + (total + arrived_ref[...].astype(WIDE)) + bias_ref[...]
        )
    else:
        (out_ref,) = refs
    out_ref[...] = total.astype(LOW)


def output_half(mine, side, attended_t, w_out, hidden, w_down, *more):
    inner, rows = attended_t.shape
    units, width = w_down.shape
    half = width // 2
    block = rows
    flip = 0 if mine else 1

    def column(i, s):
        return (0, s[0] ^ flip)

    extra = []
    if mine:
        extra = [
            pl.BlockSpec((block, half), lambda i, s: (i, 0)),
            pl.BlockSpec((block, half), lambda i, s: (i, 0)),
            pl.BlockSpec((1, half), lambda i, s: (0, 0)),
        ]
    return pl.pallas_call(
        functools.partial(output_body, mine),
        grid_spec=pltpu.PrefetchScalarGridSpec(
            num_scalar_prefetch=1,
            grid=(rows // block,),
            in_specs=[
                pl.BlockSpec((inner, block), lambda i, s: (0, i)),
                pl.BlockSpec((inner, half), column),
                pl.BlockSpec((block, units), lambda i, s: (i, 0)),
                pl.BlockSpec((units, half), column),
                *extra,
            ],
            out_specs=pl.BlockSpec((block, half), lambda i, s: (i, 0)),
        ),
        out_shape=jax.ShapeDtypeStruct((rows, half), LOW),
        compiler_params=pltpu.CompilerParams(vmem_limit_bytes=20 * MIB),
        cost_estimate=pl.CostEstimate(
            flops=2 * rows * half * (inner + units),
            bytes_accessed=2 * (rows + half) * (inner + units) + 6 * rows * half,
            transcendentals=0,
        ),
        name="output_mine" if mine else "output_away",
    )(side, attended_t, w_out, hidden, w_down, *more)


def second_dims(left, right):
    return lax.dot_general(left, right, (((1,), (1,)), ((), ())), preferred_element_type=WIDE)


def grad_in_body(mine, side_ref, grad_joined_ref, w_qkv_ref, grad_pre_ref, w_up_ref, *refs):
    total = second_dims(grad_joined_ref[...], w_qkv_ref[...]) + second_dims(
        grad_pre_ref[...], w_up_ref[...]
    )
    if not mine:
        (away_ref,) = refs
        away_ref[...] = total.astype(LOW)
        return
    tokens_ref, arrived_ref, stats_ref, gain_ref, hat_ref, sums_ref, gain_grad_ref = refs
    total = total + arrived_ref[...].astype(WIDE)
    x_hat = (tokens_ref[...].astype(WIDE) - stats_ref[:, 0:1]) * stats_ref[:, 1:2]
    grad_hat = total * gain_ref[...]
    hat_ref[...] = grad_hat
    lane = lax.broadcasted_iota(jnp.int32, sums_ref.shape, 1)
    sums_ref[...] = jnp.where(
        lane == 0,
        jnp.sum(grad_hat, axis=1, keepdims=True),
        jnp.sum(grad_hat * x_hat, axis=1, keepdims=True),
    )
    gain_grad_ref[...] = jnp.sum(total * x_hat, axis=0, keepdims=True)


def grad_in_half(mine, side, grad_joined, w_qkv, grad_pre, w_up, *more):
    rows, columns = grad_joined.shape
    width, units = w_up.shape
    half = width // 2
    flip = 0 if mine else 1

    def picked(i, s):
        return (s[0] ^ flip, 0)

    def whole(i, s):
        return (0, 0)

    extra, outs = [], [((rows, half), LOW)]
    if mine:
        extra = [
            pl.BlockSpec((rows, half), whole),
            pl.BlockSpec((rows, half), whole),
            pl.BlockSpec((rows, 128), whole),
            pl.BlockSpec((1, half), lambda i, s: (0, s[0])),
        ]
        outs = [((rows, half), WIDE), ((rows, 128), WIDE), ((1, half), WIDE)]
    return pl.pallas_call(
        functools.partial(grad_in_body, mine),
        grid_spec=pltpu.PrefetchScalarGridSpec(
            num_scalar_prefetch=1,
            grid=(1,),
            in_specs=[
                pl.BlockSpec((rows, columns), whole),
                pl.BlockSpec((half, columns), picked),
                pl.BlockSpec((rows, units), whole),
                pl.BlockSpec((half, units), picked),
                *extra,
            ],
            out_specs=[pl.BlockSpec(shape, whole) for shape, _ in outs],
        ),
        out_shape=[jax.ShapeDtypeStruct(shape, kind) for shape, kind in outs],
        compiler_params=pltpu.CompilerParams(vmem_limit_bytes=28 * MIB),
        cost_estimate=pl.CostEstimate(
            flops=2 * rows * half * (columns + units),
            bytes_accessed=2 * (rows + half) * (columns + units) + 10 * rows * half,
            transcendentals=0,
        ),
        name="grad_in_mine" if mine else "grad_in_away",
    )(side, grad_joined, w_qkv, grad_pre, w_up, *more)


def finish_body(cotangent_ref, tokens_ref, stats_ref, hat_ref, sums_ref, other_ref, out_ref):
    width = 2 * tokens_ref.shape[1]
    scaled = stats_ref[:, 1:2]
    x_hat = (tokens_ref[...].astype(WIDE) - stats_ref[:, 0:1]) * scaled
    sums = (sums_ref[:, 0:2] + other_ref[...]) / width
    out_ref[...] = (
        cotangent_ref[...].astype(WIDE)
        + scaled * (hat_ref[...] - sums[:, 0:1] - x_hat * sums[:, 1:2])
    ).astype(LOW)


def grad_in_finish(cotangent, tokens, stats, hat, sums, other):
    rows, half = tokens.shape
    block = 224

    def rows_of(columns):
        return pl.BlockSpec((block, columns), lambda i: (i, 0))

    return pl.pallas_call(
        finish_body,
        grid=(rows // block,),
        in_specs=[rows_of(c) for c in (half, half, 128, half, 128, 2)],
        out_specs=rows_of(half),
        out_shape=jax.ShapeDtypeStruct((rows, half), LOW),
        cost_estimate=pl.CostEstimate(
            flops=10 * rows * half, bytes_accessed=10 * rows * half, transcendentals=0
        ),
        name="grad_in_finish",
    )(cotangent, tokens, stats, hat, sums, other)


def part_norm(values):
    center = jnp.mean(values, axis=0, keepdims=True)
    shifted = values - center
    scaled = lax.rsqrt(jnp.mean(shifted * shifted, axis=0, keepdims=True) + EPSILON)
    return shifted * scaled, scaled


def part_norm_back(grad, normal, scaled, gain):
    g = grad * gain
    inner = jnp.mean(g * normal, axis=0, keepdims=True)
    return scaled * (g - jnp.mean(g, axis=0, keepdims=True) - normal * inner)


def lane_fold(values):
    total = values[:, 0:128]
    for start in range(128, values.shape[1], 128):
        total = total + values[:, start : start + 128]
    return total


def attention_body(rows, tiles, joined_ref, grad_ref, gain_ref, query_mark_ref, key_mark_ref,
                   attended_ref, grad_joined_ref, gain_grad_ref, key_grad, value_grad):
    factor = float(HD) ** (-0.5)
    gain_query = gain_ref[0:HD, :]
    gain_key = gain_ref[HD : 2 * HD, :]
    pieces = []
    gain_sum_query = jnp.zeros((HD, 128), WIDE)
    gain_sum_key = jnp.zeros((HD, 128), WIDE)
    one_mark = jnp.where(lax.broadcasted_iota(jnp.int32, (HD, rows), 0) < 2, 1.0, 0.0).astype(LOW)
    for head in range(2):
        base = head * 3 * HD
        query_hat, query_scale = part_norm(joined_ref[base : base + HD, :])
        key_hat, key_scale = part_norm(joined_ref[base + HD : base + 2 * HD, :])
        value_t = joined_ref[base + 2 * HD : base + 3 * HD, :].astype(LOW)
        query_t = (query_hat * gain_query).astype(LOW)
        key_t = (key_hat * gain_key).astype(LOW)
        grad_t = grad_ref[head * HD : (head + 1) * HD, :]
        query_aug = jnp.concatenate([query_t * factor, query_mark_ref[...]], axis=0)
        key_aug = jnp.transpose(jnp.concatenate([key_t, key_mark_ref[...]], axis=0))
        value_aug_t = jnp.concatenate([value_t, one_mark], axis=0)
        value_aug = jnp.transpose(value_aug_t)
        query_grads = []
        for number, (q0, q1, k0, k1) in enumerate(tiles):
            scores = jnp.dot(key_aug[k0:k1], query_aug[:, q0:q1], preferred_element_type=WIDE)
            terms = jnp.exp(scores)
            terms_low = terms.astype(LOW)
            summed = jnp.dot(value_aug_t[:, k0:k1], terms_low, preferred_element_type=WIDE)
            inverse = 1.0 / summed[HD : HD + 1, :]
            attended = summed[0:HD, :] * inverse
            attended_ref[head * HD : (head + 1) * HD, q0:q1] = attended.astype(LOW)
            grad_tile = grad_t[:, q0:q1].astype(WIDE)
            row_inner = jnp.sum(grad_tile * attended, axis=0, keepdims=True)
            inner_high = row_inner.astype(LOW)
            inner_low = (row_inner - inner_high.astype(WIDE)).astype(LOW)
            place = lax.broadcasted_iota(jnp.int32, (HD, q1 - q0), 0)
            inner_mark = jnp.where(
                place == 0,
                -inner_high.astype(WIDE),
                jnp.where(place == 1, -inner_low.astype(WIDE), 0.0),
            ).astype(LOW)
            grad_aug = jnp.concatenate([grad_t[:, q0:q1], inner_mark], axis=0)
            shifted = jnp.dot(value_aug[k0:k1], grad_aug, preferred_element_type=WIDE)
            grad_scores = (terms * shifted).astype(LOW)
            query_grads.append(
                jnp.dot(key_t[:, k0:k1], grad_scores, preferred_element_type=WIDE)
                * (inverse * factor)
            )
            query_rows = jnp.transpose(
                jnp.concatenate(
                    [query_t[:, q0:q1].astype(WIDE) * (inverse * factor), grad_tile * inverse],
                    axis=0,
                ).astype(LOW)
            )
            key_term = jnp.dot(grad_scores, query_rows, preferred_element_type=WIDE)
            value_term = jnp.dot(terms_low, query_rows, preferred_element_type=WIDE)
            if number == 0:
                key_grad[k0:k1, :] = key_term
                value_grad[k0:k1, :] = value_term
                key_grad[k1:rows, :] = jnp.zeros((rows - k1, 2 * HD), WIDE)
                value_grad[k1:rows, :] = jnp.zeros((rows - k1, 2 * HD), WIDE)
            else:
                key_grad[k0:k1, :] += key_term
                value_grad[k0:k1, :] += value_term
        lane = lax.broadcasted_iota(jnp.int32, (rows, 2 * HD), 1)
        joint = jnp.transpose(jnp.where(lane < HD, key_grad[...], value_grad[...]))
        query_grad = jnp.concatenate(query_grads, axis=1)
        key_grad_t = joint[0:HD, :]
        gain_sum_query += lane_fold(query_grad * query_hat)
        gain_sum_key += lane_fold(key_grad_t * key_hat)
        pieces += [
            part_norm_back(query_grad, query_hat, query_scale, gain_query),
            part_norm_back(key_grad_t, key_hat, key_scale, gain_key),
            joint[HD : 2 * HD, :],
        ]
    grad_joined_ref[...] = jnp.transpose(jnp.concatenate(pieces, axis=0)).astype(LOW)

    @pl.when(pl.program_id(0) == 0)
    def _():
        gain_grad_ref[...] = jnp.zeros_like(gain_grad_ref)

    gain_grad_ref[...] += jnp.concatenate([gain_sum_query, gain_sum_key], axis=0)


def attention(joined_t, grad_t, gains, query_mark, key_mark, start, heads):
    rows = joined_t.shape[1]
    width = heads * 3 * HD
    skip = start // 2
    slot = rows // 4
    far = 3 * slot
    tiles = ((0, 512, 0, far), (512, 768, 0, rows), (768, rows, far, rows))
    return pl.pallas_call(
        functools.partial(attention_body, rows, tiles),
        grid=(heads // 2,),
        in_specs=[
            pl.BlockSpec((6 * HD, rows), lambda i: (i + skip, 0)),
            pl.BlockSpec((2 * HD, rows), lambda i: (i + skip, 0)),
            pl.BlockSpec((2 * HD, 1), lambda i: (0, 0)),
            pl.BlockSpec((HD, rows), lambda i: (0, 0)),
            pl.BlockSpec((HD, rows), lambda i: (0, 0)),
        ],
        out_specs=[
            pl.BlockSpec((2 * HD, rows), lambda i: (i, 0)),
            pl.BlockSpec((rows, 6 * HD), lambda i: (0, i)),
            pl.BlockSpec((2 * HD, 128), lambda i: (0, 0)),
        ],
        out_shape=[
            jax.ShapeDtypeStruct((heads * HD, rows), LOW),
            jax.ShapeDtypeStruct((rows, width), LOW),
            jax.ShapeDtypeStruct((2 * HD, 128), WIDE),
        ],
        scratch_shapes=[
            pltpu.VMEM((rows, 2 * HD), WIDE),
            pltpu.VMEM((rows, 2 * HD), WIDE),
        ],
        compiler_params=pltpu.CompilerParams(vmem_limit_bytes=28 * MIB),
        cost_estimate=pl.CostEstimate(
            flops=heads * 20 * rows * rows * HD,
            bytes_accessed=rows * width * 6 + heads * HD * rows * 4,
            transcendentals=heads * rows * rows,
        ),
        name="attention_both",
    )(joined_t, grad_t, gains, query_mark, key_mark)


def ring_order(n):
    if n % 4:
        return list(range(n))
    up = [z * 4 + c for z in range(n // 4) for c in range(2)]
    down = [z * 4 + 2 + c for z in reversed(range(n // 4)) for c in range(2)]
    return up + down


def ring_scatter(values, n):
    return lax.psum_scatter(
        values, "batch", scatter_dimension=0, tiled=True, axis_index_groups=[ring_order(n)]
    )


def ring_gather(own, n):
    return lax.all_gather(own, "batch", axis=0, tiled=True, axis_index_groups=[ring_order(n)])


def send(values, pairs):
    return lax.ppermute(values, "batch", pairs)


def exchange(values, bit, n):
    return send(values, [(i, i ^ bit) for i in range(n)])


def added(left, right):
    return (left.astype(WIDE) + right.astype(WIDE)).astype(LOW)


def then(done, *values):
    return lax.optimization_barrier((done, values))[1]


def ring_view(values, n):
    bits = max(n.bit_length() - 3, 0)
    return values.reshape((2,) + (2,) * bits + (2, values.shape[0] // n, values.shape[1]))


def ring_half(bit, place, n):
    dims = n.bit_length()
    mine = (place // bit) % 2
    if bit == 1:
        return dims - 2, mine
    if bit == 2:
        return 0, mine
    return dims - 1 - bit.bit_length() + 1, mine ^ ((place // 2) % 2)


def pair_send(values, bit, place, n):
    dim, mine = ring_half(bit, place, n)
    return exchange(lax.dynamic_slice_in_dim(values, 1 - mine, 1, dim), bit, n)


def pair_add(values, arrived, bit, place, n):
    dim, mine = ring_half(bit, place, n)
    return added(lax.dynamic_slice_in_dim(values, mine, 1, dim), arrived)


def small_step(values, bit, n):
    return values + exchange(values, bit, n)


def on_device(n_batch, tokens, ln_gain, w_qkv, qk_gain, w_out, w_up, b_up, w_down, b_out,
              cotangent, slot_image, token_valid):
    rows, half = tokens.shape
    width = 2 * half
    slots = slot_image.shape[0]
    slot_rows = rows // slots
    side = lax.axis_index("head")
    first = side == 0

    other_tokens = swap(tokens, "head")
    held, _ = lax.optimization_barrier((cotangent, other_tokens))
    other_cotangent = swap(held, "head")

    place = lax.axis_index("batch")
    sides = jnp.reshape(side, (1,)).astype(jnp.int32)
    normed, stats = input_norm(sides, tokens, other_tokens, ln_gain)
    hidden, slope = mlp_forward(normed, w_up, b_up)
    piece = both_halves(cotangent, other_cotangent, first, 1)
    grad_pre, grad_b_up = mlp_slope(piece, w_down, slope)
    mlp_part = mlp_weights(hidden, piece, normed, grad_pre)
    mlp_own = ring_scatter(mlp_part, n_batch)

    token_image = jnp.repeat(slot_image, slot_rows, total_repeat_length=rows)
    ids = lax.broadcasted_iota(jnp.int32, (HD, rows), 0)
    same = token_image[None, :] == ids
    query_mark = jnp.where(same, 1.0, 0.0).astype(LOW)
    key_mark = jnp.where(same & (token_valid == 1)[None, :], 0.0, FAR)
    key_mark = jnp.where(ids < slots, key_mark, 0.0).astype(LOW)
    gains = qk_gain.reshape(-1, 1)
    columns, inner = w_qkv.shape[1] // 2, w_out.shape[0] // 2
    heads = columns // (3 * HD)
    bits = []
    while 4 * 2 ** len(bits) < n_batch:
        bits.append(4 * 2 ** len(bits))

    def heads_part(number, normed, piece):
        joined_t = contract(w_qkv[:, number * columns : (number + 1) * columns], normed, 0, 1)
        grad_t = contract(w_out[number * inner : (number + 1) * inner], piece, 1, 1).astype(LOW)
        return joined_t, grad_t

    def heads_both(joined_t, grad_t, normed, piece):
        attended_t, grad_joined, gain_grad = attention(
            joined_t, grad_t, gains, query_mark, key_mark, 0, heads
        )
        weights = heads_weights(normed, grad_joined, piece, attended_t)
        return attended_t, grad_joined, gain_grad, weights

    ready = heads_part(0, *then(mlp_part, normed, piece))
    att0, join0, gain0, part0 = heads_both(*ready, normed, piece)
    part0 = ring_view(part0, n_batch)
    core0 = pair_send(part0, 1, place, n_batch)
    ready = heads_part(1, *then(part0, normed, piece))
    (core0,) = then(ready, core0)
    part0 = pair_add(part0, core0, 1, place, n_batch)
    over0 = pair_send(part0, 2, place, n_batch)
    att1, join1, gain1, part1 = heads_both(*then(part0, *ready), normed, piece)
    part1 = ring_view(part1, n_batch)
    core1 = pair_send(part1, 1, place, n_batch)
    (over0,) = then(part1, over0)
    part0 = pair_add(part0, over0, 2, place, n_batch)
    sent0 = pair_send(part0, bits[0], place, n_batch)
    attended_t = jnp.concatenate([att0, att1], axis=0)
    grad_joined = jnp.concatenate([join0, join1], axis=1)
    back = (sides, grad_joined, w_qkv, grad_pre, w_up)
    (away_in,) = grad_in_half(False, *then(part0, *back))
    arrived_in = swap(away_in, "head")
    (core1,) = then(away_in, core1)
    part1 = pair_add(part1, core1, 1, place, n_batch)
    over1 = pair_send(part1, 2, place, n_batch)
    branch = (sides, attended_t, w_out, hidden, w_down)
    away_out = output_half(False, *then(part1, *branch))
    arrived_out = swap(away_out, "head")
    for bit, after in zip(bits, bits[1:] + [0]):
        (sent0,) = then(away_out, sent0)
        part0 = pair_add(part0, sent0, bit, place, n_batch)
        if after:
            sent0 = pair_send(part0, after, place, n_batch)
    (over1,) = then(away_out, over1)
    part1 = pair_add(part1, over1, 2, place, n_batch)
    for bit in bits:
        part1 = pair_add(part1, pair_send(part1, bit, place, n_batch), bit, place, n_batch)
    own = jnp.concatenate([mlp_own] + [p.reshape(-1, width) for p in (part0, part1)], axis=0)
    whole = ring_gather(own, n_batch)

    hat, sums, grad_ln = grad_in_half(
        True, *then(own, *back), tokens, arrived_in, stats, ln_gain.reshape(1, width)
    )
    sums_other = swap(sums[:, 0:2].T, "head").T
    gain_grad = jnp.sum(gain0 + gain1, axis=1)
    gain_grad = gain_grad + swap(gain_grad, "head")
    grad_b_out = jnp.sum(cotangent.astype(WIDE), axis=0)
    small = jnp.concatenate([grad_ln[0], grad_b_out, grad_b_up[0], gain_grad])
    output = output_half(True, *then(hat, *branch), tokens, arrived_out, b_out.reshape(1, half))
    grad_tokens = grad_in_finish(cotangent, tokens, stats, hat, sums, sums_other)
    for bit in [1, 2] + bits:
        small = small_step(small, bit, n_batch)
    units = b_up.shape[0]
    (whole,) = then((output, grad_tokens, small), whole)
    grad_wd, grad_wup, grad_wqkv, grad_wo = spread(whole, n_batch, units, columns, 2)
    return (
        output,
        grad_tokens,
        small[0:half],
        grad_wqkv,
        small[2 * half + units :].reshape(qk_gain.shape),
        grad_wo,
        grad_wup,
        small[2 * half : 2 * half + units],
        grad_wd,
        small[half : 2 * half],
    )


def solution(mesh):
    placed = (
        P("batch", "head"),
        P(),
        P(None, "head"),
        P(),
        P("head", None),
        P(None, "head"),
        P("head"),
        P("head", None),
        P("head"),
        P("batch", "head"),
        P("batch"),
        P("batch"),
    )
    return jax.shard_map(
        functools.partial(on_device, mesh.shape["batch"]),
        mesh=mesh,
        in_specs=placed,
        out_specs=(
            P("batch", "head"),
            P("batch", "head"),
            P("head"),
            P(None, "head"),
            P(),
            P("head", None),
            P(None, "head"),
            P("head"),
            P("head", None),
            P("head"),
        ),
        check_vma=False,
    )
```

```python
import functools

import jax
import jax.numpy as jnp
from jax import lax
from jax.experimental import pallas as pl
from jax.experimental.pallas import tpu as pltpu
from jax.sharding import PartitionSpec as P

HD = 64
EPSILON = 1e-06
FAR = -16384.0
LOW = jnp.bfloat16
WIDE = jnp.float32
MIB = 1024 * 1024
SHORT = pl.CostEstimate(flops=1024, bytes_accessed=1024, transcendentals=0)


def contract(left, right, left_dim, right_dim):
    return lax.dot_general(
        left, right, (((left_dim,), (right_dim,)), ((), ())), preferred_element_type=WIDE
    )


def swap(values, axis):
    return lax.ppermute(values, axis, [(0, 1), (1, 0)])


def both_halves(mine, other, first, dim):
    return jnp.where(
        first,
        jnp.concatenate([mine, other], axis=dim),
        jnp.concatenate([other, mine], axis=dim),
    )


def mlp_body(normed_ref, w_ref, b_ref, hidden_ref, slope_ref):
    pre = jnp.dot(normed_ref[...], w_ref[...], preferred_element_type=WIDE) + b_ref[...]
    cdf = 0.5 * (1.0 + lax.erf(pre * (0.5**0.5)))
    density = jnp.exp(-0.5 * pre * pre) * 0.3989422804014327
    hidden_ref[...] = (pre * cdf).astype(LOW)
    slope_ref[...] = (cdf + pre * density).astype(LOW)


def streamed(values):
    return pltpu.with_memory_space_constraint(values, pltpu.HBM)


def mlp_forward(normed, w_up, b_up):
    rows, width = normed.shape
    units = w_up.shape[1]
    block = 512
    return pl.pallas_call(
        mlp_body,
        grid=(units // block,),
        in_specs=[
            pl.BlockSpec((rows, width), lambda i: (0, 0)),
            pl.BlockSpec((width, block), lambda i: (0, i)),
            pl.BlockSpec((1, block), lambda i: (0, i)),
        ],
        out_specs=[
            pl.BlockSpec((rows, block), lambda i: (0, i)),
            pl.BlockSpec((rows, block), lambda i: (0, i)),
        ],
        out_shape=[
            jax.ShapeDtypeStruct((rows, units), LOW),
            jax.ShapeDtypeStruct((rows, units), LOW),
        ],
        compiler_params=pltpu.CompilerParams(vmem_limit_bytes=16 * MIB),
        cost_estimate=SHORT,
        name="mlp_forward",
    )(normed, streamed(w_up), b_up.reshape(1, units))


def norm_body(side_ref, mine_ref, other_ref, gain_ref, normed_ref, stats_ref):
    mine = mine_ref[...].astype(WIDE)
    other = other_ref[...].astype(WIDE)
    width = 2 * mine.shape[1]
    half = mine.shape[1]
    center = (
        jnp.sum(mine, axis=1, keepdims=True) + jnp.sum(other, axis=1, keepdims=True)
    ) / width
    mine = mine - center
    other = other - center
    spread = (
        jnp.sum(mine * mine, axis=1, keepdims=True)
        + jnp.sum(other * other, axis=1, keepdims=True)
    ) / width
    scaled = lax.rsqrt(spread + EPSILON)
    first = side_ref[0] == 0
    left = jnp.where(first, mine, other)
    right = jnp.where(first, other, mine)
    normed_ref[:, 0:half] = (left * scaled * gain_ref[:, 0:half]).astype(LOW)
    normed_ref[:, half:width] = (right * scaled * gain_ref[:, half:width]).astype(LOW)
    lane = lax.broadcasted_iota(jnp.int32, stats_ref.shape, 1)
    stats_ref[...] = jnp.where(lane == 0, center, scaled)


def input_norm(side, mine, other, gain):
    rows, half = mine.shape
    block = 224
    return pl.pallas_call(
        norm_body,
        grid_spec=pltpu.PrefetchScalarGridSpec(
            num_scalar_prefetch=1,
            grid=(rows // block,),
            in_specs=[
                pl.BlockSpec((block, half), lambda i, s: (i, 0)),
                pl.BlockSpec((block, half), lambda i, s: (i, 0)),
                pl.BlockSpec((1, 2 * half), lambda i, s: (0, 0)),
            ],
            out_specs=[
                pl.BlockSpec((block, 2 * half), lambda i, s: (i, 0)),
                pl.BlockSpec((block, 128), lambda i, s: (i, 0)),
            ],
        ),
        out_shape=[
            jax.ShapeDtypeStruct((rows, 2 * half), LOW),
            jax.ShapeDtypeStruct((rows, 128), WIDE),
        ],
        cost_estimate=SHORT,
        name="input_norm",
    )(side, mine, other, gain.reshape(1, 2 * half))


def slope_body(piece_ref, w_ref, slope_ref, grad_pre_ref, bias_ref):
    back = lax.dot_general(
        piece_ref[...], w_ref[...], (((1,), (1,)), ((), ())), preferred_element_type=WIDE
    )
    low = (back * slope_ref[...].astype(WIDE)).astype(LOW)
    grad_pre_ref[...] = low
    bias_ref[...] = jnp.sum(low.astype(WIDE), axis=0, keepdims=True)


def mlp_slope(piece, w_down, slope):
    rows, width = piece.shape
    units = w_down.shape[0]
    block = 512
    return pl.pallas_call(
        slope_body,
        grid=(units // block,),
        in_specs=[
            pl.BlockSpec((rows, width), lambda i: (0, 0)),
            pl.BlockSpec((block, width), lambda i: (i, 0)),
            pl.BlockSpec((rows, block), lambda i: (0, i)),
        ],
        out_specs=[
            pl.BlockSpec((rows, block), lambda i: (0, i)),
            pl.BlockSpec((1, block), lambda i: (0, i)),
        ],
        out_shape=[
            jax.ShapeDtypeStruct((rows, units), LOW),
            jax.ShapeDtypeStruct((1, units), WIDE),
        ],
        compiler_params=pltpu.CompilerParams(vmem_limit_bytes=16 * MIB),
        cost_estimate=SHORT,
        name="mlp_slope",
    )(piece, streamed(w_down), slope)


def first_dims(left, right):
    return lax.dot_general(left, right, (((0,), (0,)), ((), ())), preferred_element_type=WIDE)


def mlp_weights_body(down_steps, hidden_ref, piece_ref, normed_ref, grad_pre_ref, *refs):
    step = pl.program_id(0)
    out_ref = refs[-1]

    def put(total):
        if len(refs) == 2:
            total = total + refs[0][...].astype(WIDE)
        out_ref[...] = total.astype(LOW)

    @pl.when(step < down_steps)
    def _():
        put(first_dims(hidden_ref[...], piece_ref[...]))

    @pl.when(step >= down_steps)
    def _():
        put(first_dims(normed_ref[...], grad_pre_ref[...]))


def mlp_weights(hidden, piece, normed, grad_pre, *before):
    rows, units = hidden.shape
    width = piece.shape[1]
    block = 512
    down = units // block
    across = width // block
    halves = units // width

    def later(i):
        return jnp.maximum(i - down, 0)

    return pl.pallas_call(
        functools.partial(mlp_weights_body, down),
        grid=(down + halves * across,),
        in_specs=[
            pl.BlockSpec((rows, block), lambda i: (0, jnp.minimum(i, down - 1))),
            pl.BlockSpec((rows, width), lambda i: (0, 0)),
            pl.BlockSpec((rows, block), lambda i: (0, later(i) % across)),
            pl.BlockSpec((rows, width), lambda i: (0, later(i) // across)),
        ]
        + [pl.BlockSpec((block, width), lambda i: (i, 0)) for _ in before],
        out_specs=pl.BlockSpec((block, width), lambda i: (i, 0)),
        out_shape=pltpu.HBM((2 * units, width), LOW),
        input_output_aliases={4: 0} if before else {},
        compiler_params=pltpu.CompilerParams(vmem_limit_bytes=24 * MIB),
        cost_estimate=SHORT,
        name="mlp_weights",
    )(hidden, piece, normed, grad_pre, *before)


def heads_weights_body(count, normed_ref, piece_ref, *refs):
    grad_joined_refs, attended_refs, out_ref = refs[:count], refs[count : 2 * count], refs[-1]
    start = 0
    for ref in grad_joined_refs:
        out_ref[:, start : start + ref.shape[1]] = first_dims(normed_ref[...], ref[...]).astype(LOW)
        start += ref.shape[1]
    for ref in attended_refs:
        out_ref[:, start : start + ref.shape[0]] = lax.dot_general(
            piece_ref[...], ref[...], (((0,), (1,)), ((), ())), preferred_element_type=WIDE
        ).astype(LOW)
        start += ref.shape[0]


def heads_weights(normed, grad_joined, piece, attended_t):
    rows, width = normed.shape
    columns = sum(v.shape[1] for v in grad_joined)
    inner = sum(v.shape[0] for v in attended_t)
    block = 256
    return pl.pallas_call(
        functools.partial(heads_weights_body, len(grad_joined)),
        grid=(width // block,),
        in_specs=[
            pl.BlockSpec((rows, block), lambda i: (0, i)),
            pl.BlockSpec((rows, block), lambda i: (0, i)),
        ]
        + [pl.BlockSpec(v.shape, lambda i: (0, 0)) for v in (*grad_joined, *attended_t)],
        out_specs=pl.BlockSpec((block, columns + inner), lambda i: (i, 0)),
        out_shape=jax.ShapeDtypeStruct((width, columns + inner), LOW),
        compiler_params=pltpu.CompilerParams(vmem_limit_bytes=16 * MIB),
        cost_estimate=pl.CostEstimate(
            flops=2 * rows * width * (columns + inner),
            bytes_accessed=2 * (2 * rows * width + (rows + width) * (columns + inner)),
            transcendentals=0,
        ),
        name="heads_weights",
    )(normed, piece, *grad_joined, *attended_t)


def mlp_spread_body(whole_ref, down_ref, up_ref):
    step = pl.program_id(0)
    steps = pl.num_programs(0)

    @pl.when(step < steps // 2)
    def _():
        down_ref[...] = whole_ref[...].astype(WIDE)

    @pl.when(step >= steps // 2)
    def _():
        up_ref[...] = whole_ref[...].astype(WIDE)


def mlp_spread(whole):
    units, width = whole.shape[0] // 2, whole.shape[1]
    block = 512
    down = units // block
    across = width // block

    def later(i):
        return jnp.maximum(i - down, 0)

    return pl.pallas_call(
        mlp_spread_body,
        grid=(2 * down,),
        in_specs=[pl.BlockSpec((block, width), lambda i: (i, 0))],
        out_specs=[
            pl.BlockSpec((block, width), lambda i: (jnp.minimum(i, down - 1), 0)),
            pl.BlockSpec((block, width), lambda i: (later(i) % across, later(i) // across)),
        ],
        out_shape=[
            jax.ShapeDtypeStruct((units, width), WIDE),
            jax.ShapeDtypeStruct((width, units), WIDE),
        ],
        compiler_params=pltpu.CompilerParams(vmem_limit_bytes=16 * MIB),
        cost_estimate=SHORT,
        name="mlp_spread",
    )(streamed(whole))


def heads_spread_body(columns, *refs):
    heads_refs, (qkv_ref, out_ref) = refs[:-2], refs[-2:]
    for number, ref in enumerate(heads_refs):
        value = ref[...].astype(WIDE).reshape(qkv_ref.shape[0], -1)
        inner = value.shape[1] - columns
        qkv_ref[:, columns * number : columns * (number + 1)] = value[:, 0:columns]
        out_ref[inner * number : inner * (number + 1), :] = jnp.transpose(value[:, columns:])


def heads_spread(whole, n, columns, count):
    width = whole.shape[1]
    heads_rows = width // n
    inner = width - columns
    lines = 256
    parts = streamed(whole.reshape(n, count, heads_rows, width))

    def part(number):
        return pl.BlockSpec((lines // heads_rows, 1, heads_rows, width), lambda i: (i, number, 0, 0))

    return pl.pallas_call(
        functools.partial(heads_spread_body, columns),
        grid=(width // lines,),
        in_specs=[part(number) for number in range(count)],
        out_specs=[
            pl.BlockSpec((lines, columns * count), lambda i: (i, 0)),
            pl.BlockSpec((inner * count, lines), lambda i: (0, i)),
        ],
        out_shape=[
            jax.ShapeDtypeStruct((width, columns * count), WIDE),
            jax.ShapeDtypeStruct((inner * count, width), WIDE),
        ],
        compiler_params=pltpu.CompilerParams(vmem_limit_bytes=16 * MIB),
        cost_estimate=SHORT,
        name="heads_spread",
    )(*[parts] * count)


def output_body(mine, count, side_ref, w_out_ref, hidden_ref, w_down_ref, *refs):
    attended_refs, more, out_ref = refs[:count], refs[count:-1], refs[-1]
    rows = out_ref.shape[0]
    for r0, r1 in ((0, rows),):
        attended = jnp.concatenate([ref[...] for ref in attended_refs], axis=0)
        total = jnp.dot(
            hidden_ref[...], w_down_ref[...], preferred_element_type=WIDE
        ) + first_dims(attended, w_out_ref[...])
        if mine:
            tokens_ref, arrived_ref, bias_ref = more
            total = (
                tokens_ref[r0:r1, :].astype(WIDE)
                + (total + arrived_ref[r0:r1, :].astype(WIDE))
                + bias_ref[...]
            )
        out_ref[r0:r1, :] = total.astype(LOW)


def output_half(mine, side, w_out, hidden, w_down, attended_t, *more):
    rows, units = hidden.shape
    inner, width = w_out.shape
    half = width // 2
    flip = 0 if mine else 1

    def column(i, s):
        return (0, s[0] ^ flip)

    def whole(i, s):
        return (0, 0)

    return pl.pallas_call(
        functools.partial(output_body, mine, len(attended_t)),
        grid_spec=pltpu.PrefetchScalarGridSpec(
            num_scalar_prefetch=1,
            grid=(1,),
            in_specs=[
                pl.BlockSpec((inner, half), column),
                pl.BlockSpec((rows, units), whole),
                pl.BlockSpec((units, half), column),
            ]
            + [pl.BlockSpec(v.shape, whole) for v in (*attended_t, *more)],
            out_specs=pl.BlockSpec((rows, half), whole),
        ),
        out_shape=jax.ShapeDtypeStruct((rows, half), LOW),
        compiler_params=pltpu.CompilerParams(vmem_limit_bytes=20 * MIB),
        cost_estimate=SHORT,
        name="output_mine" if mine else "output_away",
    )(side, w_out, hidden, w_down, *attended_t, *more)


def second_dims(left, right):
    return lax.dot_general(left, right, (((1,), (1,)), ((), ())), preferred_element_type=WIDE)


def grad_in_body(mine, count, side_ref, w_qkv_ref, grad_pre_ref, w_up_ref, *refs):
    more = refs[count:]
    rows = grad_pre_ref.shape[0]
    if mine:
        tokens_ref, arrived_ref, stats_ref, gain_ref, hat_ref, sums_ref, gain_grad_ref = more
        gain_grad = 0.0
    for r0, r1 in ((0, rows),):
        grad_joined = jnp.concatenate([ref[...] for ref in refs[:count]], axis=1)
        total = second_dims(grad_joined, w_qkv_ref[...]) + second_dims(
            grad_pre_ref[...], w_up_ref[...]
        )
        if not mine:
            more[0][r0:r1, :] = total.astype(LOW)
            continue
        total = total + arrived_ref[r0:r1, :].astype(WIDE)
        stats = stats_ref[r0:r1, :]
        x_hat = (tokens_ref[r0:r1, :].astype(WIDE) - stats[:, 0:1]) * stats[:, 1:2]
        grad_hat = total * gain_ref[...]
        hat_ref[r0:r1, :] = grad_hat
        lane = lax.broadcasted_iota(jnp.int32, stats.shape, 1)
        sums_ref[r0:r1, :] = jnp.where(
            lane == 0,
            jnp.sum(grad_hat, axis=1, keepdims=True),
            jnp.sum(grad_hat * x_hat, axis=1, keepdims=True),
        )
        gain_grad = gain_grad + jnp.sum(total * x_hat, axis=0, keepdims=True)
    if mine:
        gain_grad_ref[...] = gain_grad


def grad_in_half(mine, side, w_qkv, grad_pre, w_up, grad_joined, *more):
    rows, units = grad_pre.shape
    width, columns = w_qkv.shape
    half = width // 2
    flip = 0 if mine else 1

    def picked(i, s):
        return (s[0] ^ flip, 0)

    def whole(i, s):
        return (0, 0)

    extra, outs = [], [((rows, half), LOW)]
    if mine:
        extra = [
            pl.BlockSpec((rows, half), whole),
            pl.BlockSpec((rows, half), whole),
            pl.BlockSpec((rows, 128), whole),
            pl.BlockSpec((1, half), lambda i, s: (0, s[0])),
        ]
        outs = [((rows, half), WIDE), ((rows, 128), WIDE), ((1, half), WIDE)]
    return pl.pallas_call(
        functools.partial(grad_in_body, mine, len(grad_joined)),
        grid_spec=pltpu.PrefetchScalarGridSpec(
            num_scalar_prefetch=1,
            grid=(1,),
            in_specs=[
                pl.BlockSpec((half, columns), picked),
                pl.BlockSpec((rows, units), whole),
                pl.BlockSpec((half, units), picked),
                *[pl.BlockSpec(v.shape, whole) for v in grad_joined],
                *extra,
            ],
            out_specs=[pl.BlockSpec(shape, whole) for shape, _ in outs],
        ),
        out_shape=[jax.ShapeDtypeStruct(shape, kind) for shape, kind in outs],
        compiler_params=pltpu.CompilerParams(vmem_limit_bytes=28 * MIB),
        cost_estimate=SHORT,
        name="grad_in_mine" if mine else "grad_in_away",
    )(side, w_qkv, grad_pre, w_up, *grad_joined, *more)


def finish_body(cotangent_ref, tokens_ref, stats_ref, hat_ref, sums_ref, other_ref, out_ref):
    width = 2 * tokens_ref.shape[1]
    scaled = stats_ref[:, 1:2]
    x_hat = (tokens_ref[...].astype(WIDE) - stats_ref[:, 0:1]) * scaled
    sums = (sums_ref[:, 0:2] + other_ref[...]) / width
    out_ref[...] = (
        cotangent_ref[...].astype(WIDE)
        + scaled * (hat_ref[...] - sums[:, 0:1] - x_hat * sums[:, 1:2])
    ).astype(LOW)


def grad_in_finish(cotangent, tokens, stats, hat, sums, other):
    rows, half = tokens.shape
    block = 224

    def rows_of(columns):
        return pl.BlockSpec((block, columns), lambda i: (i, 0))

    return pl.pallas_call(
        finish_body,
        grid=(rows // block,),
        in_specs=[rows_of(c) for c in (half, half, 128, half, 128, 2)],
        out_specs=rows_of(half),
        out_shape=jax.ShapeDtypeStruct((rows, half), LOW),
        cost_estimate=SHORT,
        name="grad_in_finish",
    )(cotangent, tokens, stats, hat, sums, other)


def part_norm(values):
    center = jnp.mean(values, axis=0, keepdims=True)
    shifted = values - center
    scaled = lax.rsqrt(jnp.mean(shifted * shifted, axis=0, keepdims=True) + EPSILON)
    return shifted * scaled, scaled


def part_norm_back(grad, normal, scaled, gain):
    g = grad * gain
    inner = jnp.mean(g * normal, axis=0, keepdims=True)
    return scaled * (g - jnp.mean(g, axis=0, keepdims=True) - normal * inner)


def lane_fold(values):
    total = values[:, 0:128]
    for start in range(128, values.shape[1], 128):
        total = total + values[:, start : start + 128]
    return total


def attention_body(rows, tiles, count, *refs):
    joined_refs, grad_refs = refs[:count], refs[count : 2 * count]
    (gain_ref, query_mark_ref, key_mark_ref, attended_ref, grad_joined_ref, gain_grad_ref,
     key_grad, value_grad) = refs[2 * count :]

    def part(some, r0, r1):
        return jnp.concatenate([ref[r0:r1, :] for ref in some], axis=1)

    factor = float(HD) ** (-0.5)
    gain_query = gain_ref[0:HD, :]
    gain_key = gain_ref[HD : 2 * HD, :]
    pieces = []
    gain_sum_query = jnp.zeros((HD, 128), WIDE)
    gain_sum_key = jnp.zeros((HD, 128), WIDE)
    one_mark = jnp.where(lax.broadcasted_iota(jnp.int32, (HD, rows), 0) < 2, 1.0, 0.0).astype(LOW)
    for head in range(2):
        base = head * 3 * HD
        query_hat, query_scale = part_norm(part(joined_refs, base, base + HD))
        key_hat, key_scale = part_norm(part(joined_refs, base + HD, base + 2 * HD))
        value_t = part(joined_refs, base + 2 * HD, base + 3 * HD).astype(LOW)
        query_t = (query_hat * gain_query).astype(LOW)
        key_t = (key_hat * gain_key).astype(LOW)
        grad_t = part(grad_refs, head * HD, (head + 1) * HD)
        query_aug = jnp.concatenate([query_t * factor, query_mark_ref[...]], axis=0)
        key_aug = jnp.transpose(jnp.concatenate([key_t, key_mark_ref[...]], axis=0))
        value_aug_t = jnp.concatenate([value_t, one_mark], axis=0)
        value_aug = jnp.transpose(value_aug_t)
        query_grads = []
        for number, (q0, q1, k0, k1) in enumerate(tiles):
            scores = jnp.dot(key_aug[k0:k1], query_aug[:, q0:q1], preferred_element_type=WIDE)
            terms = jnp.exp(scores)
            terms_low = terms.astype(LOW)
            summed = jnp.dot(value_aug_t[:, k0:k1], terms_low, preferred_element_type=WIDE)
            inverse = 1.0 / summed[HD : HD + 1, :]
            attended = summed[0:HD, :] * inverse
            attended_ref[head * HD : (head + 1) * HD, q0:q1] = attended.astype(LOW)
            grad_tile = grad_t[:, q0:q1].astype(WIDE)
            row_inner = jnp.sum(grad_tile * attended, axis=0, keepdims=True)
            inner_high = row_inner.astype(LOW)
            inner_low = (row_inner - inner_high.astype(WIDE)).astype(LOW)
            place = lax.broadcasted_iota(jnp.int32, (HD, q1 - q0), 0)
            inner_mark = jnp.where(
                place == 0,
                -inner_high.astype(WIDE),
                jnp.where(place == 1, -inner_low.astype(WIDE), 0.0),
            ).astype(LOW)
            grad_aug = jnp.concatenate([grad_t[:, q0:q1], inner_mark], axis=0)
            shifted = jnp.dot(value_aug[k0:k1], grad_aug, preferred_element_type=WIDE)
            grad_scores = (terms * shifted).astype(LOW)
            query_grads.append(
                jnp.dot(key_t[:, k0:k1], grad_scores, preferred_element_type=WIDE)
                * (inverse * factor)
            )
            query_rows = jnp.transpose(
                jnp.concatenate(
                    [query_t[:, q0:q1].astype(WIDE) * (inverse * factor), grad_tile * inverse],
                    axis=0,
                ).astype(LOW)
            )
            key_term = jnp.dot(grad_scores, query_rows, preferred_element_type=WIDE)
            value_term = jnp.dot(terms_low, query_rows, preferred_element_type=WIDE)
            if number == 0:
                key_grad[k0:k1, :] = key_term
                value_grad[k0:k1, :] = value_term
                key_grad[k1:rows, :] = jnp.zeros((rows - k1, 2 * HD), WIDE)
                value_grad[k1:rows, :] = jnp.zeros((rows - k1, 2 * HD), WIDE)
            else:
                key_grad[k0:k1, :] += key_term
                value_grad[k0:k1, :] += value_term
        lane = lax.broadcasted_iota(jnp.int32, (rows, 2 * HD), 1)
        joint = jnp.transpose(jnp.where(lane < HD, key_grad[...], value_grad[...]))
        query_grad = jnp.concatenate(query_grads, axis=1)
        key_grad_t = joint[0:HD, :]
        gain_sum_query += lane_fold(query_grad * query_hat)
        gain_sum_key += lane_fold(key_grad_t * key_hat)
        pieces += [
            part_norm_back(query_grad, query_hat, query_scale, gain_query),
            part_norm_back(key_grad_t, key_hat, key_scale, gain_key),
            joint[HD : 2 * HD, :],
        ]
    grad_joined_ref[...] = jnp.transpose(jnp.concatenate(pieces, axis=0)).astype(LOW)

    @pl.when(pl.program_id(0) == 0)
    def _():
        gain_grad_ref[...] = jnp.zeros_like(gain_grad_ref)

    gain_grad_ref[...] += jnp.concatenate([gain_sum_query, gain_sum_key], axis=0)


def attention(joined_t, grad_t, gains, query_mark, key_mark, skip):
    rows = query_mark.shape[1]
    heads = 2
    width = heads * 3 * HD
    far = 3 * (rows // 4)
    tiles = ((0, 512, 0, far), (512, 768, 0, rows), (768, rows, far, rows))

    def whole(i):
        return (0, 0)

    return pl.pallas_call(
        functools.partial(attention_body, rows, tiles, len(joined_t)),
        grid=(heads // 2,),
        in_specs=[pl.BlockSpec((6 * HD, v.shape[1]), lambda i: (skip, 0)) for v in joined_t]
        + [pl.BlockSpec((2 * HD, v.shape[1]), lambda i: (skip, 0)) for v in grad_t]
        + [
            pl.BlockSpec((2 * HD, 1), whole),
            pl.BlockSpec((HD, rows), whole),
            pl.BlockSpec((HD, rows), whole),
        ],
        out_specs=[
            pl.BlockSpec((2 * HD, rows), lambda i: (i, 0)),
            pl.BlockSpec((rows, 6 * HD), lambda i: (0, i)),
            pl.BlockSpec((2 * HD, 128), whole),
        ],
        out_shape=[
            jax.ShapeDtypeStruct((heads * HD, rows), LOW),
            jax.ShapeDtypeStruct((rows, width), LOW),
            jax.ShapeDtypeStruct((2 * HD, 128), WIDE),
        ],
        scratch_shapes=[
            pltpu.VMEM((rows, 2 * HD), WIDE),
            pltpu.VMEM((rows, 2 * HD), WIDE),
        ],
        compiler_params=pltpu.CompilerParams(vmem_limit_bytes=20 * MIB),
        cost_estimate=SHORT,
        name="attention_both",
    )(*joined_t, *grad_t, gains, query_mark, key_mark)


def ring_order(n):
    if n % 4:
        return list(range(n))
    up = [z * 4 + c for z in range(n // 4) for c in range(2)]
    down = [z * 4 + 2 + c for z in reversed(range(n // 4)) for c in range(2)]
    return up + down


def ring_scatter(values, n):
    return lax.psum_scatter(
        values, "batch", scatter_dimension=0, tiled=True, axis_index_groups=[ring_order(n)]
    )


def ring_gather(own, n):
    return lax.all_gather(own, "batch", axis=0, tiled=True, axis_index_groups=[ring_order(n)])


def send(values, pairs):
    return lax.ppermute(values, "batch", pairs)


def exchange(values, bit, n):
    return send(values, [(i, i ^ bit) for i in range(n)])


def added(left, right):
    return (left.astype(WIDE) + right.astype(WIDE)).astype(LOW)


def then(done, *values):
    return lax.optimization_barrier((done, values))[1]


def ring_view(values, n):
    bits = max(n.bit_length() - 3, 0)
    return values.reshape((2,) + (2,) * bits + (2, values.shape[0] // n, values.shape[1]))


def ring_half(bit, place, n):
    dims = n.bit_length()
    mine = (place // bit) % 2
    if bit == 1:
        return dims - 2, mine
    if bit == 2:
        return 0, mine
    return dims - 1 - bit.bit_length() + 1, mine ^ ((place // 2) % 2)


def pair_send(values, bit, place, n):
    dim, mine = ring_half(bit, place, n)
    return exchange(lax.dynamic_slice_in_dim(values, 1 - mine, 1, dim), bit, n)


def pair_add(values, arrived, bit, place, n):
    dim, mine = ring_half(bit, place, n)
    return added(lax.dynamic_slice_in_dim(values, mine, 1, dim), arrived)


def pair_join(mine, other, bit, place, n):
    dim, half = ring_half(bit, place, n)
    return both_halves(mine, other, half == 0, dim)


def small_sums(values, n, afters):
    bit = 1
    while bit < n:
        bits = (bit, 2 * bit, 3 * bit) if bit * 4 <= n else (bit,)
        moved = [exchange(values, b, n) for b in bits]
        if afters:
            moved = then(afters.pop(0), *moved)
        values = values + moved[0]
        if len(bits) == 3:
            values = values + (moved[1] + moved[2])
        bit *= 4
    return values


def on_device(n_batch, tokens, ln_gain, w_qkv, qk_gain, w_out, w_up, b_up, w_down, b_out,
              cotangent, slot_image, token_valid):
    rows, half = tokens.shape
    width = 2 * half
    slots = slot_image.shape[0]
    slot_rows = rows // slots
    side = lax.axis_index("head")
    first = side == 0
    place = lax.axis_index("batch")
    sides = jnp.reshape(side, (1,)).astype(jnp.int32)
    columns, inner = w_qkv.shape[1] // 2, w_out.shape[0] // 2
    bits = []
    while 4 * 2 ** len(bits) < n_batch:
        bits.append(4 * 2 ** len(bits))

    other_tokens = swap(tokens, "head")
    (held,) = then(tokens, cotangent)
    other_cotangent = swap(held, "head")

    token_image = jnp.repeat(slot_image, slot_rows, total_repeat_length=rows)
    ids = lax.broadcasted_iota(jnp.int32, (HD, rows), 0)
    same = token_image[None, :] == ids
    query_mark = jnp.where(same, 1.0, 0.0).astype(LOW)
    key_mark = jnp.where(same & (token_valid == 1)[None, :], 0.0, FAR)
    key_mark = jnp.where(ids < slots, key_mark, 0.0).astype(LOW)
    gains = qk_gain.reshape(-1, 1)
    grad_b_out = jnp.sum(cotangent.astype(WIDE), axis=0)
    (query_mark, key_mark, gains, grad_b_out), other_tokens = lax.optimization_barrier(
        ((query_mark, key_mark, gains, grad_b_out), other_tokens)
    )

    normed, stats = input_norm(sides, tokens, other_tokens, ln_gain)
    hidden, slope = mlp_forward(normed, w_up, b_up)
    piece = both_halves(cotangent, other_cotangent, first, 1)
    grad_pre, grad_b_up = mlp_slope(piece, w_down, slope)
    mlp_part = mlp_weights(hidden, piece, normed, grad_pre)
    mlp_own = ring_scatter(mlp_part, n_batch)

    def prepared(group, after):
        some, part = then(after, normed, piece)
        joined_t = contract(w_qkv[:, group * columns : (group + 1) * columns], some, 0, 1)
        return joined_t, contract(w_out[group * inner : (group + 1) * inner], part, 1, 1).astype(LOW)

    def two_heads(ready, skip, after):
        joined_t, grad_t = then(after, *ready)
        return attention([joined_t], [grad_t], gains, query_mark, key_mark, skip)

    def sent(part, bit):
        return pair_send(part, bit, place, n_batch)

    def summed(after, part, arrived, bit):
        (arrived,) = then(after, arrived)
        return pair_add(part, arrived, bit, place, n_batch)

    ready0 = prepared(0, mlp_part)
    pair0 = two_heads(ready0, 0, ready0)
    pair1 = two_heads(ready0, 1, pair0)
    part0 = ring_view(
        heads_weights(normed, [pair0[1], pair1[1]], piece, [pair0[0], pair1[0]]), n_batch
    )
    way0 = sent(part0, 1)
    ready1 = prepared(1, part0)
    part0 = summed(ready1, part0, way0, 1)
    way0 = sent(part0, 2)
    pair2 = two_heads(ready1, 0, part0)
    pair3 = two_heads(ready1, 1, pair2)
    part1 = heads_weights(normed, [pair2[1], pair3[1]], piece, [pair2[0], pair3[0]])
    part0 = summed(part1, part0, way0, 2)
    way0 = sent(part0, bits[0])
    (part1,) = then(part0, part1)
    part1 = ring_view(part1, n_batch)
    way1 = sent(part1, 1)
    attended = [pair0[0], pair1[0], pair2[0], pair3[0]]
    grad_joined = [pair0[1], pair1[1], pair2[1], pair3[1]]
    branch = (sides, w_out, hidden, w_down, attended)
    back = (sides, w_qkv, grad_pre, w_up, grad_joined)
    (away_in,) = grad_in_half(False, *then(part1, *back))
    arrived_in = swap(away_in, "head")
    part1 = summed(away_in, part1, way1, 1)
    way1 = sent(part1, 2)
    (mlp_own,) = then(part1, mlp_own)
    mlp_whole = ring_gather(mlp_own, n_batch)
    away_out = output_half(False, *then(mlp_own, *branch))
    arrived_out = swap(away_out, "head")
    for bit, after in zip(bits, bits[1:] + [0]):
        part0 = summed(away_out, part0, way0, bit)
        if after:
            way0 = sent(part0, after)
    part1 = summed(part0, part1, way1, 2)
    way1 = sent(part1, bits[0])
    hat, sums, grad_ln = grad_in_half(
        True, *then(part1, *back), tokens, arrived_in, stats, ln_gain.reshape(1, width)
    )
    gain_grad = jnp.sum(pair0[2] + pair1[2] + pair2[2] + pair3[2], axis=1).reshape(2, HD)
    joint = jnp.concatenate([sums[:, 0:2].T, gain_grad], axis=1)
    joint_other = swap(joint, "head")
    done = (hat, arrived_out)
    for bit, after in zip(bits, bits[1:] + [0]):
        part1 = summed(done, part1, way1, bit)
        done = (part1, joint_other)
        if after:
            way1 = sent(part1, after)
    heads_own = jnp.concatenate([p.reshape(-1, width) for p in (part0, part1)], axis=0)
    heads_whole = ring_gather(heads_own, n_batch)
    sums_other = joint_other[:, 0:rows].T
    gain_grad = (gain_grad + joint_other[:, rows:]).reshape(-1)
    small = jnp.concatenate([grad_ln[0], grad_b_out, grad_b_up[0], gain_grad])
    (mlp_whole,) = then(heads_own, mlp_whole)
    grad_wd, grad_wup = mlp_spread(mlp_whole)
    grad_tokens = grad_in_finish(*then(grad_wd, cotangent, tokens, stats, hat, sums, sums_other))
    output = output_half(
        True, *then(grad_tokens, *branch), tokens, arrived_out, b_out.reshape(1, half)
    )
    small = small_sums(small, n_batch, [grad_wd, output])
    units = b_up.shape[0]
    (heads_whole,) = then((output, grad_tokens, small), heads_whole)
    grad_wqkv, grad_wo = heads_spread(heads_whole, n_batch, columns, 2)
    return (
        output,
        grad_tokens,
        small[0:half],
        grad_wqkv,
        small[2 * half + units :].reshape(qk_gain.shape),
        grad_wo,
        grad_wup,
        small[2 * half : 2 * half + units],
        grad_wd,
        small[half : 2 * half],
    )


def solution(mesh):
    placed = (
        P("batch", "head"),
        P(),
        P(None, "head"),
        P(),
        P("head", None),
        P(None, "head"),
        P("head"),
        P("head", None),
        P("head"),
        P("batch", "head"),
        P("batch"),
        P("batch"),
    )
    return jax.shard_map(
        functools.partial(on_device, mesh.shape["batch"]),
        mesh=mesh,
        in_specs=placed,
        out_specs=(
            P("batch", "head"),
            P("batch", "head"),
            P("head"),
            P(None, "head"),
            P(),
            P("head", None),
            P(None, "head"),
            P("head"),
            P("head", None),
            P("head"),
        ),
        check_vma=False,
    )
```

```python
import functools

import jax
import jax.numpy as jnp
from jax import lax
from jax.experimental import pallas as pl
from jax.experimental.pallas import tpu as pltpu
from jax.sharding import PartitionSpec as P

HD = 64
EPSILON = 1e-06
FAR = -16384.0
LOW = jnp.bfloat16
WIDE = jnp.float32
MIB = 1024 * 1024
SHORT = pl.CostEstimate(flops=1024, bytes_accessed=1024, transcendentals=0)


def contract(left, right, left_dim, right_dim):
    return lax.dot_general(
        left, right, (((left_dim,), (right_dim,)), ((), ())), preferred_element_type=WIDE
    )


def swap(values, axis):
    return lax.ppermute(values, axis, [(0, 1), (1, 0)])


def both_halves(mine, other, first, dim):
    return jnp.where(
        first,
        jnp.concatenate([mine, other], axis=dim),
        jnp.concatenate([other, mine], axis=dim),
    )


def mlp_body(normed_ref, w_ref, b_ref, hidden_ref, slope_ref):
    pre = jnp.dot(normed_ref[...], w_ref[...], preferred_element_type=WIDE) + b_ref[...]
    cdf = 0.5 * (1.0 + lax.erf(pre * (0.5**0.5)))
    density = jnp.exp(-0.5 * pre * pre) * 0.3989422804014327
    hidden_ref[...] = (pre * cdf).astype(LOW)
    slope_ref[...] = (cdf + pre * density).astype(LOW)


def streamed(values):
    return pltpu.with_memory_space_constraint(values, pltpu.HBM)


def mlp_forward(normed, w_up, b_up):
    rows, width = normed.shape
    units = w_up.shape[1]
    block = 512
    return pl.pallas_call(
        mlp_body,
        grid=(units // block,),
        in_specs=[
            pl.BlockSpec((rows, width), lambda i: (0, 0)),
            pl.BlockSpec((width, block), lambda i: (0, i)),
            pl.BlockSpec((1, block), lambda i: (0, i)),
        ],
        out_specs=[
            pl.BlockSpec((rows, block), lambda i: (0, i)),
            pl.BlockSpec((rows, block), lambda i: (0, i)),
        ],
        out_shape=[
            jax.ShapeDtypeStruct((rows, units), LOW),
            jax.ShapeDtypeStruct((rows, units), LOW),
        ],
        compiler_params=pltpu.CompilerParams(vmem_limit_bytes=16 * MIB),
        cost_estimate=SHORT,
        name="mlp_forward",
    )(normed, streamed(w_up), b_up.reshape(1, units))


def norm_body(side_ref, mine_ref, other_ref, gain_ref, normed_ref, stats_ref):
    mine = mine_ref[...].astype(WIDE)
    other = other_ref[...].astype(WIDE)
    width = 2 * mine.shape[1]
    half = mine.shape[1]
    center = (
        jnp.sum(mine, axis=1, keepdims=True) + jnp.sum(other, axis=1, keepdims=True)
    ) / width
    mine = mine - center
    other = other - center
    spread = (
        jnp.sum(mine * mine, axis=1, keepdims=True)
        + jnp.sum(other * other, axis=1, keepdims=True)
    ) / width
    scaled = lax.rsqrt(spread + EPSILON)
    first = side_ref[0] == 0
    left = jnp.where(first, mine, other)
    right = jnp.where(first, other, mine)
    normed_ref[:, 0:half] = (left * scaled * gain_ref[:, 0:half]).astype(LOW)
    normed_ref[:, half:width] = (right * scaled * gain_ref[:, half:width]).astype(LOW)
    lane = lax.broadcasted_iota(jnp.int32, stats_ref.shape, 1)
    stats_ref[...] = jnp.where(lane == 0, center, scaled)


def input_norm(side, mine, other, gain):
    rows, half = mine.shape
    block = 224
    return pl.pallas_call(
        norm_body,
        grid_spec=pltpu.PrefetchScalarGridSpec(
            num_scalar_prefetch=1,
            grid=(rows // block,),
            in_specs=[
                pl.BlockSpec((block, half), lambda i, s: (i, 0)),
                pl.BlockSpec((block, half), lambda i, s: (i, 0)),
                pl.BlockSpec((1, 2 * half), lambda i, s: (0, 0)),
            ],
            out_specs=[
                pl.BlockSpec((block, 2 * half), lambda i, s: (i, 0)),
                pl.BlockSpec((block, 128), lambda i, s: (i, 0)),
            ],
        ),
        out_shape=[
            jax.ShapeDtypeStruct((rows, 2 * half), LOW),
            jax.ShapeDtypeStruct((rows, 128), WIDE),
        ],
        cost_estimate=SHORT,
        name="input_norm",
    )(side, mine, other, gain.reshape(1, 2 * half))


def slope_body(side_ref, mine_ref, other_ref, w_ref, slope_ref, grad_pre_ref, bias_ref, piece_ref):
    half = mine_ref.shape[1]

    @pl.when(pl.program_id(0) == 0)
    def _():
        first = side_ref[0] == 0
        mine, other = mine_ref[...], other_ref[...]
        piece_ref[:, 0:half] = jnp.where(first, mine, other)
        piece_ref[:, half:] = jnp.where(first, other, mine)

    back = lax.dot_general(
        piece_ref[...], w_ref[...], (((1,), (1,)), ((), ())), preferred_element_type=WIDE
    )
    low = (back * slope_ref[...].astype(WIDE)).astype(LOW)
    grad_pre_ref[...] = low
    bias_ref[...] = jnp.sum(low.astype(WIDE), axis=0, keepdims=True)


def mlp_slope(side, mine, other, w_down, slope):
    rows, half = mine.shape
    units, width = w_down.shape
    block = 512

    def whole(i, s):
        return (0, 0)

    return pl.pallas_call(
        slope_body,
        grid_spec=pltpu.PrefetchScalarGridSpec(
            num_scalar_prefetch=1,
            grid=(units // block,),
            in_specs=[
                pl.BlockSpec((rows, half), whole),
                pl.BlockSpec((rows, half), whole),
                pl.BlockSpec((block, width), lambda i, s: (i, 0)),
                pl.BlockSpec((rows, block), lambda i, s: (0, i)),
            ],
            out_specs=[
                pl.BlockSpec((rows, block), lambda i, s: (0, i)),
                pl.BlockSpec((1, block), lambda i, s: (0, i)),
                pl.BlockSpec((rows, width), whole),
            ],
        ),
        out_shape=[
            jax.ShapeDtypeStruct((rows, units), LOW),
            jax.ShapeDtypeStruct((1, units), WIDE),
            jax.ShapeDtypeStruct((rows, width), LOW),
        ],
        compiler_params=pltpu.CompilerParams(vmem_limit_bytes=20 * MIB),
        cost_estimate=SHORT,
        name="mlp_slope",
    )(side, mine, other, streamed(w_down), slope)


def first_dims(left, right):
    return lax.dot_general(left, right, (((0,), (0,)), ((), ())), preferred_element_type=WIDE)


def mlp_weights_body(down_steps, hidden_ref, piece_ref, normed_ref, grad_pre_ref, *refs):
    step = pl.program_id(0)
    out_ref = refs[-1]

    def put(total):
        if len(refs) == 2:
            total = total + refs[0][...].astype(WIDE)
        out_ref[...] = total.astype(LOW)

    @pl.when(step < down_steps)
    def _():
        put(first_dims(hidden_ref[...], piece_ref[...]))

    @pl.when(step >= down_steps)
    def _():
        put(first_dims(normed_ref[...], grad_pre_ref[...]))


def mlp_weights(hidden, piece, normed, grad_pre, *before):
    rows, units = hidden.shape
    width = piece.shape[1]
    block = 512
    down = units // block
    across = width // block
    halves = units // width

    def later(i):
        return jnp.maximum(i - down, 0)

    return pl.pallas_call(
        functools.partial(mlp_weights_body, down),
        grid=(down + halves * across,),
        in_specs=[
            pl.BlockSpec((rows, block), lambda i: (0, jnp.minimum(i, down - 1))),
            pl.BlockSpec((rows, width), lambda i: (0, 0)),
            pl.BlockSpec((rows, block), lambda i: (0, later(i) % across)),
            pl.BlockSpec((rows, width), lambda i: (0, later(i) // across)),
        ]
        + [pl.BlockSpec((block, width), lambda i: (i, 0)) for _ in before],
        out_specs=pl.BlockSpec((block, width), lambda i: (i, 0)),
        out_shape=pltpu.HBM((2 * units, width), LOW),
        input_output_aliases={4: 0} if before else {},
        compiler_params=pltpu.CompilerParams(vmem_limit_bytes=24 * MIB),
        cost_estimate=SHORT,
        name="mlp_weights",
    )(hidden, piece, normed, grad_pre, *before)


def heads_weights_body(steps, normed_ref, piece_ref, grad_joined_ref, attended_ref, out_ref):
    width = out_ref.shape[1]
    rest = grad_joined_ref.shape[1] - width

    block = out_ref.shape[0]
    lines = pl.ds(pl.multiple_of(pl.program_id(0) % steps * block, block), block)

    @pl.when(pl.program_id(0) < steps)
    def _():
        out_ref[...] = first_dims(normed_ref[:, lines], grad_joined_ref[:, 0:width]).astype(LOW)

    @pl.when(pl.program_id(0) >= steps)
    def _():
        out_ref[:, 0:rest] = first_dims(
            normed_ref[:, lines], grad_joined_ref[:, width:]
        ).astype(LOW)
        out_ref[:, rest:] = lax.dot_general(
            piece_ref[:, lines], attended_ref[...], (((0,), (1,)), ((), ())), preferred_element_type=WIDE
        ).astype(LOW)


def heads_weights(normed, grad_joined, piece, attended_t):
    rows, width = normed.shape
    block = 512
    steps = width // block
    return pl.pallas_call(
        functools.partial(heads_weights_body, steps),
        grid=(2 * steps,),
        in_specs=[
            pl.BlockSpec(normed.shape, lambda i: (0, 0)),
            pl.BlockSpec(piece.shape, lambda i: (0, 0)),
            pl.BlockSpec(grad_joined.shape, lambda i: (0, 0)),
            pl.BlockSpec(attended_t.shape, lambda i: (0, 0)),
        ],
        out_specs=pl.BlockSpec((block, width), lambda i: (i, 0)),
        out_shape=pltpu.HBM((2 * width, width), LOW),
        compiler_params=pltpu.CompilerParams(vmem_limit_bytes=20 * MIB),
        cost_estimate=SHORT,
        name="heads_weights",
    )(normed, piece, grad_joined, attended_t)


def spread_body(mlp_ref, left_ref, right_ref, down_ref, up_ref, qkv_ref, out_ref):
    step = pl.program_id(0)
    steps = pl.num_programs(0)

    @pl.when(step < steps // 2)
    def _():
        down_ref[...] = mlp_ref[...].astype(WIDE).reshape(down_ref.shape)

    @pl.when(step >= steps // 2)
    def _():
        up_ref[...] = mlp_ref[...].astype(WIDE).reshape(up_ref.shape)

    lines, columns = qkv_ref.shape
    width = left_ref.shape[-1]
    qkv_ref[:, 0:width] = left_ref[...].astype(WIDE).reshape(lines, width)
    right = right_ref[...].astype(WIDE).reshape(lines, width)
    qkv_ref[:, width:columns] = right[:, 0 : columns - width]
    out_ref[...] = jnp.transpose(right[:, columns - width :])


def spread(whole, n, units, columns):
    width = whole.shape[1]
    mlp_rows, heads_rows = 2 * units // n, 2 * width // n
    assert whole.shape[0] == n * (mlp_rows + heads_rows) and mlp_rows % heads_rows == 0
    steps = width // 128
    block = 2 * units // steps
    inner = 2 * width - columns
    across = width // block
    skip = mlp_rows // heads_rows

    def later(i):
        return jnp.maximum(i - steps // 2, 0)

    by_rows = streamed(whole.reshape(n, -1, width))
    by_parts = streamed(whole.reshape(n, -1, heads_rows, width))
    part = (n // (2 * steps), 1, heads_rows, width)
    return pl.pallas_call(
        spread_body,
        grid=(steps,),
        in_specs=[
            pl.BlockSpec((n // steps, mlp_rows, width), lambda i: (i, 0, 0)),
            pl.BlockSpec(part, lambda i: (i, skip, 0, 0)),
            pl.BlockSpec(part, lambda i: (i + steps, skip, 0, 0)),
        ],
        out_specs=[
            pl.BlockSpec((block, width), lambda i: (jnp.minimum(i, steps // 2 - 1), 0)),
            pl.BlockSpec((block, width), lambda i: (later(i) % across, later(i) // across)),
            pl.BlockSpec((128, columns), lambda i: (i, 0)),
            pl.BlockSpec((inner, 128), lambda i: (0, i)),
        ],
        out_shape=[
            jax.ShapeDtypeStruct((units, width), WIDE),
            jax.ShapeDtypeStruct((width, units), WIDE),
            jax.ShapeDtypeStruct((width, columns), WIDE),
            jax.ShapeDtypeStruct((inner, width), WIDE),
        ],
        compiler_params=pltpu.CompilerParams(vmem_limit_bytes=32 * MIB),
        cost_estimate=SHORT,
        name="spread",
    )(by_rows, by_parts, by_parts)


def output_body(count, side_ref, w_out_ref, hidden_ref, w_down_ref, *refs):
    attended_refs, (away_ref, kept_ref) = refs[:count], refs[count:]
    step = pl.program_id(0)
    attended = jnp.concatenate([ref[...] for ref in attended_refs], axis=0)
    total = jnp.dot(
        hidden_ref[...], w_down_ref[...], preferred_element_type=WIDE
    ) + first_dims(attended, w_out_ref[...])

    @pl.when(step == 0)
    def _():
        away_ref[...] = total.astype(LOW)

    @pl.when(step == 1)
    def _():
        kept_ref[...] = total


def output_terms(side, w_out, hidden, w_down, attended_t):
    rows, units = hidden.shape
    inner, width = w_out.shape
    half = width // 2

    def column(i, s):
        return (0, s[0] ^ (1 - i))

    def whole(i, s):
        return (0, 0)

    return pl.pallas_call(
        functools.partial(output_body, len(attended_t)),
        grid_spec=pltpu.PrefetchScalarGridSpec(
            num_scalar_prefetch=1,
            grid=(2,),
            in_specs=[
                pl.BlockSpec((inner, half), column),
                pl.BlockSpec((rows, units), whole),
                pl.BlockSpec((units, half), column),
            ]
            + [pl.BlockSpec(v.shape, whole) for v in attended_t],
            out_specs=[pl.BlockSpec((rows, half), whole)] * 2,
        ),
        out_shape=[
            jax.ShapeDtypeStruct((rows, half), LOW),
            jax.ShapeDtypeStruct((rows, half), WIDE),
        ],
        compiler_params=pltpu.CompilerParams(vmem_limit_bytes=24 * MIB),
        cost_estimate=SHORT,
        name="output_terms",
    )(side, w_out, hidden, w_down, *attended_t)


def second_dims(left, right):
    return lax.dot_general(left, right, (((1,), (1,)), ((), ())), preferred_element_type=WIDE)


def grad_in_body(count, side_ref, w_qkv_ref, grad_pre_ref, w_up_ref, *refs):
    away_ref, kept_ref = refs[count:]
    step = pl.program_id(0)
    grad_joined = jnp.concatenate([ref[...] for ref in refs[:count]], axis=1)
    total = second_dims(grad_joined, w_qkv_ref[...]) + second_dims(
        grad_pre_ref[...], w_up_ref[...]
    )

    @pl.when(step == 0)
    def _():
        away_ref[...] = total.astype(LOW)

    @pl.when(step == 1)
    def _():
        kept_ref[...] = total


def grad_in_terms(side, w_qkv, grad_pre, w_up, grad_joined):
    rows, units = grad_pre.shape
    width, columns = w_qkv.shape
    half = width // 2

    def picked(i, s):
        return (s[0] ^ (1 - i), 0)

    def whole(i, s):
        return (0, 0)

    return pl.pallas_call(
        functools.partial(grad_in_body, len(grad_joined)),
        grid_spec=pltpu.PrefetchScalarGridSpec(
            num_scalar_prefetch=1,
            grid=(2,),
            in_specs=[
                pl.BlockSpec((half, columns), picked),
                pl.BlockSpec((rows, units), whole),
                pl.BlockSpec((half, units), picked),
            ]
            + [pl.BlockSpec(v.shape, whole) for v in grad_joined],
            out_specs=[pl.BlockSpec((rows, half), whole)] * 2,
        ),
        out_shape=[
            jax.ShapeDtypeStruct((rows, half), LOW),
            jax.ShapeDtypeStruct((rows, half), WIDE),
        ],
        compiler_params=pltpu.CompilerParams(vmem_limit_bytes=24 * MIB),
        cost_estimate=SHORT,
        name="grad_in_terms",
    )(side, streamed(w_qkv), grad_pre, streamed(w_up), *grad_joined)


def hat_body(side_ref, kept_ref, arrived_ref, tokens_ref, stats_ref, gain_ref,
             hat_ref, sums_ref, gain_grad_ref):
    total = kept_ref[...] + arrived_ref[...].astype(WIDE)
    stats = stats_ref[...]
    x_hat = (tokens_ref[...].astype(WIDE) - stats[:, 0:1]) * stats[:, 1:2]
    grad_hat = total * gain_ref[...]
    hat_ref[...] = grad_hat
    lane = lax.broadcasted_iota(jnp.int32, stats.shape, 1)
    sums_ref[...] = jnp.where(
        lane == 0,
        jnp.sum(grad_hat, axis=1, keepdims=True),
        jnp.sum(grad_hat * x_hat, axis=1, keepdims=True),
    )

    @pl.when(pl.program_id(0) == 0)
    def _():
        gain_grad_ref[...] = jnp.zeros_like(gain_grad_ref)

    gain_grad_ref[...] += jnp.sum(total * x_hat, axis=0, keepdims=True)


def grad_in_hat(side, kept, arrived, tokens, stats, gain):
    rows, half = tokens.shape
    block = 448

    def rows_of(columns):
        return pl.BlockSpec((block, columns), lambda i, s: (i, 0))

    return pl.pallas_call(
        hat_body,
        grid_spec=pltpu.PrefetchScalarGridSpec(
            num_scalar_prefetch=1,
            grid=(rows // block,),
            in_specs=[rows_of(half), rows_of(half), rows_of(half), rows_of(128),
                      pl.BlockSpec((1, half), lambda i, s: (0, s[0]))],
            out_specs=[rows_of(half), rows_of(128), pl.BlockSpec((1, half), lambda i, s: (0, 0))],
        ),
        out_shape=[
            jax.ShapeDtypeStruct((rows, half), WIDE),
            jax.ShapeDtypeStruct((rows, 128), WIDE),
            jax.ShapeDtypeStruct((1, half), WIDE),
        ],
        cost_estimate=SHORT,
        name="grad_in_hat",
    )(side, kept, arrived, tokens, stats, gain)


def finish_body(cotangent_ref, tokens_ref, stats_ref, hat_ref, sums_ref, other_ref, out_ref):
    width = 2 * tokens_ref.shape[1]
    scaled = stats_ref[:, 1:2]
    x_hat = (tokens_ref[...].astype(WIDE) - stats_ref[:, 0:1]) * scaled
    sums = (sums_ref[:, 0:2] + other_ref[...]) / width
    out_ref[...] = (
        cotangent_ref[...].astype(WIDE)
        + scaled * (hat_ref[...] - sums[:, 0:1] - x_hat * sums[:, 1:2])
    ).astype(LOW)


def grad_in_finish(cotangent, tokens, stats, hat, sums, other):
    rows, half = tokens.shape
    block = 224

    def rows_of(columns):
        return pl.BlockSpec((block, columns), lambda i: (i, 0))

    return pl.pallas_call(
        finish_body,
        grid=(rows // block,),
        in_specs=[rows_of(c) for c in (half, half, 128, half, 128, 2)],
        out_specs=rows_of(half),
        out_shape=jax.ShapeDtypeStruct((rows, half), LOW),
        cost_estimate=SHORT,
        name="grad_in_finish",
    )(cotangent, tokens, stats, hat, sums, other)


def part_norm(values):
    center = jnp.mean(values, axis=0, keepdims=True)
    shifted = values - center
    scaled = lax.rsqrt(jnp.mean(shifted * shifted, axis=0, keepdims=True) + EPSILON)
    return shifted * scaled, scaled


def part_norm_back(grad, normal, scaled, gain):
    g = grad * gain
    inner = jnp.mean(g * normal, axis=0, keepdims=True)
    return scaled * (g - jnp.mean(g, axis=0, keepdims=True) - normal * inner)


def lane_fold(values):
    total = values[:, 0:128]
    for start in range(128, values.shape[1], 128):
        total = total + values[:, start : start + 128]
    return total


def attention_body(rows, tiles, count, *refs):
    joined_refs, grad_refs = refs[:count], refs[count : 2 * count]
    (gain_ref, query_mark_ref, key_mark_ref, attended_ref, grad_joined_ref, gain_grad_ref,
     key_grad, value_grad) = refs[2 * count :]

    def part(some, r0, r1):
        return jnp.concatenate([ref[r0:r1, :] for ref in some], axis=1)

    factor = float(HD) ** (-0.5)
    gain_query = gain_ref[0:HD, :]
    gain_key = gain_ref[HD : 2 * HD, :]
    pieces = []
    gain_sum_query = jnp.zeros((HD, 128), WIDE)
    gain_sum_key = jnp.zeros((HD, 128), WIDE)
    one_mark = jnp.where(lax.broadcasted_iota(jnp.int32, (HD, rows), 0) < 2, 1.0, 0.0).astype(LOW)
    for head in range(2):
        base = head * 3 * HD
        query_hat, query_scale = part_norm(part(joined_refs, base, base + HD))
        key_hat, key_scale = part_norm(part(joined_refs, base + HD, base + 2 * HD))
        value_t = part(joined_refs, base + 2 * HD, base + 3 * HD).astype(LOW)
        query_t = (query_hat * gain_query).astype(LOW)
        key_t = (key_hat * gain_key).astype(LOW)
        grad_t = part(grad_refs, head * HD, (head + 1) * HD)
        query_aug = jnp.concatenate([query_t * factor, query_mark_ref[...]], axis=0)
        key_aug = jnp.transpose(jnp.concatenate([key_t, key_mark_ref[...]], axis=0))
        value_aug_t = jnp.concatenate([value_t, one_mark], axis=0)
        value_aug = jnp.transpose(value_aug_t)
        query_grads = []
        for number, (q0, q1, k0, k1) in enumerate(tiles):
            scores = jnp.dot(key_aug[k0:k1], query_aug[:, q0:q1], preferred_element_type=WIDE)
            terms = jnp.exp(scores)
            terms_low = terms.astype(LOW)
            summed = jnp.dot(value_aug_t[:, k0:k1], terms_low, preferred_element_type=WIDE)
            inverse = 1.0 / summed[HD : HD + 1, :]
            attended = summed[0:HD, :] * inverse
            attended_ref[head * HD : (head + 1) * HD, q0:q1] = attended.astype(LOW)
            grad_tile = grad_t[:, q0:q1].astype(WIDE)
            row_inner = jnp.sum(grad_tile * attended, axis=0, keepdims=True)
            inner_high = row_inner.astype(LOW)
            inner_low = (row_inner - inner_high.astype(WIDE)).astype(LOW)
            place = lax.broadcasted_iota(jnp.int32, (HD, q1 - q0), 0)
            inner_mark = jnp.where(
                place == 0,
                -inner_high.astype(WIDE),
                jnp.where(place == 1, -inner_low.astype(WIDE), 0.0),
            ).astype(LOW)
            grad_aug = jnp.concatenate([grad_t[:, q0:q1], inner_mark], axis=0)
            shifted = jnp.dot(value_aug[k0:k1], grad_aug, preferred_element_type=WIDE)
            grad_scores = (terms * shifted).astype(LOW)
            query_grads.append(
                jnp.dot(key_t[:, k0:k1], grad_scores, preferred_element_type=WIDE)
                * (inverse * factor)
            )
            query_rows = jnp.transpose(
                jnp.concatenate(
                    [query_t[:, q0:q1].astype(WIDE) * (inverse * factor), grad_tile * inverse],
                    axis=0,
                ).astype(LOW)
            )
            key_term = jnp.dot(grad_scores, query_rows, preferred_element_type=WIDE)
            value_term = jnp.dot(terms_low, query_rows, preferred_element_type=WIDE)
            if number == 0:
                key_grad[k0:k1, :] = key_term
                value_grad[k0:k1, :] = value_term
                key_grad[k1:rows, :] = jnp.zeros((rows - k1, 2 * HD), WIDE)
                value_grad[k1:rows, :] = jnp.zeros((rows - k1, 2 * HD), WIDE)
            else:
                key_grad[k0:k1, :] += key_term
                value_grad[k0:k1, :] += value_term
        lane = lax.broadcasted_iota(jnp.int32, (rows, 2 * HD), 1)
        joint = jnp.transpose(jnp.where(lane < HD, key_grad[...], value_grad[...]))
        query_grad = jnp.concatenate(query_grads, axis=1)
        key_grad_t = joint[0:HD, :]
        gain_sum_query += lane_fold(query_grad * query_hat)
        gain_sum_key += lane_fold(key_grad_t * key_hat)
        pieces += [
            part_norm_back(query_grad, query_hat, query_scale, gain_query),
            part_norm_back(key_grad_t, key_hat, key_scale, gain_key),
            joint[HD : 2 * HD, :],
        ]
    grad_joined_ref[...] = jnp.transpose(jnp.concatenate(pieces, axis=0)).astype(LOW)

    @pl.when(pl.program_id(0) == 0)
    def _():
        gain_grad_ref[...] = jnp.zeros_like(gain_grad_ref)

    gain_grad_ref[...] += jnp.concatenate([gain_sum_query, gain_sum_key], axis=0)


def attention(joined_t, grad_t, gains, query_mark, key_mark, skip, pairs):
    rows = query_mark.shape[1]
    heads = 2 * pairs
    width = heads * 3 * HD
    far = 3 * (rows // 4)
    tiles = ((0, 512, 0, far), (512, 768, 0, rows), (768, rows, far, rows))

    def whole(i):
        return (0, 0)

    return pl.pallas_call(
        functools.partial(attention_body, rows, tiles, len(joined_t)),
        grid=(heads // 2,),
        in_specs=[pl.BlockSpec((6 * HD, v.shape[1]), lambda i: (i + skip, 0)) for v in joined_t]
        + [pl.BlockSpec((2 * HD, v.shape[1]), lambda i: (i + skip, 0)) for v in grad_t]
        + [
            pl.BlockSpec((2 * HD, 1), whole),
            pl.BlockSpec((HD, rows), whole),
            pl.BlockSpec((HD, rows), whole),
        ],
        out_specs=[
            pl.BlockSpec((2 * HD, rows), lambda i: (i, 0)),
            pl.BlockSpec((rows, 6 * HD), lambda i: (0, i)),
            pl.BlockSpec((2 * HD, 128), whole),
        ],
        out_shape=[
            jax.ShapeDtypeStruct((heads * HD, rows), LOW),
            jax.ShapeDtypeStruct((rows, width), LOW),
            jax.ShapeDtypeStruct((2 * HD, 128), WIDE),
        ],
        scratch_shapes=[
            pltpu.VMEM((rows, 2 * HD), WIDE),
            pltpu.VMEM((rows, 2 * HD), WIDE),
        ],
        compiler_params=pltpu.CompilerParams(vmem_limit_bytes=20 * MIB),
        cost_estimate=SHORT,
        name="attention_both",
    )(*joined_t, *grad_t, gains, query_mark, key_mark)


def ring_order(n):
    if n % 4:
        return list(range(n))
    up = [z * 4 + c for z in range(n // 4) for c in range(2)]
    down = [z * 4 + 2 + c for z in reversed(range(n // 4)) for c in range(2)]
    return up + down


def ring_scatter(values, n):
    return lax.psum_scatter(
        values, "batch", scatter_dimension=0, tiled=True, axis_index_groups=[ring_order(n)]
    )


def chips_scatter(values, n):
    order = ring_order(n)
    groups = [order[0::2], order[1::2]]
    return lax.psum_scatter(
        values, "batch", scatter_dimension=0, tiled=True, axis_index_groups=groups
    )


def ring_gather(own, n):
    return lax.all_gather(own, "batch", axis=0, tiled=True, axis_index_groups=[ring_order(n)])


def send(values, pairs):
    return lax.ppermute(values, "batch", pairs)


def exchange(values, bit, n):
    return send(values, [(i, i ^ bit) for i in range(n)])


def added(left, right):
    return (left.astype(WIDE) + right.astype(WIDE)).astype(LOW)


def then(done, *values):
    return lax.optimization_barrier((done, values))[1]


def ring_view(values, n):
    bits = max(n.bit_length() - 3, 0)
    return values.reshape((2,) + (2,) * bits + (2, values.shape[0] // n, values.shape[1]))


def ring_half(bit, place, n):
    dims = n.bit_length()
    mine = (place // bit) % 2
    if bit == 1:
        return dims - 2, mine
    if bit == 2:
        return 0, mine
    return dims - 1 - bit.bit_length() + 1, mine ^ ((place // 2) % 2)


def pair_send(values, bit, place, n):
    dim, mine = ring_half(bit, place, n)
    return exchange(lax.dynamic_slice_in_dim(values, 1 - mine, 1, dim), bit, n)


def pair_add(values, arrived, bit, place, n):
    dim, mine = ring_half(bit, place, n)
    return added(lax.dynamic_slice_in_dim(values, mine, 1, dim), arrived)


def pair_join(mine, other, bit, place, n):
    dim, half = ring_half(bit, place, n)
    return both_halves(mine, other, half == 0, dim)


def line_place(place, n):
    count = n // 4
    up = place // 4
    return jnp.where((place // 2) % 2 == 0, up, count - 1 - up), count


def line_send(values, place, n):
    mine, count = line_place(place, n)
    blocks = values.reshape(count, values.size // count // values.shape[-1], values.shape[-1])
    return blocks, [
        exchange(lax.dynamic_index_in_dim(blocks, mine ^ k, 0, False), 4 * k, n)
        for k in range(1, count)
    ]


def line_add(blocks, arrived, place, n):
    mine, _ = line_place(place, n)
    total = lax.dynamic_index_in_dim(blocks, mine, 0, False).astype(WIDE)
    for values in arrived:
        total = total + values.astype(WIDE)
    return total.astype(LOW)


def small_sums(values, n, afters):
    bit = 1
    while bit < n:
        bits = (bit, 2 * bit, 3 * bit) if bit * 4 <= n else (bit,)
        moved = [exchange(values, b, n) for b in bits]
        if afters:
            moved = then(afters.pop(0), *moved)
        values = values + moved[0]
        if len(bits) == 3:
            values = values + (moved[1] + moved[2])
        bit *= 4
    return values


def on_device(n_batch, tokens, ln_gain, w_qkv, qk_gain, w_out, w_up, b_up, w_down, b_out,
              cotangent, slot_image, token_valid):
    rows, half = tokens.shape
    width = 2 * half
    slots = slot_image.shape[0]
    slot_rows = rows // slots
    side = lax.axis_index("head")
    first = side == 0
    place = lax.axis_index("batch")
    sides = jnp.reshape(side, (1,)).astype(jnp.int32)
    bits = []
    while 4 * 2 ** len(bits) < n_batch:
        bits.append(4 * 2 ** len(bits))

    other_tokens = swap(tokens, "head")
    (held,) = then(tokens, cotangent)
    other_cotangent = swap(held, "head")

    token_image = jnp.repeat(slot_image, slot_rows, total_repeat_length=rows)
    ids = lax.broadcasted_iota(jnp.int32, (HD, rows), 0)
    same = token_image[None, :] == ids
    query_mark = jnp.where(same, 1.0, 0.0).astype(LOW)
    key_mark = jnp.where(same & (token_valid == 1)[None, :], 0.0, FAR)
    key_mark = jnp.where(ids < slots, key_mark, 0.0).astype(LOW)
    gains = qk_gain.reshape(-1, 1)
    grad_b_out = jnp.sum(cotangent.astype(WIDE), axis=0)
    (query_mark, key_mark, gains, grad_b_out), other_tokens = lax.optimization_barrier(
        ((query_mark, key_mark, gains, grad_b_out), other_tokens)
    )

    normed, stats = input_norm(sides, tokens, other_tokens, ln_gain)
    hidden, slope = mlp_forward(normed, w_up, b_up)
    grad_pre, grad_b_up, piece = mlp_slope(sides, cotangent, other_cotangent, w_down, slope)
    mlp_part = mlp_weights(hidden, piece, normed, grad_pre)
    mlp_own = ring_scatter(mlp_part, n_batch)

    def sent(part, bit):
        return pair_send(part, bit, place, n_batch)

    def summed(after, part, arrived, bit):
        (arrived,) = then(after, arrived)
        return pair_add(part, arrived, bit, place, n_batch)

    part, some = then(mlp_part, piece, normed)
    joined_t = contract(w_qkv, some, 0, 1)
    grad_t = contract(w_out, part, 1, 1).astype(LOW)
    marks = (gains, query_mark, key_mark)
    pairs = w_out.shape[0] // (2 * HD)
    joined_t, grad_t = then((joined_t, grad_t), joined_t, grad_t)
    attended, grad_joined, gain_grad = attention([joined_t], [grad_t], *marks, 0, pairs)
    heads_part = heads_weights(normed, grad_joined, piece, attended)
    heads_part = ring_view(heads_part, n_batch)
    branch = (sides, w_out, hidden, w_down, [attended])
    back = (sides, w_qkv, grad_pre, w_up, [grad_joined])
    way = sent(heads_part, 1)
    heads_part = summed(heads_part, heads_part, way, 1)
    mlp_own, heads_part = then(heads_part, mlp_own, heads_part)
    heads_own = chips_scatter(heads_part.reshape(-1, width), n_batch)
    mlp_rows = mlp_own.shape[0]
    away_in, kept_in = grad_in_terms(*then(mlp_own, *back))
    arrived_in = swap(away_in, "head")
    (mlp_own,) = then(away_in, mlp_own)
    own = lax.dynamic_update_slice(
        jnp.zeros((mlp_rows + 2 * width // n_batch, width), LOW), mlp_own, (0, 0)
    )
    away_out, kept_out = output_terms(*then(away_in, *branch))
    arrived_out = swap(away_out, "head")
    own, heads_own = then((away_out, arrived_in), own, heads_own)
    own = lax.dynamic_update_slice(own, heads_own, (mlp_rows, 0))
    whole = ring_gather(own, n_batch)

    (arrived_in,) = then(own, arrived_in)
    hat, sums, grad_ln = grad_in_hat(
        sides, kept_in, arrived_in, tokens, stats, ln_gain.reshape(1, width)
    )
    gain_grad = jnp.sum(gain_grad, axis=1).reshape(2, HD)
    joint = jnp.concatenate([sums[:, 0:2].T, gain_grad], axis=1)
    joint_other = swap(joint, "head")
    (joint_other,) = then(hat, joint_other)
    sums_other = joint_other[:, 0:rows].T
    gain_grad = (gain_grad + joint_other[:, rows:]).reshape(-1)
    small = jnp.concatenate([grad_ln[0], grad_b_out, grad_b_up[0], gain_grad])
    grad_tokens = grad_in_finish(cotangent, tokens, stats, hat, sums, sums_other)
    (arrived_out,) = then(grad_tokens, arrived_out)
    output = (
        tokens.astype(WIDE) + (kept_out + arrived_out.astype(WIDE)) + b_out
    ).astype(LOW)
    small = small_sums(small, n_batch, [grad_tokens, output])
    units = b_up.shape[0]
    (whole,) = then((output, grad_tokens, small), whole)
    grad_wd, grad_wup, grad_wqkv, grad_wo = spread(whole, n_batch, units, w_qkv.shape[1])
    return (
        output,
        grad_tokens,
        small[0:half],
        grad_wqkv,
        small[2 * half + units :].reshape(qk_gain.shape),
        grad_wo,
        grad_wup,
        small[2 * half : 2 * half + units],
        grad_wd,
        small[half : 2 * half],
    )


def solution(mesh):
    placed = (
        P("batch", "head"),
        P(),
        P(None, "head"),
        P(),
        P("head", None),
        P(None, "head"),
        P("head"),
        P("head", None),
        P("head"),
        P("batch", "head"),
        P("batch"),
        P("batch"),
    )
    return jax.shard_map(
        functools.partial(on_device, mesh.shape["batch"]),
        mesh=mesh,
        in_specs=placed,
        out_specs=(
            P("batch", "head"),
            P("batch", "head"),
            P("head"),
            P(None, "head"),
            P(),
            P("head", None),
            P(None, "head"),
            P("head"),
            P("head", None),
            P("head"),
        ),
        check_vma=False,
    )
```

```python
import functools

import jax
import jax.numpy as jnp
from jax import lax
from jax.experimental import pallas as pl
from jax.experimental.pallas import tpu as pltpu
from jax.sharding import PartitionSpec as P

HD = 64
EPSILON = 1e-06
FAR = -16384.0
LOW = jnp.bfloat16
WIDE = jnp.float32
MIB = 1024 * 1024
SHORT = pl.CostEstimate(flops=1024, bytes_accessed=1024, transcendentals=0)


def contract(left, right, left_dim, right_dim):
    return lax.dot_general(
        left, right, (((left_dim,), (right_dim,)), ((), ())), preferred_element_type=WIDE
    )


def swap(values, axis):
    return lax.ppermute(values, axis, [(0, 1), (1, 0)])


def both_halves(mine, other, first, dim):
    return jnp.where(
        first,
        jnp.concatenate([mine, other], axis=dim),
        jnp.concatenate([other, mine], axis=dim),
    )


def mlp_body(normed_ref, w_ref, b_ref, hidden_ref, slope_ref):
    pre = jnp.dot(normed_ref[...], w_ref[...], preferred_element_type=WIDE) + b_ref[...]
    cdf = 0.5 * (1.0 + lax.erf(pre * (0.5**0.5)))
    density = jnp.exp(-0.5 * pre * pre) * 0.3989422804014327
    hidden_ref[...] = (pre * cdf).astype(LOW)
    slope_ref[...] = (cdf + pre * density).astype(LOW)


def streamed(values):
    return pltpu.with_memory_space_constraint(values, pltpu.HBM)


def mlp_forward(normed, w_up, b_up):
    rows, width = normed.shape
    units = w_up.shape[1]
    block = 512
    return pl.pallas_call(
        mlp_body,
        grid=(units // block,),
        in_specs=[
            pl.BlockSpec((rows, width), lambda i: (0, 0)),
            pl.BlockSpec((width, block), lambda i: (0, i)),
            pl.BlockSpec((1, block), lambda i: (0, i)),
        ],
        out_specs=[
            pl.BlockSpec((rows, block), lambda i: (0, i)),
            pl.BlockSpec((rows, block), lambda i: (0, i)),
        ],
        out_shape=[
            jax.ShapeDtypeStruct((rows, units), LOW),
            jax.ShapeDtypeStruct((rows, units), LOW),
        ],
        compiler_params=pltpu.CompilerParams(vmem_limit_bytes=16 * MIB),
        cost_estimate=SHORT,
        name="mlp_forward",
    )(normed, streamed(w_up), b_up.reshape(1, units))


def norm_body(side_ref, mine_ref, other_ref, gain_ref, normed_ref, stats_ref):
    mine = mine_ref[...].astype(WIDE)
    other = other_ref[...].astype(WIDE)
    width = 2 * mine.shape[1]
    half = mine.shape[1]
    center = (
        jnp.sum(mine, axis=1, keepdims=True) + jnp.sum(other, axis=1, keepdims=True)
    ) / width
    mine = mine - center
    other = other - center
    spread = (
        jnp.sum(mine * mine, axis=1, keepdims=True)
        + jnp.sum(other * other, axis=1, keepdims=True)
    ) / width
    scaled = lax.rsqrt(spread + EPSILON)
    first = side_ref[0] == 0
    left = jnp.where(first, mine, other)
    right = jnp.where(first, other, mine)
    normed_ref[:, 0:half] = (left * scaled * gain_ref[:, 0:half]).astype(LOW)
    normed_ref[:, half:width] = (right * scaled * gain_ref[:, half:width]).astype(LOW)
    lane = lax.broadcasted_iota(jnp.int32, stats_ref.shape, 1)
    stats_ref[...] = jnp.where(lane == 0, center, scaled)


def input_norm(side, mine, other, gain):
    rows, half = mine.shape
    block = 224
    return pl.pallas_call(
        norm_body,
        grid_spec=pltpu.PrefetchScalarGridSpec(
            num_scalar_prefetch=1,
            grid=(rows // block,),
            in_specs=[
                pl.BlockSpec((block, half), lambda i, s: (i, 0)),
                pl.BlockSpec((block, half), lambda i, s: (i, 0)),
                pl.BlockSpec((1, 2 * half), lambda i, s: (0, 0)),
            ],
            out_specs=[
                pl.BlockSpec((block, 2 * half), lambda i, s: (i, 0)),
                pl.BlockSpec((block, 128), lambda i, s: (i, 0)),
            ],
        ),
        out_shape=[
            jax.ShapeDtypeStruct((rows, 2 * half), LOW),
            jax.ShapeDtypeStruct((rows, 128), WIDE),
        ],
        cost_estimate=SHORT,
        name="input_norm",
    )(side, mine, other, gain.reshape(1, 2 * half))


def slope_body(side_ref, mine_ref, other_ref, w_ref, slope_ref, grad_pre_ref, bias_ref, piece_ref):
    half = mine_ref.shape[1]

    @pl.when(pl.program_id(0) == 0)
    def _():
        first = side_ref[0] == 0
        mine, other = mine_ref[...], other_ref[...]
        piece_ref[:, 0:half] = jnp.where(first, mine, other)
        piece_ref[:, half:] = jnp.where(first, other, mine)

    back = lax.dot_general(
        piece_ref[...], w_ref[...], (((1,), (1,)), ((), ())), preferred_element_type=WIDE
    )
    low = (back * slope_ref[...].astype(WIDE)).astype(LOW)
    grad_pre_ref[...] = low
    bias_ref[...] = jnp.sum(low.astype(WIDE), axis=0, keepdims=True)


def mlp_slope(side, mine, other, w_down, slope):
    rows, half = mine.shape
    units, width = w_down.shape
    block = 512

    def whole(i, s):
        return (0, 0)

    return pl.pallas_call(
        slope_body,
        grid_spec=pltpu.PrefetchScalarGridSpec(
            num_scalar_prefetch=1,
            grid=(units // block,),
            in_specs=[
                pl.BlockSpec((rows, half), whole),
                pl.BlockSpec((rows, half), whole),
                pl.BlockSpec((block, width), lambda i, s: (i, 0)),
                pl.BlockSpec((rows, block), lambda i, s: (0, i)),
            ],
            out_specs=[
                pl.BlockSpec((rows, block), lambda i, s: (0, i)),
                pl.BlockSpec((1, block), lambda i, s: (0, i)),
                pl.BlockSpec((rows, width), whole),
            ],
        ),
        out_shape=[
            jax.ShapeDtypeStruct((rows, units), LOW),
            jax.ShapeDtypeStruct((1, units), WIDE),
            jax.ShapeDtypeStruct((rows, width), LOW),
        ],
        compiler_params=pltpu.CompilerParams(vmem_limit_bytes=20 * MIB),
        cost_estimate=SHORT,
        name="mlp_slope",
    )(side, mine, other, streamed(w_down), slope)


def first_dims(left, right):
    return lax.dot_general(left, right, (((0,), (0,)), ((), ())), preferred_element_type=WIDE)


def mlp_weights_body(down_steps, hidden_ref, piece_ref, normed_ref, grad_pre_ref, *refs):
    step = pl.program_id(0)
    out_ref = refs[-1]

    def put(total):
        if len(refs) == 2:
            total = total + refs[0][...].astype(WIDE)
        out_ref[...] = total.astype(LOW)

    @pl.when(step < down_steps)
    def _():
        put(first_dims(hidden_ref[...], piece_ref[...]))

    @pl.when(step >= down_steps)
    def _():
        put(first_dims(normed_ref[...], grad_pre_ref[...]))


def mlp_weights(hidden, piece, normed, grad_pre, *before):
    rows, units = hidden.shape
    width = piece.shape[1]
    block = 512
    down = units // block
    across = width // block
    halves = units // width

    def later(i):
        return jnp.maximum(i - down, 0)

    return pl.pallas_call(
        functools.partial(mlp_weights_body, down),
        grid=(down + halves * across,),
        in_specs=[
            pl.BlockSpec((rows, block), lambda i: (0, jnp.minimum(i, down - 1))),
            pl.BlockSpec((rows, width), lambda i: (0, 0)),
            pl.BlockSpec((rows, block), lambda i: (0, later(i) % across)),
            pl.BlockSpec((rows, width), lambda i: (0, later(i) // across)),
        ]
        + [pl.BlockSpec((block, width), lambda i: (i, 0)) for _ in before],
        out_specs=pl.BlockSpec((block, width), lambda i: (i, 0)),
        out_shape=pltpu.HBM((2 * units, width), LOW),
        input_output_aliases={4: 0} if before else {},
        compiler_params=pltpu.CompilerParams(vmem_limit_bytes=24 * MIB),
        cost_estimate=SHORT,
        name="mlp_weights",
    )(hidden, piece, normed, grad_pre, *before)


def heads_weights_body(steps, normed_ref, piece_ref, grad_joined_ref, attended_ref, out_ref):
    width = out_ref.shape[1]
    rest = grad_joined_ref.shape[1] - width

    block = out_ref.shape[0]
    lines = pl.ds(pl.multiple_of(pl.program_id(0) % steps * block, block), block)

    @pl.when(pl.program_id(0) < steps)
    def _():
        out_ref[...] = first_dims(normed_ref[:, lines], grad_joined_ref[:, 0:width]).astype(LOW)

    @pl.when(pl.program_id(0) >= steps)
    def _():
        out_ref[:, 0:rest] = first_dims(
            normed_ref[:, lines], grad_joined_ref[:, width:]
        ).astype(LOW)
        out_ref[:, rest:] = lax.dot_general(
            piece_ref[:, lines], attended_ref[...], (((0,), (1,)), ((), ())), preferred_element_type=WIDE
        ).astype(LOW)


def heads_weights(normed, grad_joined, piece, attended_t):
    rows, width = normed.shape
    block = 512
    steps = width // block
    return pl.pallas_call(
        functools.partial(heads_weights_body, steps),
        grid=(2 * steps,),
        in_specs=[
            pl.BlockSpec(normed.shape, lambda i: (0, 0)),
            pl.BlockSpec(piece.shape, lambda i: (0, 0)),
            pl.BlockSpec(grad_joined.shape, lambda i: (0, 0)),
            pl.BlockSpec(attended_t.shape, lambda i: (0, 0)),
        ],
        out_specs=pl.BlockSpec((block, width), lambda i: (i, 0)),
        out_shape=pltpu.HBM((2 * width, width), LOW),
        compiler_params=pltpu.CompilerParams(vmem_limit_bytes=20 * MIB),
        cost_estimate=SHORT,
        name="heads_weights",
    )(normed, piece, grad_joined, attended_t)


def spread_body(mlp_ref, left_ref, right_ref, down_ref, up_ref, qkv_ref, out_ref):
    step = pl.program_id(0)
    steps = pl.num_programs(0)

    @pl.when(step < steps // 2)
    def _():
        down_ref[...] = mlp_ref[...].astype(WIDE).reshape(down_ref.shape)

    @pl.when(step >= steps // 2)
    def _():
        up_ref[...] = mlp_ref[...].astype(WIDE).reshape(up_ref.shape)

    lines, columns = qkv_ref.shape
    width = left_ref.shape[-1]
    qkv_ref[:, 0:width] = left_ref[...].astype(WIDE).reshape(lines, width)
    right = right_ref[...].astype(WIDE).reshape(lines, width)
    qkv_ref[:, width:columns] = right[:, 0 : columns - width]
    out_ref[...] = jnp.transpose(right[:, columns - width :])


def spread(whole, n, units, columns):
    width = whole.shape[1]
    mlp_rows, heads_rows = 2 * units // n, 2 * width // n
    assert whole.shape[0] == n * (mlp_rows + heads_rows) and mlp_rows % heads_rows == 0
    lines = 256
    steps = width // lines
    block = 2 * units // steps
    inner = 2 * width - columns
    across = width // block
    skip = mlp_rows // heads_rows

    def later(i):
        return jnp.maximum(i - steps // 2, 0)

    by_rows = streamed(whole.reshape(n, -1, width))
    by_parts = streamed(whole.reshape(n, -1, heads_rows, width))
    part = (n // (2 * steps), 1, heads_rows, width)
    return pl.pallas_call(
        spread_body,
        grid=(steps,),
        in_specs=[
            pl.BlockSpec((n // steps, mlp_rows, width), lambda i: (i, 0, 0)),
            pl.BlockSpec(part, lambda i: (i, skip, 0, 0)),
            pl.BlockSpec(part, lambda i: (i + steps, skip, 0, 0)),
        ],
        out_specs=[
            pl.BlockSpec((block, width), lambda i: (jnp.minimum(i, steps // 2 - 1), 0)),
            pl.BlockSpec((block, width), lambda i: (later(i) % across, later(i) // across)),
            pl.BlockSpec((lines, columns), lambda i: (i, 0)),
            pl.BlockSpec((inner, lines), lambda i: (0, i)),
        ],
        out_shape=[
            jax.ShapeDtypeStruct((units, width), WIDE),
            jax.ShapeDtypeStruct((width, units), WIDE),
            jax.ShapeDtypeStruct((width, columns), WIDE),
            jax.ShapeDtypeStruct((inner, width), WIDE),
        ],
        compiler_params=pltpu.CompilerParams(vmem_limit_bytes=32 * MIB),
        cost_estimate=SHORT,
        name="spread",
    )(by_rows, by_parts, by_parts)


def output_body(count, side_ref, w_out_ref, hidden_ref, w_down_ref, *refs):
    attended_refs, (away_ref, kept_ref) = refs[:count], refs[count:]
    step = pl.program_id(0)
    attended = jnp.concatenate([ref[...] for ref in attended_refs], axis=0)
    total = jnp.dot(
        hidden_ref[...], w_down_ref[...], preferred_element_type=WIDE
    ) + first_dims(attended, w_out_ref[...])

    @pl.when(step == 0)
    def _():
        away_ref[...] = total.astype(LOW)

    @pl.when(step == 1)
    def _():
        kept_ref[...] = total


def output_terms(side, w_out, hidden, w_down, attended_t):
    rows, units = hidden.shape
    inner, width = w_out.shape
    half = width // 2

    def column(i, s):
        return (0, s[0] ^ (1 - i))

    def whole(i, s):
        return (0, 0)

    return pl.pallas_call(
        functools.partial(output_body, len(attended_t)),
        grid_spec=pltpu.PrefetchScalarGridSpec(
            num_scalar_prefetch=1,
            grid=(2,),
            in_specs=[
                pl.BlockSpec((inner, half), column),
                pl.BlockSpec((rows, units), whole),
                pl.BlockSpec((units, half), column),
            ]
            + [pl.BlockSpec(v.shape, whole) for v in attended_t],
            out_specs=[pl.BlockSpec((rows, half), whole)] * 2,
        ),
        out_shape=[
            jax.ShapeDtypeStruct((rows, half), LOW),
            jax.ShapeDtypeStruct((rows, half), WIDE),
        ],
        compiler_params=pltpu.CompilerParams(vmem_limit_bytes=24 * MIB),
        cost_estimate=SHORT,
        name="output_terms",
    )(side, w_out, hidden, w_down, *attended_t)


def second_dims(left, right):
    return lax.dot_general(left, right, (((1,), (1,)), ((), ())), preferred_element_type=WIDE)


def grad_in_body(count, side_ref, w_qkv_ref, grad_pre_ref, w_up_ref, *refs):
    away_ref, kept_ref = refs[count:]
    step = pl.program_id(0)
    grad_joined = jnp.concatenate([ref[...] for ref in refs[:count]], axis=1)
    total = second_dims(grad_joined, w_qkv_ref[...]) + second_dims(
        grad_pre_ref[...], w_up_ref[...]
    )

    @pl.when(step == 0)
    def _():
        away_ref[...] = total.astype(LOW)

    @pl.when(step == 1)
    def _():
        kept_ref[...] = total


def grad_in_terms(side, w_qkv, grad_pre, w_up, grad_joined):
    rows, units = grad_pre.shape
    width, columns = w_qkv.shape
    half = width // 2

    def picked(i, s):
        return (s[0] ^ (1 - i), 0)

    def whole(i, s):
        return (0, 0)

    return pl.pallas_call(
        functools.partial(grad_in_body, len(grad_joined)),
        grid_spec=pltpu.PrefetchScalarGridSpec(
            num_scalar_prefetch=1,
            grid=(2,),
            in_specs=[
                pl.BlockSpec((half, columns), picked),
                pl.BlockSpec((rows, units), whole),
                pl.BlockSpec((half, units), picked),
            ]
            + [pl.BlockSpec(v.shape, whole) for v in grad_joined],
            out_specs=[pl.BlockSpec((rows, half), whole)] * 2,
        ),
        out_shape=[
            jax.ShapeDtypeStruct((rows, half), LOW),
            jax.ShapeDtypeStruct((rows, half), WIDE),
        ],
        compiler_params=pltpu.CompilerParams(vmem_limit_bytes=24 * MIB),
        cost_estimate=SHORT,
        name="grad_in_terms",
    )(side, streamed(w_qkv), grad_pre, streamed(w_up), *grad_joined)


def hat_body(side_ref, kept_ref, arrived_ref, tokens_ref, stats_ref, gain_ref,
             hat_ref, sums_ref, gain_grad_ref):
    total = kept_ref[...] + arrived_ref[...].astype(WIDE)
    stats = stats_ref[...]
    x_hat = (tokens_ref[...].astype(WIDE) - stats[:, 0:1]) * stats[:, 1:2]
    grad_hat = total * gain_ref[...]
    hat_ref[...] = grad_hat
    lane = lax.broadcasted_iota(jnp.int32, stats.shape, 1)
    sums_ref[...] = jnp.where(
        lane == 0,
        jnp.sum(grad_hat, axis=1, keepdims=True),
        jnp.sum(grad_hat * x_hat, axis=1, keepdims=True),
    )

    @pl.when(pl.program_id(0) == 0)
    def _():
        gain_grad_ref[...] = jnp.zeros_like(gain_grad_ref)

    gain_grad_ref[...] += jnp.sum(total * x_hat, axis=0, keepdims=True)


def grad_in_hat(side, kept, arrived, tokens, stats, gain):
    rows, half = tokens.shape
    block = 448

    def rows_of(columns):
        return pl.BlockSpec((block, columns), lambda i, s: (i, 0))

    return pl.pallas_call(
        hat_body,
        grid_spec=pltpu.PrefetchScalarGridSpec(
            num_scalar_prefetch=1,
            grid=(rows // block,),
            in_specs=[rows_of(half), rows_of(half), rows_of(half), rows_of(128),
                      pl.BlockSpec((1, half), lambda i, s: (0, s[0]))],
            out_specs=[rows_of(half), rows_of(128), pl.BlockSpec((1, half), lambda i, s: (0, 0))],
        ),
        out_shape=[
            jax.ShapeDtypeStruct((rows, half), WIDE),
            jax.ShapeDtypeStruct((rows, 128), WIDE),
            jax.ShapeDtypeStruct((1, half), WIDE),
        ],
        cost_estimate=SHORT,
        name="grad_in_hat",
    )(side, kept, arrived, tokens, stats, gain)


def finish_body(cotangent_ref, tokens_ref, stats_ref, hat_ref, sums_ref, other_ref, out_ref):
    width = 2 * tokens_ref.shape[1]
    scaled = stats_ref[:, 1:2]
    x_hat = (tokens_ref[...].astype(WIDE) - stats_ref[:, 0:1]) * scaled
    sums = (sums_ref[:, 0:2] + other_ref[...]) / width
    out_ref[...] = (
        cotangent_ref[...].astype(WIDE)
        + scaled * (hat_ref[...] - sums[:, 0:1] - x_hat * sums[:, 1:2])
    ).astype(LOW)


def grad_in_finish(cotangent, tokens, stats, hat, sums, other):
    rows, half = tokens.shape
    block = 224

    def rows_of(columns):
        return pl.BlockSpec((block, columns), lambda i: (i, 0))

    return pl.pallas_call(
        finish_body,
        grid=(rows // block,),
        in_specs=[rows_of(c) for c in (half, half, 128, half, 128, 2)],
        out_specs=rows_of(half),
        out_shape=jax.ShapeDtypeStruct((rows, half), LOW),
        cost_estimate=SHORT,
        name="grad_in_finish",
    )(cotangent, tokens, stats, hat, sums, other)


def part_norm(values):
    center = jnp.mean(values, axis=0, keepdims=True)
    shifted = values - center
    scaled = lax.rsqrt(jnp.mean(shifted * shifted, axis=0, keepdims=True) + EPSILON)
    return shifted * scaled, scaled


def part_norm_back(grad, normal, scaled, gain):
    g = grad * gain
    inner = jnp.mean(g * normal, axis=0, keepdims=True)
    return scaled * (g - jnp.mean(g, axis=0, keepdims=True) - normal * inner)


def lane_fold(values):
    total = values[:, 0:128]
    for start in range(128, values.shape[1], 128):
        total = total + values[:, start : start + 128]
    return total


def attention_body(rows, tiles, count, *refs):
    joined_refs, grad_refs = refs[:count], refs[count : 2 * count]
    (gain_ref, query_mark_ref, key_mark_ref, attended_ref, grad_joined_ref, gain_grad_ref,
     key_grad, value_grad) = refs[2 * count :]

    def part(some, r0, r1):
        return jnp.concatenate([ref[r0:r1, :] for ref in some], axis=1)

    factor = float(HD) ** (-0.5)
    gain_query = gain_ref[0:HD, :]
    gain_key = gain_ref[HD : 2 * HD, :]
    pieces = []
    gain_sum_query = jnp.zeros((HD, 128), WIDE)
    gain_sum_key = jnp.zeros((HD, 128), WIDE)
    one_mark = jnp.where(lax.broadcasted_iota(jnp.int32, (HD, rows), 0) < 2, 1.0, 0.0).astype(LOW)
    for head in range(2):
        base = head * 3 * HD
        query_hat, query_scale = part_norm(part(joined_refs, base, base + HD))
        key_hat, key_scale = part_norm(part(joined_refs, base + HD, base + 2 * HD))
        value_t = part(joined_refs, base + 2 * HD, base + 3 * HD).astype(LOW)
        query_t = (query_hat * gain_query).astype(LOW)
        key_t = (key_hat * gain_key).astype(LOW)
        grad_t = part(grad_refs, head * HD, (head + 1) * HD)
        query_aug = jnp.concatenate([query_t * factor, query_mark_ref[...]], axis=0)
        key_aug = jnp.transpose(jnp.concatenate([key_t, key_mark_ref[...]], axis=0))
        value_aug_t = jnp.concatenate([value_t, one_mark], axis=0)
        value_aug = jnp.transpose(value_aug_t)
        query_grads = []
        for number, (q0, q1, k0, k1) in enumerate(tiles):
            scores = jnp.dot(key_aug[k0:k1], query_aug[:, q0:q1], preferred_element_type=WIDE)
            terms = jnp.exp(scores)
            terms_low = terms.astype(LOW)
            summed = jnp.dot(value_aug_t[:, k0:k1], terms_low, preferred_element_type=WIDE)
            inverse = 1.0 / summed[HD : HD + 1, :]
            attended = summed[0:HD, :] * inverse
            attended_ref[head * HD : (head + 1) * HD, q0:q1] = attended.astype(LOW)
            grad_tile = grad_t[:, q0:q1].astype(WIDE)
            row_inner = jnp.sum(grad_tile * attended, axis=0, keepdims=True)
            inner_high = row_inner.astype(LOW)
            inner_low = (row_inner - inner_high.astype(WIDE)).astype(LOW)
            place = lax.broadcasted_iota(jnp.int32, (HD, q1 - q0), 0)
            inner_mark = jnp.where(
                place == 0,
                -inner_high.astype(WIDE),
                jnp.where(place == 1, -inner_low.astype(WIDE), 0.0),
            ).astype(LOW)
            grad_aug = jnp.concatenate([grad_t[:, q0:q1], inner_mark], axis=0)
            shifted = jnp.dot(value_aug[k0:k1], grad_aug, preferred_element_type=WIDE)
            grad_scores = (terms * shifted).astype(LOW)
            query_grads.append(
                jnp.dot(key_t[:, k0:k1], grad_scores, preferred_element_type=WIDE)
                * (inverse * factor)
            )
            query_rows = jnp.transpose(
                jnp.concatenate(
                    [query_t[:, q0:q1].astype(WIDE) * (inverse * factor), grad_tile * inverse],
                    axis=0,
                ).astype(LOW)
            )
            key_term = jnp.dot(grad_scores, query_rows, preferred_element_type=WIDE)
            value_term = jnp.dot(terms_low, query_rows, preferred_element_type=WIDE)
            if number == 0:
                key_grad[k0:k1, :] = key_term
                value_grad[k0:k1, :] = value_term
                key_grad[k1:rows, :] = jnp.zeros((rows - k1, 2 * HD), WIDE)
                value_grad[k1:rows, :] = jnp.zeros((rows - k1, 2 * HD), WIDE)
            else:
                key_grad[k0:k1, :] += key_term
                value_grad[k0:k1, :] += value_term
        lane = lax.broadcasted_iota(jnp.int32, (rows, 2 * HD), 1)
        joint = jnp.transpose(jnp.where(lane < HD, key_grad[...], value_grad[...]))
        query_grad = jnp.concatenate(query_grads, axis=1)
        key_grad_t = joint[0:HD, :]
        gain_sum_query += lane_fold(query_grad * query_hat)
        gain_sum_key += lane_fold(key_grad_t * key_hat)
        pieces += [
            part_norm_back(query_grad, query_hat, query_scale, gain_query),
            part_norm_back(key_grad_t, key_hat, key_scale, gain_key),
            joint[HD : 2 * HD, :],
        ]
    grad_joined_ref[...] = jnp.transpose(jnp.concatenate(pieces, axis=0)).astype(LOW)

    @pl.when(pl.program_id(0) == 0)
    def _():
        gain_grad_ref[...] = jnp.zeros_like(gain_grad_ref)

    gain_grad_ref[...] += jnp.concatenate([gain_sum_query, gain_sum_key], axis=0)


def attention(joined_t, grad_t, gains, query_mark, key_mark, skip, pairs):
    rows = query_mark.shape[1]
    heads = 2 * pairs
    width = heads * 3 * HD
    far = 3 * (rows // 4)
    tiles = ((0, 512, 0, far), (512, 768, 0, rows), (768, rows, far, rows))

    def whole(i):
        return (0, 0)

    return pl.pallas_call(
        functools.partial(attention_body, rows, tiles, len(joined_t)),
        grid=(heads // 2,),
        in_specs=[pl.BlockSpec((6 * HD, v.shape[1]), lambda i: (i + skip, 0)) for v in joined_t]
        + [pl.BlockSpec((2 * HD, v.shape[1]), lambda i: (i + skip, 0)) for v in grad_t]
        + [
            pl.BlockSpec((2 * HD, 1), whole),
            pl.BlockSpec((HD, rows), whole),
            pl.BlockSpec((HD, rows), whole),
        ],
        out_specs=[
            pl.BlockSpec((2 * HD, rows), lambda i: (i, 0)),
            pl.BlockSpec((rows, 6 * HD), lambda i: (0, i)),
            pl.BlockSpec((2 * HD, 128), whole),
        ],
        out_shape=[
            jax.ShapeDtypeStruct((heads * HD, rows), LOW),
            jax.ShapeDtypeStruct((rows, width), LOW),
            jax.ShapeDtypeStruct((2 * HD, 128), WIDE),
        ],
        scratch_shapes=[
            pltpu.VMEM((rows, 2 * HD), WIDE),
            pltpu.VMEM((rows, 2 * HD), WIDE),
        ],
        compiler_params=pltpu.CompilerParams(vmem_limit_bytes=20 * MIB),
        cost_estimate=SHORT,
        name="attention_both",
    )(*joined_t, *grad_t, gains, query_mark, key_mark)


def ring_order(n):
    if n % 4:
        return list(range(n))
    up = [z * 4 + c for z in range(n // 4) for c in range(2)]
    down = [z * 4 + 2 + c for z in reversed(range(n // 4)) for c in range(2)]
    return up + down


def ring_scatter(values, n):
    return lax.psum_scatter(
        values, "batch", scatter_dimension=0, tiled=True, axis_index_groups=[ring_order(n)]
    )


def chips_scatter(values, n):
    order = ring_order(n)
    groups = [order[0::2], order[1::2]]
    return lax.psum_scatter(
        values, "batch", scatter_dimension=0, tiled=True, axis_index_groups=groups
    )


def ring_gather(own, n):
    return lax.all_gather(own, "batch", axis=0, tiled=True, axis_index_groups=[ring_order(n)])


def send(values, pairs):
    return lax.ppermute(values, "batch", pairs)


def exchange(values, bit, n):
    return send(values, [(i, i ^ bit) for i in range(n)])


def added(left, right):
    return (left.astype(WIDE) + right.astype(WIDE)).astype(LOW)


def then(done, *values):
    return lax.optimization_barrier((done, values))[1]


def ring_view(values, n):
    bits = max(n.bit_length() - 3, 0)
    return values.reshape((2,) + (2,) * bits + (2, values.shape[0] // n, values.shape[1]))


def ring_half(bit, place, n):
    dims = n.bit_length()
    mine = (place // bit) % 2
    if bit == 1:
        return dims - 2, mine
    if bit == 2:
        return 0, mine
    return dims - 1 - bit.bit_length() + 1, mine ^ ((place // 2) % 2)


def pair_send(values, bit, place, n):
    dim, mine = ring_half(bit, place, n)
    return exchange(lax.dynamic_slice_in_dim(values, 1 - mine, 1, dim), bit, n)


def pair_add(values, arrived, bit, place, n):
    dim, mine = ring_half(bit, place, n)
    return added(lax.dynamic_slice_in_dim(values, mine, 1, dim), arrived)


def pair_join(mine, other, bit, place, n):
    dim, half = ring_half(bit, place, n)
    return both_halves(mine, other, half == 0, dim)


def line_place(place, n):
    count = n // 4
    up = place // 4
    return jnp.where((place // 2) % 2 == 0, up, count - 1 - up), count


def line_send(values, place, n):
    mine, count = line_place(place, n)
    blocks = values.reshape(count, values.size // count // values.shape[-1], values.shape[-1])
    return blocks, [
        exchange(lax.dynamic_index_in_dim(blocks, mine ^ k, 0, False), 4 * k, n)
        for k in range(1, count)
    ]


def line_add(blocks, arrived, place, n):
    mine, _ = line_place(place, n)
    total = lax.dynamic_index_in_dim(blocks, mine, 0, False).astype(WIDE)
    for values in arrived:
        total = total + values.astype(WIDE)
    return total.astype(LOW)


def small_sums(values, n, afters):
    bit = 1
    while bit < n:
        bits = (bit, 2 * bit, 3 * bit) if bit * 4 <= n else (bit,)
        moved = [exchange(values, b, n) for b in bits]
        if afters:
            moved = then(afters.pop(0), *moved)
        values = values + moved[0]
        if len(bits) == 3:
            values = values + (moved[1] + moved[2])
        bit *= 4
    return values


def on_device(n_batch, tokens, ln_gain, w_qkv, qk_gain, w_out, w_up, b_up, w_down, b_out,
              cotangent, slot_image, token_valid):
    rows, half = tokens.shape
    width = 2 * half
    slots = slot_image.shape[0]
    slot_rows = rows // slots
    side = lax.axis_index("head")
    first = side == 0
    place = lax.axis_index("batch")
    sides = jnp.reshape(side, (1,)).astype(jnp.int32)
    bits = []
    while 4 * 2 ** len(bits) < n_batch:
        bits.append(4 * 2 ** len(bits))

    other_tokens = swap(tokens, "head")
    (held,) = then(tokens, cotangent)
    other_cotangent = swap(held, "head")

    token_image = jnp.repeat(slot_image, slot_rows, total_repeat_length=rows)
    ids = lax.broadcasted_iota(jnp.int32, (HD, rows), 0)
    same = token_image[None, :] == ids
    query_mark = jnp.where(same, 1.0, 0.0).astype(LOW)
    key_mark = jnp.where(same & (token_valid == 1)[None, :], 0.0, FAR)
    key_mark = jnp.where(ids < slots, key_mark, 0.0).astype(LOW)
    gains = qk_gain.reshape(-1, 1)
    grad_b_out = jnp.sum(cotangent.astype(WIDE), axis=0)
    (query_mark, key_mark, gains, grad_b_out), other_tokens = lax.optimization_barrier(
        ((query_mark, key_mark, gains, grad_b_out), other_tokens)
    )

    normed, stats = input_norm(sides, tokens, other_tokens, ln_gain)
    hidden, slope = mlp_forward(normed, w_up, b_up)
    grad_pre, grad_b_up, piece = mlp_slope(sides, cotangent, other_cotangent, w_down, slope)
    mlp_part = mlp_weights(hidden, piece, normed, grad_pre)
    mlp_own = ring_scatter(mlp_part, n_batch)

    def sent(part, bit):
        return pair_send(part, bit, place, n_batch)

    def summed(after, part, arrived, bit):
        (arrived,) = then(after, arrived)
        return pair_add(part, arrived, bit, place, n_batch)

    part, some = then(mlp_part, piece, normed)
    joined_t = contract(w_qkv, some, 0, 1)
    grad_t = contract(w_out, part, 1, 1).astype(LOW)
    marks = (gains, query_mark, key_mark)
    pairs = w_out.shape[0] // (2 * HD)
    joined_t, grad_t = then((joined_t, grad_t), joined_t, grad_t)
    attended, grad_joined, gain_grad = attention([joined_t], [grad_t], *marks, 0, pairs)
    heads_part = heads_weights(normed, grad_joined, piece, attended)
    heads_part = ring_view(heads_part, n_batch)
    branch = (sides, w_out, hidden, w_down, [attended])
    back = (sides, w_qkv, grad_pre, w_up, [grad_joined])
    way = sent(heads_part, 1)
    heads_part = summed(heads_part, heads_part, way, 1)
    mlp_own, heads_part = then(heads_part, mlp_own, heads_part)
    heads_own = chips_scatter(heads_part.reshape(-1, width), n_batch)
    mlp_rows = mlp_own.shape[0]
    away_in, kept_in = grad_in_terms(*then(mlp_own, *back))
    arrived_in = swap(away_in, "head")
    (mlp_own,) = then(away_in, mlp_own)
    own = lax.dynamic_update_slice(
        jnp.zeros((mlp_rows + 2 * width // n_batch, width), LOW), mlp_own, (0, 0)
    )
    away_out, kept_out = output_terms(*then(away_in, *branch))
    arrived_out = swap(away_out, "head")
    own, heads_own = then((away_out, arrived_in), own, heads_own)
    own = lax.dynamic_update_slice(own, heads_own, (mlp_rows, 0))
    whole = ring_gather(own, n_batch)

    (arrived_in,) = then(own, arrived_in)
    hat, sums, grad_ln = grad_in_hat(
        sides, kept_in, arrived_in, tokens, stats, ln_gain.reshape(1, width)
    )
    gain_grad = jnp.sum(gain_grad, axis=1).reshape(2, HD)
    joint = jnp.concatenate([sums[:, 0:2].T, gain_grad], axis=1)
    joint_other = swap(joint, "head")
    (joint_other,) = then(hat, joint_other)
    sums_other = joint_other[:, 0:rows].T
    gain_grad = (gain_grad + joint_other[:, rows:]).reshape(-1)
    small = jnp.concatenate([grad_ln[0], grad_b_out, grad_b_up[0], gain_grad])
    grad_tokens = grad_in_finish(cotangent, tokens, stats, hat, sums, sums_other)
    (arrived_out,) = then(grad_tokens, arrived_out)
    output = (
        tokens.astype(WIDE) + (kept_out + arrived_out.astype(WIDE)) + b_out
    ).astype(LOW)
    small = small_sums(small, n_batch, [grad_tokens, output])
    units = b_up.shape[0]
    (whole,) = then((output, grad_tokens, small), whole)
    grad_wd, grad_wup, grad_wqkv, grad_wo = spread(whole, n_batch, units, w_qkv.shape[1])
    return (
        output,
        grad_tokens,
        small[0:half],
        grad_wqkv,
        small[2 * half + units :].reshape(qk_gain.shape),
        grad_wo,
        grad_wup,
        small[2 * half : 2 * half + units],
        grad_wd,
        small[half : 2 * half],
    )


def solution(mesh):
    placed = (
        P("batch", "head"),
        P(),
        P(None, "head"),
        P(),
        P("head", None),
        P(None, "head"),
        P("head"),
        P("head", None),
        P("head"),
        P("batch", "head"),
        P("batch"),
        P("batch"),
    )
    return jax.shard_map(
        functools.partial(on_device, mesh.shape["batch"]),
        mesh=mesh,
        in_specs=placed,
        out_specs=(
            P("batch", "head"),
            P("batch", "head"),
            P("head"),
            P(None, "head"),
            P(),
            P("head", None),
            P(None, "head"),
            P("head"),
            P("head", None),
            P("head"),
        ),
        check_vma=False,
    )
```

```python
import functools

import jax
import jax.numpy as jnp
from jax import lax
from jax.experimental import pallas as pl
from jax.experimental.pallas import tpu as pltpu
from jax.sharding import PartitionSpec as P

HD = 64
EPSILON = 1e-06
FAR = -16384.0
LOW = jnp.bfloat16
WIDE = jnp.float32
MIB = 1024 * 1024
SHORT = pl.CostEstimate(flops=1024, bytes_accessed=1024, transcendentals=0)


def contract(left, right, left_dim, right_dim):
    return lax.dot_general(
        left, right, (((left_dim,), (right_dim,)), ((), ())), preferred_element_type=WIDE
    )


def swap(values, axis):
    return lax.ppermute(values, axis, [(0, 1), (1, 0)])


def both_halves(mine, other, first, dim):
    return jnp.where(
        first,
        jnp.concatenate([mine, other], axis=dim),
        jnp.concatenate([other, mine], axis=dim),
    )


def mlp_body(normed_ref, w_ref, b_ref, hidden_ref, slope_ref):
    pre = jnp.dot(normed_ref[...], w_ref[...], preferred_element_type=WIDE) + b_ref[...]
    cdf = 0.5 * (1.0 + lax.erf(pre * (0.5**0.5)))
    density = jnp.exp(-0.5 * pre * pre) * 0.3989422804014327
    hidden_ref[...] = (pre * cdf).astype(LOW)
    slope_ref[...] = (cdf + pre * density).astype(LOW)


def streamed(values):
    return pltpu.with_memory_space_constraint(values, pltpu.HBM)


def mlp_forward(normed, w_up, b_up):
    rows, width = normed.shape
    units = w_up.shape[1]
    block = 512
    return pl.pallas_call(
        mlp_body,
        grid=(units // block,),
        in_specs=[
            pl.BlockSpec((rows, width), lambda i: (0, 0)),
            pl.BlockSpec((width, block), lambda i: (0, i)),
            pl.BlockSpec((1, block), lambda i: (0, i)),
        ],
        out_specs=[
            pl.BlockSpec((rows, block), lambda i: (0, i)),
            pl.BlockSpec((rows, block), lambda i: (0, i)),
        ],
        out_shape=[
            jax.ShapeDtypeStruct((rows, units), LOW),
            jax.ShapeDtypeStruct((rows, units), LOW),
        ],
        compiler_params=pltpu.CompilerParams(vmem_limit_bytes=16 * MIB),
        cost_estimate=SHORT,
        name="mlp_forward",
    )(normed, streamed(w_up), b_up.reshape(1, units))


def norm_body(side_ref, mine_ref, other_ref, gain_ref, normed_ref, stats_ref):
    mine = mine_ref[...].astype(WIDE)
    other = other_ref[...].astype(WIDE)
    width = 2 * mine.shape[1]
    half = mine.shape[1]
    center = (
        jnp.sum(mine, axis=1, keepdims=True) + jnp.sum(other, axis=1, keepdims=True)
    ) / width
    mine = mine - center
    other = other - center
    spread = (
        jnp.sum(mine * mine, axis=1, keepdims=True)
        + jnp.sum(other * other, axis=1, keepdims=True)
    ) / width
    scaled = lax.rsqrt(spread + EPSILON)
    first = side_ref[0] == 0
    left = jnp.where(first, mine, other)
    right = jnp.where(first, other, mine)
    normed_ref[:, 0:half] = (left * scaled * gain_ref[:, 0:half]).astype(LOW)
    normed_ref[:, half:width] = (right * scaled * gain_ref[:, half:width]).astype(LOW)
    lane = lax.broadcasted_iota(jnp.int32, stats_ref.shape, 1)
    stats_ref[...] = jnp.where(lane == 0, center, scaled)


def input_norm(side, mine, other, gain):
    rows, half = mine.shape
    block = 224
    return pl.pallas_call(
        norm_body,
        grid_spec=pltpu.PrefetchScalarGridSpec(
            num_scalar_prefetch=1,
            grid=(rows // block,),
            in_specs=[
                pl.BlockSpec((block, half), lambda i, s: (i, 0)),
                pl.BlockSpec((block, half), lambda i, s: (i, 0)),
                pl.BlockSpec((1, 2 * half), lambda i, s: (0, 0)),
            ],
            out_specs=[
                pl.BlockSpec((block, 2 * half), lambda i, s: (i, 0)),
                pl.BlockSpec((block, 128), lambda i, s: (i, 0)),
            ],
        ),
        out_shape=[
            jax.ShapeDtypeStruct((rows, 2 * half), LOW),
            jax.ShapeDtypeStruct((rows, 128), WIDE),
        ],
        cost_estimate=SHORT,
        name="input_norm",
    )(side, mine, other, gain.reshape(1, 2 * half))


def slope_body(side_ref, mine_ref, other_ref, w_ref, slope_ref, grad_pre_ref, bias_ref, piece_ref,
               later_grad_ref, later_piece_ref):
    half = mine_ref.shape[1]
    lines = later_piece_ref.shape[0]

    @pl.when(pl.program_id(0) == 0)
    def _():
        first = side_ref[0] == 0
        mine, other = mine_ref[...], other_ref[...]
        piece_ref[:, 0:half] = jnp.where(first, mine, other)
        piece_ref[:, half:] = jnp.where(first, other, mine)

    back = lax.dot_general(
        piece_ref[...], w_ref[...], (((1,), (1,)), ((), ())), preferred_element_type=WIDE
    )
    low = (back * slope_ref[...].astype(WIDE)).astype(LOW)
    grad_pre_ref[...] = low
    later_grad_ref[...] = low
    bias_ref[...] = jnp.sum(low.astype(WIDE), axis=0, keepdims=True)
    start = pl.multiple_of(pl.program_id(0) * lines, lines)
    later_piece_ref[...] = piece_ref[pl.ds(start, lines), :]


def mlp_slope(side, mine, other, w_down, slope):
    rows, half = mine.shape
    units, width = w_down.shape
    block = 512
    lines = rows * block // units

    def whole(i, s):
        return (0, 0)

    return pl.pallas_call(
        slope_body,
        grid_spec=pltpu.PrefetchScalarGridSpec(
            num_scalar_prefetch=1,
            grid=(units // block,),
            in_specs=[
                pl.BlockSpec((rows, half), whole),
                pl.BlockSpec((rows, half), whole),
                pl.BlockSpec((block, width), lambda i, s: (i, 0)),
                pl.BlockSpec((rows, block), lambda i, s: (0, i)),
            ],
            out_specs=[
                pl.BlockSpec((rows, block), lambda i, s: (0, i)),
                pl.BlockSpec((1, block), lambda i, s: (0, i)),
                pl.BlockSpec((rows, width), whole),
                pl.BlockSpec((rows, block), lambda i, s: (0, i)),
                pl.BlockSpec((lines, width), lambda i, s: (i, 0)),
            ],
        ),
        out_shape=[
            jax.ShapeDtypeStruct((rows, units), LOW),
            jax.ShapeDtypeStruct((1, units), WIDE),
            jax.ShapeDtypeStruct((rows, width), LOW),
            pltpu.HBM((rows, units), LOW),
            pltpu.HBM((rows, width), LOW),
        ],
        compiler_params=pltpu.CompilerParams(vmem_limit_bytes=20 * MIB),
        cost_estimate=SHORT,
        name="mlp_slope",
    )(side, mine, other, streamed(w_down), slope)


def first_dims(left, right):
    return lax.dot_general(left, right, (((0,), (0,)), ((), ())), preferred_element_type=WIDE)


def mlp_weights_body(down_steps, hidden_ref, piece_ref, normed_ref, grad_pre_ref, *refs):
    step = pl.program_id(0)
    out_ref = refs[-1]

    def put(total):
        if len(refs) == 2:
            total = total + refs[0][...].astype(WIDE)
        out_ref[...] = total.astype(LOW)

    @pl.when(step < down_steps)
    def _():
        put(first_dims(hidden_ref[...], piece_ref[...]))

    @pl.when(step >= down_steps)
    def _():
        put(first_dims(normed_ref[...], grad_pre_ref[...]))


def mlp_weights(hidden, piece, normed, grad_pre, *before):
    rows, units = hidden.shape
    width = piece.shape[1]
    block = 512
    down = units // block
    across = width // block
    halves = units // width

    def later(i):
        return jnp.maximum(i - down, 0)

    return pl.pallas_call(
        functools.partial(mlp_weights_body, down),
        grid=(down + halves * across,),
        in_specs=[
            pl.BlockSpec((rows, block), lambda i: (0, jnp.minimum(i, down - 1))),
            pl.BlockSpec((rows, width), lambda i: (0, 0)),
            pl.BlockSpec((rows, block), lambda i: (0, later(i) % across)),
            pl.BlockSpec((rows, width), lambda i: (0, later(i) // across)),
        ]
        + [pl.BlockSpec((block, width), lambda i: (i, 0)) for _ in before],
        out_specs=pl.BlockSpec((block, width), lambda i: (i, 0)),
        out_shape=pltpu.HBM((2 * units, width), LOW),
        input_output_aliases={4: 0} if before else {},
        compiler_params=pltpu.CompilerParams(vmem_limit_bytes=24 * MIB),
        cost_estimate=SHORT,
        name="mlp_weights",
    )(hidden, piece, normed, grad_pre, *before)


def heads_weights_body(steps, normed_ref, piece_ref, grad_joined_ref, attended_ref, out_ref):
    width = out_ref.shape[1]
    rest = grad_joined_ref.shape[1] - width

    block = out_ref.shape[0]
    lines = pl.ds(pl.multiple_of(pl.program_id(0) % steps * block, block), block)

    @pl.when(pl.program_id(0) < steps)
    def _():
        out_ref[...] = first_dims(normed_ref[:, lines], grad_joined_ref[:, 0:width]).astype(LOW)

    @pl.when(pl.program_id(0) >= steps)
    def _():
        out_ref[:, 0:rest] = first_dims(
            normed_ref[:, lines], grad_joined_ref[:, width:]
        ).astype(LOW)
        out_ref[:, rest:] = lax.dot_general(
            piece_ref[:, lines], attended_ref[...], (((0,), (1,)), ((), ())), preferred_element_type=WIDE
        ).astype(LOW)


def heads_weights(normed, grad_joined, piece, attended_t):
    rows, width = normed.shape
    block = 512
    steps = width // block
    return pl.pallas_call(
        functools.partial(heads_weights_body, steps),
        grid=(2 * steps,),
        in_specs=[
            pl.BlockSpec(normed.shape, lambda i: (0, 0)),
            pl.BlockSpec(piece.shape, lambda i: (0, 0)),
            pl.BlockSpec(grad_joined.shape, lambda i: (0, 0)),
            pl.BlockSpec(attended_t.shape, lambda i: (0, 0)),
        ],
        out_specs=pl.BlockSpec((block, width), lambda i: (i, 0)),
        out_shape=pltpu.HBM((2 * width, width), LOW),
        compiler_params=pltpu.CompilerParams(vmem_limit_bytes=20 * MIB),
        cost_estimate=SHORT,
        name="heads_weights",
    )(normed, piece, grad_joined, attended_t)


def spread_body(mlp_ref, left_ref, right_ref, down_ref, up_ref, qkv_ref, out_ref):
    step = pl.program_id(0)
    steps = pl.num_programs(0)

    @pl.when(step < steps // 2)
    def _():
        down_ref[...] = mlp_ref[...].astype(WIDE).reshape(down_ref.shape)

    @pl.when(step >= steps // 2)
    def _():
        up_ref[...] = mlp_ref[...].astype(WIDE).reshape(up_ref.shape)

    lines, columns = qkv_ref.shape
    width = left_ref.shape[-1]
    qkv_ref[:, 0:width] = left_ref[...].astype(WIDE).reshape(lines, width)
    right = right_ref[...].astype(WIDE).reshape(lines, width)
    qkv_ref[:, width:columns] = right[:, 0 : columns - width]
    out_ref[...] = jnp.transpose(right[:, columns - width :])


def spread(whole, n, units, columns):
    width = whole.shape[1]
    mlp_rows, heads_rows = 2 * units // n, 2 * width // n
    assert whole.shape[0] == n * (mlp_rows + heads_rows) and mlp_rows % heads_rows == 0
    lines = 256
    steps = width // lines
    block = 2 * units // steps
    inner = 2 * width - columns
    across = width // block
    skip = mlp_rows // heads_rows

    def later(i):
        return jnp.maximum(i - steps // 2, 0)

    by_rows = streamed(whole.reshape(n, -1, width))
    by_parts = streamed(whole.reshape(n, -1, heads_rows, width))
    part = (n // (2 * steps), 1, heads_rows, width)
    return pl.pallas_call(
        spread_body,
        grid=(steps,),
        in_specs=[
            pl.BlockSpec((n // steps, mlp_rows, width), lambda i: (i, 0, 0)),
            pl.BlockSpec(part, lambda i: (i, skip, 0, 0)),
            pl.BlockSpec(part, lambda i: (i + steps, skip, 0, 0)),
        ],
        out_specs=[
            pl.BlockSpec((block, width), lambda i: (jnp.minimum(i, steps // 2 - 1), 0)),
            pl.BlockSpec((block, width), lambda i: (later(i) % across, later(i) // across)),
            pl.BlockSpec((lines, columns), lambda i: (i, 0)),
            pl.BlockSpec((inner, lines), lambda i: (0, i)),
        ],
        out_shape=[
            jax.ShapeDtypeStruct((units, width), WIDE),
            jax.ShapeDtypeStruct((width, units), WIDE),
            jax.ShapeDtypeStruct((width, columns), WIDE),
            jax.ShapeDtypeStruct((inner, width), WIDE),
        ],
        compiler_params=pltpu.CompilerParams(vmem_limit_bytes=32 * MIB),
        cost_estimate=SHORT,
        name="spread",
    )(by_rows, by_parts, by_parts)


def output_body(count, side_ref, w_out_ref, hidden_ref, w_down_ref, *refs):
    attended_refs, (away_ref, kept_ref) = refs[:count], refs[count:]
    step = pl.program_id(0)
    attended = jnp.concatenate([ref[...] for ref in attended_refs], axis=0)
    total = jnp.dot(
        hidden_ref[...], w_down_ref[...], preferred_element_type=WIDE
    ) + first_dims(attended, w_out_ref[...])

    @pl.when(step == 0)
    def _():
        away_ref[...] = total.astype(LOW)

    @pl.when(step == 1)
    def _():
        kept_ref[...] = total


def output_terms(side, w_out, hidden, w_down, attended_t):
    rows, units = hidden.shape
    inner, width = w_out.shape
    half = width // 2

    def column(i, s):
        return (0, s[0] ^ (1 - i))

    def whole(i, s):
        return (0, 0)

    return pl.pallas_call(
        functools.partial(output_body, len(attended_t)),
        grid_spec=pltpu.PrefetchScalarGridSpec(
            num_scalar_prefetch=1,
            grid=(2,),
            in_specs=[
                pl.BlockSpec((inner, half), column),
                pl.BlockSpec((rows, units), whole),
                pl.BlockSpec((units, half), column),
            ]
            + [pl.BlockSpec(v.shape, whole) for v in attended_t],
            out_specs=[pl.BlockSpec((rows, half), whole)] * 2,
        ),
        out_shape=[
            jax.ShapeDtypeStruct((rows, half), LOW),
            jax.ShapeDtypeStruct((rows, half), WIDE),
        ],
        compiler_params=pltpu.CompilerParams(vmem_limit_bytes=24 * MIB),
        cost_estimate=SHORT,
        name="output_terms",
    )(side, w_out, hidden, w_down, *attended_t)


def second_dims(left, right):
    return lax.dot_general(left, right, (((1,), (1,)), ((), ())), preferred_element_type=WIDE)


def grad_in_body(count, side_ref, w_qkv_ref, grad_pre_ref, w_up_ref, *refs):
    away_ref, kept_ref = refs[count:]
    step = pl.program_id(0)
    grad_joined = jnp.concatenate([ref[...] for ref in refs[:count]], axis=1)
    total = second_dims(grad_joined, w_qkv_ref[...]) + second_dims(
        grad_pre_ref[...], w_up_ref[...]
    )

    @pl.when(step == 0)
    def _():
        away_ref[...] = total.astype(LOW)

    @pl.when(step == 1)
    def _():
        kept_ref[...] = total


def grad_in_terms(side, w_qkv, grad_pre, w_up, grad_joined):
    rows, units = grad_pre.shape
    width, columns = w_qkv.shape
    half = width // 2

    def picked(i, s):
        return (s[0] ^ (1 - i), 0)

    def whole(i, s):
        return (0, 0)

    return pl.pallas_call(
        functools.partial(grad_in_body, len(grad_joined)),
        grid_spec=pltpu.PrefetchScalarGridSpec(
            num_scalar_prefetch=1,
            grid=(2,),
            in_specs=[
                pl.BlockSpec((half, columns), picked),
                pl.BlockSpec((rows, units), whole),
                pl.BlockSpec((half, units), picked),
            ]
            + [pl.BlockSpec(v.shape, whole) for v in grad_joined],
            out_specs=[pl.BlockSpec((rows, half), whole)] * 2,
        ),
        out_shape=[
            jax.ShapeDtypeStruct((rows, half), LOW),
            jax.ShapeDtypeStruct((rows, half), WIDE),
        ],
        compiler_params=pltpu.CompilerParams(vmem_limit_bytes=24 * MIB),
        cost_estimate=SHORT,
        name="grad_in_terms",
    )(side, streamed(w_qkv), grad_pre, streamed(w_up), *grad_joined)


def hat_body(side_ref, kept_ref, arrived_ref, tokens_ref, stats_ref, gain_ref,
             hat_ref, sums_ref, gain_grad_ref):
    total = kept_ref[...] + arrived_ref[...].astype(WIDE)
    stats = stats_ref[...]
    x_hat = (tokens_ref[...].astype(WIDE) - stats[:, 0:1]) * stats[:, 1:2]
    grad_hat = total * gain_ref[...]
    hat_ref[...] = grad_hat
    lane = lax.broadcasted_iota(jnp.int32, stats.shape, 1)
    sums_ref[...] = jnp.where(
        lane == 0,
        jnp.sum(grad_hat, axis=1, keepdims=True),
        jnp.sum(grad_hat * x_hat, axis=1, keepdims=True),
    )

    @pl.when(pl.program_id(0) == 0)
    def _():
        gain_grad_ref[...] = jnp.zeros_like(gain_grad_ref)

    gain_grad_ref[...] += jnp.sum(total * x_hat, axis=0, keepdims=True)


def grad_in_hat(side, kept, arrived, tokens, stats, gain):
    rows, half = tokens.shape
    block = 448

    def rows_of(columns):
        return pl.BlockSpec((block, columns), lambda i, s: (i, 0))

    return pl.pallas_call(
        hat_body,
        grid_spec=pltpu.PrefetchScalarGridSpec(
            num_scalar_prefetch=1,
            grid=(rows // block,),
            in_specs=[rows_of(half), rows_of(half), rows_of(half), rows_of(128),
                      pl.BlockSpec((1, half), lambda i, s: (0, s[0]))],
            out_specs=[rows_of(half), rows_of(128), pl.BlockSpec((1, half), lambda i, s: (0, 0))],
        ),
        out_shape=[
            jax.ShapeDtypeStruct((rows, half), WIDE),
            jax.ShapeDtypeStruct((rows, 128), WIDE),
            jax.ShapeDtypeStruct((1, half), WIDE),
        ],
        cost_estimate=SHORT,
        name="grad_in_hat",
    )(side, kept, arrived, tokens, stats, gain)


def finish_body(cotangent_ref, tokens_ref, stats_ref, hat_ref, sums_ref, other_ref, out_ref):
    width = 2 * tokens_ref.shape[1]
    scaled = stats_ref[:, 1:2]
    x_hat = (tokens_ref[...].astype(WIDE) - stats_ref[:, 0:1]) * scaled
    sums = (sums_ref[:, 0:2] + other_ref[...]) / width
    out_ref[...] = (
        cotangent_ref[...].astype(WIDE)
        + scaled * (hat_ref[...] - sums[:, 0:1] - x_hat * sums[:, 1:2])
    ).astype(LOW)


def grad_in_finish(cotangent, tokens, stats, hat, sums, other):
    rows, half = tokens.shape
    block = 224

    def rows_of(columns):
        return pl.BlockSpec((block, columns), lambda i: (i, 0))

    return pl.pallas_call(
        finish_body,
        grid=(rows // block,),
        in_specs=[rows_of(c) for c in (half, half, 128, half, 128, 2)],
        out_specs=rows_of(half),
        out_shape=jax.ShapeDtypeStruct((rows, half), LOW),
        cost_estimate=SHORT,
        name="grad_in_finish",
    )(cotangent, tokens, stats, hat, sums, other)


def part_norm(values):
    center = jnp.mean(values, axis=0, keepdims=True)
    shifted = values - center
    scaled = lax.rsqrt(jnp.mean(shifted * shifted, axis=0, keepdims=True) + EPSILON)
    return shifted * scaled, scaled


def part_norm_back(grad, normal, scaled, gain):
    g = grad * gain
    inner = jnp.mean(g * normal, axis=0, keepdims=True)
    return scaled * (g - jnp.mean(g, axis=0, keepdims=True) - normal * inner)


def lane_fold(values):
    total = values[:, 0:128]
    for start in range(128, values.shape[1], 128):
        total = total + values[:, start : start + 128]
    return total


def attention_body(rows, tiles, count, *refs):
    joined_refs, grad_refs = refs[:count], refs[count : 2 * count]
    (gain_ref, query_mark_ref, key_mark_ref, attended_ref, grad_joined_ref, gain_grad_ref,
     key_grad, value_grad) = refs[2 * count :]

    def part(some, r0, r1):
        return jnp.concatenate([ref[r0:r1, :] for ref in some], axis=1)

    factor = float(HD) ** (-0.5)
    gain_query = gain_ref[0:HD, :]
    gain_key = gain_ref[HD : 2 * HD, :]
    pieces = []
    gain_sum_query = jnp.zeros((HD, 128), WIDE)
    gain_sum_key = jnp.zeros((HD, 128), WIDE)
    one_mark = jnp.where(lax.broadcasted_iota(jnp.int32, (HD, rows), 0) < 2, 1.0, 0.0).astype(LOW)
    for head in range(2):
        base = head * 3 * HD
        query_hat, query_scale = part_norm(part(joined_refs, base, base + HD))
        key_hat, key_scale = part_norm(part(joined_refs, base + HD, base + 2 * HD))
        value_t = part(joined_refs, base + 2 * HD, base + 3 * HD).astype(LOW)
        query_t = (query_hat * gain_query).astype(LOW)
        key_t = (key_hat * gain_key).astype(LOW)
        grad_t = part(grad_refs, head * HD, (head + 1) * HD)
        query_aug = jnp.concatenate([query_t * factor, query_mark_ref[...]], axis=0)
        key_aug = jnp.transpose(jnp.concatenate([key_t, key_mark_ref[...]], axis=0))
        value_aug_t = jnp.concatenate([value_t, one_mark], axis=0)
        value_aug = jnp.transpose(value_aug_t)
        query_grads = []
        for number, (q0, q1, k0, k1) in enumerate(tiles):
            scores = jnp.dot(key_aug[k0:k1], query_aug[:, q0:q1], preferred_element_type=WIDE)
            terms = jnp.exp(scores)
            terms_low = terms.astype(LOW)
            summed = jnp.dot(value_aug_t[:, k0:k1], terms_low, preferred_element_type=WIDE)
            inverse = 1.0 / summed[HD : HD + 1, :]
            attended = summed[0:HD, :] * inverse
            attended_ref[head * HD : (head + 1) * HD, q0:q1] = attended.astype(LOW)
            grad_tile = grad_t[:, q0:q1].astype(WIDE)
            row_inner = jnp.sum(grad_tile * attended, axis=0, keepdims=True)
            inner_high = row_inner.astype(LOW)
            inner_low = (row_inner - inner_high.astype(WIDE)).astype(LOW)
            place = lax.broadcasted_iota(jnp.int32, (HD, q1 - q0), 0)
            inner_mark = jnp.where(
                place == 0,
                -inner_high.astype(WIDE),
                jnp.where(place == 1, -inner_low.astype(WIDE), 0.0),
            ).astype(LOW)
            grad_aug = jnp.concatenate([grad_t[:, q0:q1], inner_mark], axis=0)
            shifted = jnp.dot(value_aug[k0:k1], grad_aug, preferred_element_type=WIDE)
            grad_scores = (terms * shifted).astype(LOW)
            query_grads.append(
                jnp.dot(key_t[:, k0:k1], grad_scores, preferred_element_type=WIDE)
                * (inverse * factor)
            )
            query_rows = jnp.transpose(
                jnp.concatenate(
                    [query_t[:, q0:q1].astype(WIDE) * (inverse * factor), grad_tile * inverse],
                    axis=0,
                ).astype(LOW)
            )
            key_term = jnp.dot(grad_scores, query_rows, preferred_element_type=WIDE)
            value_term = jnp.dot(terms_low, query_rows, preferred_element_type=WIDE)
            if number == 0:
                key_grad[k0:k1, :] = key_term
                value_grad[k0:k1, :] = value_term
                key_grad[k1:rows, :] = jnp.zeros((rows - k1, 2 * HD), WIDE)
                value_grad[k1:rows, :] = jnp.zeros((rows - k1, 2 * HD), WIDE)
            else:
                key_grad[k0:k1, :] += key_term
                value_grad[k0:k1, :] += value_term
        lane = lax.broadcasted_iota(jnp.int32, (rows, 2 * HD), 1)
        joint = jnp.transpose(jnp.where(lane < HD, key_grad[...], value_grad[...]))
        query_grad = jnp.concatenate(query_grads, axis=1)
        key_grad_t = joint[0:HD, :]
        gain_sum_query += lane_fold(query_grad * query_hat)
        gain_sum_key += lane_fold(key_grad_t * key_hat)
        pieces += [
            part_norm_back(query_grad, query_hat, query_scale, gain_query),
            part_norm_back(key_grad_t, key_hat, key_scale, gain_key),
            joint[HD : 2 * HD, :],
        ]
    grad_joined_ref[...] = jnp.transpose(jnp.concatenate(pieces, axis=0)).astype(LOW)

    @pl.when(pl.program_id(0) == 0)
    def _():
        gain_grad_ref[...] = jnp.zeros_like(gain_grad_ref)

    gain_grad_ref[...] += jnp.concatenate([gain_sum_query, gain_sum_key], axis=0)


def attention(joined_t, grad_t, gains, query_mark, key_mark, skip, pairs):
    rows = query_mark.shape[1]
    heads = 2 * pairs
    width = heads * 3 * HD
    far = 3 * (rows // 4)
    tiles = ((0, 512, 0, far), (512, 768, 0, rows), (768, rows, far, rows))

    def whole(i):
        return (0, 0)

    return pl.pallas_call(
        functools.partial(attention_body, rows, tiles, len(joined_t)),
        grid=(heads // 2,),
        in_specs=[pl.BlockSpec((6 * HD, v.shape[1]), lambda i: (i + skip, 0)) for v in joined_t]
        + [pl.BlockSpec((2 * HD, v.shape[1]), lambda i: (i + skip, 0)) for v in grad_t]
        + [
            pl.BlockSpec((2 * HD, 1), whole),
            pl.BlockSpec((HD, rows), whole),
            pl.BlockSpec((HD, rows), whole),
        ],
        out_specs=[
            pl.BlockSpec((2 * HD, rows), lambda i: (i, 0)),
            pl.BlockSpec((rows, 6 * HD), lambda i: (0, i)),
            pl.BlockSpec((2 * HD, 128), whole),
        ],
        out_shape=[
            jax.ShapeDtypeStruct((heads * HD, rows), LOW),
            jax.ShapeDtypeStruct((rows, width), LOW),
            jax.ShapeDtypeStruct((2 * HD, 128), WIDE),
        ],
        scratch_shapes=[
            pltpu.VMEM((rows, 2 * HD), WIDE),
            pltpu.VMEM((rows, 2 * HD), WIDE),
        ],
        compiler_params=pltpu.CompilerParams(vmem_limit_bytes=20 * MIB),
        cost_estimate=SHORT,
        name="attention_both",
    )(*joined_t, *grad_t, gains, query_mark, key_mark)


def ring_order(n):
    if n % 4:
        return list(range(n))
    up = [z * 4 + c for z in range(n // 4) for c in range(2)]
    down = [z * 4 + 2 + c for z in reversed(range(n // 4)) for c in range(2)]
    return up + down


def ring_scatter(values, n):
    return lax.psum_scatter(
        values, "batch", scatter_dimension=0, tiled=True, axis_index_groups=[ring_order(n)]
    )


def chips_scatter(values, n):
    order = ring_order(n)
    groups = [order[0::2], order[1::2]]
    return lax.psum_scatter(
        values, "batch", scatter_dimension=0, tiled=True, axis_index_groups=groups
    )


def ring_gather(own, n):
    return lax.all_gather(own, "batch", axis=0, tiled=True, axis_index_groups=[ring_order(n)])


def send(values, pairs):
    return lax.ppermute(values, "batch", pairs)


def exchange(values, bit, n):
    return send(values, [(i, i ^ bit) for i in range(n)])


def added(left, right):
    return (left.astype(WIDE) + right.astype(WIDE)).astype(LOW)


def then(done, *values):
    return lax.optimization_barrier((done, values))[1]


def ring_view(values, n):
    bits = max(n.bit_length() - 3, 0)
    return values.reshape((2,) + (2,) * bits + (2, values.shape[0] // n, values.shape[1]))


def ring_half(bit, place, n):
    dims = n.bit_length()
    mine = (place // bit) % 2
    if bit == 1:
        return dims - 2, mine
    if bit == 2:
        return 0, mine
    return dims - 1 - bit.bit_length() + 1, mine ^ ((place // 2) % 2)


def pair_send(values, bit, place, n):
    dim, mine = ring_half(bit, place, n)
    return exchange(lax.dynamic_slice_in_dim(values, 1 - mine, 1, dim), bit, n)


def pair_add(values, arrived, bit, place, n):
    dim, mine = ring_half(bit, place, n)
    return added(lax.dynamic_slice_in_dim(values, mine, 1, dim), arrived)


def pair_join(mine, other, bit, place, n):
    dim, half = ring_half(bit, place, n)
    return both_halves(mine, other, half == 0, dim)


def line_place(place, n):
    count = n // 4
    up = place // 4
    return jnp.where((place // 2) % 2 == 0, up, count - 1 - up), count


def line_send(values, place, n):
    mine, count = line_place(place, n)
    blocks = values.reshape(count, values.size // count // values.shape[-1], values.shape[-1])
    return blocks, [
        exchange(lax.dynamic_index_in_dim(blocks, mine ^ k, 0, False), 4 * k, n)
        for k in range(1, count)
    ]


def line_add(blocks, arrived, place, n):
    mine, _ = line_place(place, n)
    total = lax.dynamic_index_in_dim(blocks, mine, 0, False).astype(WIDE)
    for values in arrived:
        total = total + values.astype(WIDE)
    return total.astype(LOW)


def small_sums(values, n, afters):
    bit = 1
    while bit < n:
        bits = (bit, 2 * bit, 3 * bit) if bit * 4 <= n else (bit,)
        moved = [exchange(values, b, n) for b in bits]
        if afters:
            moved = then(afters.pop(0), *moved)
        values = values + moved[0]
        if len(bits) == 3:
            values = values + (moved[1] + moved[2])
        bit *= 4
    return values


def on_device(n_batch, tokens, ln_gain, w_qkv, qk_gain, w_out, w_up, b_up, w_down, b_out,
              cotangent, slot_image, token_valid):
    rows, half = tokens.shape
    width = 2 * half
    slots = slot_image.shape[0]
    slot_rows = rows // slots
    side = lax.axis_index("head")
    first = side == 0
    place = lax.axis_index("batch")
    sides = jnp.reshape(side, (1,)).astype(jnp.int32)
    bits = []
    while 4 * 2 ** len(bits) < n_batch:
        bits.append(4 * 2 ** len(bits))

    other_tokens = swap(tokens, "head")
    (held,) = then(tokens, cotangent)
    other_cotangent = swap(held, "head")

    token_image = jnp.repeat(slot_image, slot_rows, total_repeat_length=rows)
    ids = lax.broadcasted_iota(jnp.int32, (HD, rows), 0)
    same = token_image[None, :] == ids
    query_mark = jnp.where(same, 1.0, 0.0).astype(LOW)
    key_mark = jnp.where(same & (token_valid == 1)[None, :], 0.0, FAR)
    key_mark = jnp.where(ids < slots, key_mark, 0.0).astype(LOW)
    gains = qk_gain.reshape(-1, 1)
    grad_b_out = jnp.sum(cotangent.astype(WIDE), axis=0)
    (query_mark, key_mark, gains, grad_b_out), other_tokens = lax.optimization_barrier(
        ((query_mark, key_mark, gains, grad_b_out), other_tokens)
    )

    normed, stats = input_norm(sides, tokens, other_tokens, ln_gain)
    hidden, slope = mlp_forward(normed, w_up, b_up)
    grad_first, grad_b_up, piece_first, grad_pre, piece = mlp_slope(
        sides, cotangent, other_cotangent, w_down, slope
    )
    mlp_part = mlp_weights(hidden, piece_first, normed, grad_first)
    mlp_own = ring_scatter(mlp_part, n_batch)

    def sent(part, bit):
        return pair_send(part, bit, place, n_batch)

    def summed(after, part, arrived, bit):
        (arrived,) = then(after, arrived)
        return pair_add(part, arrived, bit, place, n_batch)

    part, some = then(mlp_part, piece, normed)
    joined_t = contract(w_qkv, some, 0, 1)
    grad_t = contract(w_out, part, 1, 1).astype(LOW)
    marks = (gains, query_mark, key_mark)
    pairs = w_out.shape[0] // (2 * HD)
    joined_t, grad_t = then((joined_t, grad_t), joined_t, grad_t)
    attended, grad_joined, gain_grad = attention([joined_t], [grad_t], *marks, 0, pairs)
    heads_part = heads_weights(normed, grad_joined, piece, attended)
    heads_part = ring_view(heads_part, n_batch)
    branch = (sides, w_out, hidden, w_down, [attended])
    back = (sides, w_qkv, grad_pre, w_up, [grad_joined])
    way = sent(heads_part, 1)
    heads_part = summed(heads_part, heads_part, way, 1)
    mlp_own, heads_part = then(heads_part, mlp_own, heads_part)
    heads_own = chips_scatter(heads_part.reshape(-1, width), n_batch)
    mlp_rows = mlp_own.shape[0]
    away_in, kept_in = grad_in_terms(*then(mlp_own, *back))
    arrived_in = swap(away_in, "head")
    (mlp_own,) = then(away_in, mlp_own)
    own = lax.dynamic_update_slice(
        jnp.zeros((mlp_rows + 2 * width // n_batch, width), LOW), mlp_own, (0, 0)
    )
    away_out, kept_out = output_terms(*then(away_in, *branch))
    arrived_out = swap(away_out, "head")
    own, heads_own = then((away_out, arrived_in), own, heads_own)
    own = lax.dynamic_update_slice(own, heads_own, (mlp_rows, 0))
    whole = ring_gather(own, n_batch)

    (arrived_in,) = then(own, arrived_in)
    hat, sums, grad_ln = grad_in_hat(
        sides, kept_in, arrived_in, tokens, stats, ln_gain.reshape(1, width)
    )
    gain_grad = jnp.sum(gain_grad, axis=1).reshape(2, HD)
    joint = jnp.concatenate([sums[:, 0:2].T, gain_grad], axis=1)
    joint_other = swap(joint, "head")
    (joint_other,) = then(hat, joint_other)
    sums_other = joint_other[:, 0:rows].T
    gain_grad = (gain_grad + joint_other[:, rows:]).reshape(-1)
    small = jnp.concatenate([grad_ln[0], grad_b_out, grad_b_up[0], gain_grad])
    grad_tokens = grad_in_finish(cotangent, tokens, stats, hat, sums, sums_other)
    (arrived_out,) = then(grad_tokens, arrived_out)
    output = (
        tokens.astype(WIDE) + (kept_out + arrived_out.astype(WIDE)) + b_out
    ).astype(LOW)
    small = small_sums(small, n_batch, [grad_tokens, output])
    units = b_up.shape[0]
    (whole,) = then((output, grad_tokens, small), whole)
    grad_wd, grad_wup, grad_wqkv, grad_wo = spread(whole, n_batch, units, w_qkv.shape[1])
    return (
        output,
        grad_tokens,
        small[0:half],
        grad_wqkv,
        small[2 * half + units :].reshape(qk_gain.shape),
        grad_wo,
        grad_wup,
        small[2 * half : 2 * half + units],
        grad_wd,
        small[half : 2 * half],
    )


def solution(mesh):
    placed = (
        P("batch", "head"),
        P(),
        P(None, "head"),
        P(),
        P("head", None),
        P(None, "head"),
        P("head"),
        P("head", None),
        P("head"),
        P("batch", "head"),
        P("batch"),
        P("batch"),
    )
    return jax.shard_map(
        functools.partial(on_device, mesh.shape["batch"]),
        mesh=mesh,
        in_specs=placed,
        out_specs=(
            P("batch", "head"),
            P("batch", "head"),
            P("head"),
            P(None, "head"),
            P(),
            P("head", None),
            P(None, "head"),
            P("head"),
            P("head", None),
            P("head"),
        ),
        check_vma=False,
    )
```

```python
import functools

import jax
import jax.numpy as jnp
from jax import lax
from jax.experimental import pallas as pl
from jax.experimental.pallas import tpu as pltpu
from jax.sharding import PartitionSpec as P

HD = 64
EPSILON = 1e-06
FAR = -16384.0
LOW = jnp.bfloat16
WIDE = jnp.float32
MIB = 1024 * 1024
SHORT = pl.CostEstimate(flops=1024, bytes_accessed=1024, transcendentals=0)


def contract(left, right, left_dim, right_dim):
    return lax.dot_general(
        left, right, (((left_dim,), (right_dim,)), ((), ())), preferred_element_type=WIDE
    )


def swap(values, axis):
    return lax.ppermute(values, axis, [(0, 1), (1, 0)])


def both_halves(mine, other, first, dim):
    return jnp.where(
        first,
        jnp.concatenate([mine, other], axis=dim),
        jnp.concatenate([other, mine], axis=dim),
    )


def mlp_body(normed_ref, w_ref, b_ref, hidden_ref, slope_ref):
    pre = jnp.dot(normed_ref[...], w_ref[...], preferred_element_type=WIDE) + b_ref[...]
    cdf = 0.5 * (1.0 + lax.erf(pre * (0.5**0.5)))
    density = jnp.exp(-0.5 * pre * pre) * 0.3989422804014327
    hidden_ref[...] = (pre * cdf).astype(LOW)
    slope_ref[...] = (cdf + pre * density).astype(LOW)


def streamed(values):
    return pltpu.with_memory_space_constraint(values, pltpu.HBM)


def mlp_forward(normed, w_up, b_up):
    rows, width = normed.shape
    units = w_up.shape[1]
    block = 512
    return pl.pallas_call(
        mlp_body,
        grid=(units // block,),
        in_specs=[
            pl.BlockSpec((rows, width), lambda i: (0, 0)),
            pl.BlockSpec((width, block), lambda i: (0, i)),
            pl.BlockSpec((1, block), lambda i: (0, i)),
        ],
        out_specs=[
            pl.BlockSpec((rows, block), lambda i: (0, i)),
            pl.BlockSpec((rows, block), lambda i: (0, i)),
        ],
        out_shape=[
            jax.ShapeDtypeStruct((rows, units), LOW),
            jax.ShapeDtypeStruct((rows, units), LOW),
        ],
        compiler_params=pltpu.CompilerParams(vmem_limit_bytes=16 * MIB),
        cost_estimate=SHORT,
        name="mlp_forward",
    )(normed, streamed(w_up), b_up.reshape(1, units))


def norm_body(side_ref, mine_ref, other_ref, gain_ref, normed_ref, stats_ref):
    mine = mine_ref[...].astype(WIDE)
    other = other_ref[...].astype(WIDE)
    width = 2 * mine.shape[1]
    half = mine.shape[1]
    center = (
        jnp.sum(mine, axis=1, keepdims=True) + jnp.sum(other, axis=1, keepdims=True)
    ) / width
    mine = mine - center
    other = other - center
    spread = (
        jnp.sum(mine * mine, axis=1, keepdims=True)
        + jnp.sum(other * other, axis=1, keepdims=True)
    ) / width
    scaled = lax.rsqrt(spread + EPSILON)
    first = side_ref[0] == 0
    left = jnp.where(first, mine, other)
    right = jnp.where(first, other, mine)
    normed_ref[:, 0:half] = (left * scaled * gain_ref[:, 0:half]).astype(LOW)
    normed_ref[:, half:width] = (right * scaled * gain_ref[:, half:width]).astype(LOW)
    lane = lax.broadcasted_iota(jnp.int32, stats_ref.shape, 1)
    stats_ref[...] = jnp.where(lane == 0, center, scaled)


def input_norm(side, mine, other, gain):
    rows, half = mine.shape
    block = 224
    return pl.pallas_call(
        norm_body,
        grid_spec=pltpu.PrefetchScalarGridSpec(
            num_scalar_prefetch=1,
            grid=(rows // block,),
            in_specs=[
                pl.BlockSpec((block, half), lambda i, s: (i, 0)),
                pl.BlockSpec((block, half), lambda i, s: (i, 0)),
                pl.BlockSpec((1, 2 * half), lambda i, s: (0, 0)),
            ],
            out_specs=[
                pl.BlockSpec((block, 2 * half), lambda i, s: (i, 0)),
                pl.BlockSpec((block, 128), lambda i, s: (i, 0)),
            ],
        ),
        out_shape=[
            jax.ShapeDtypeStruct((rows, 2 * half), LOW),
            jax.ShapeDtypeStruct((rows, 128), WIDE),
        ],
        cost_estimate=SHORT,
        name="input_norm",
    )(side, mine, other, gain.reshape(1, 2 * half))


def slope_body(side_ref, mine_ref, other_ref, w_ref, slope_ref, grad_pre_ref, bias_ref, piece_ref,
               later_grad_ref, later_piece_ref):
    half = mine_ref.shape[1]
    lines = later_piece_ref.shape[0]

    @pl.when(pl.program_id(0) == 0)
    def _():
        first = side_ref[0] == 0
        mine, other = mine_ref[...], other_ref[...]
        piece_ref[:, 0:half] = jnp.where(first, mine, other)
        piece_ref[:, half:] = jnp.where(first, other, mine)

    back = lax.dot_general(
        piece_ref[...], w_ref[...], (((1,), (1,)), ((), ())), preferred_element_type=WIDE
    )
    low = (back * slope_ref[...].astype(WIDE)).astype(LOW)
    grad_pre_ref[...] = low
    later_grad_ref[...] = low
    bias_ref[...] = jnp.sum(low.astype(WIDE), axis=0, keepdims=True)
    start = pl.multiple_of(pl.program_id(0) * lines, lines)
    later_piece_ref[...] = piece_ref[pl.ds(start, lines), :]


def mlp_slope(side, mine, other, w_down, slope):
    rows, half = mine.shape
    units, width = w_down.shape
    block = 512
    lines = rows * block // units

    def whole(i, s):
        return (0, 0)

    return pl.pallas_call(
        slope_body,
        grid_spec=pltpu.PrefetchScalarGridSpec(
            num_scalar_prefetch=1,
            grid=(units // block,),
            in_specs=[
                pl.BlockSpec((rows, half), whole),
                pl.BlockSpec((rows, half), whole),
                pl.BlockSpec((block, width), lambda i, s: (i, 0)),
                pl.BlockSpec((rows, block), lambda i, s: (0, i)),
            ],
            out_specs=[
                pl.BlockSpec((rows, block), lambda i, s: (0, i)),
                pl.BlockSpec((1, block), lambda i, s: (0, i)),
                pl.BlockSpec((rows, width), whole),
                pl.BlockSpec((rows, block), lambda i, s: (0, i)),
                pl.BlockSpec((lines, width), lambda i, s: (i, 0)),
            ],
        ),
        out_shape=[
            jax.ShapeDtypeStruct((rows, units), LOW),
            jax.ShapeDtypeStruct((1, units), WIDE),
            jax.ShapeDtypeStruct((rows, width), LOW),
            pltpu.HBM((rows, units), LOW),
            pltpu.HBM((rows, width), LOW),
        ],
        compiler_params=pltpu.CompilerParams(vmem_limit_bytes=20 * MIB),
        cost_estimate=SHORT,
        name="mlp_slope",
    )(side, mine, other, w_down, slope)


def first_dims(left, right):
    return lax.dot_general(left, right, (((0,), (0,)), ((), ())), preferred_element_type=WIDE)


def mlp_weights_body(down_steps, hidden_ref, piece_ref, normed_ref, grad_pre_ref, *refs):
    step = pl.program_id(0)
    out_ref = refs[-1]

    def put(total):
        if len(refs) == 2:
            total = total + refs[0][...].astype(WIDE)
        out_ref[...] = total.astype(LOW)

    @pl.when(step < down_steps)
    def _():
        put(first_dims(hidden_ref[...], piece_ref[...]))

    @pl.when(step >= down_steps)
    def _():
        put(first_dims(normed_ref[...], grad_pre_ref[...]))


def mlp_weights(hidden, piece, normed, grad_pre, *before):
    rows, units = hidden.shape
    width = piece.shape[1]
    block = 512
    down = units // block
    across = width // block
    halves = units // width

    def later(i):
        return jnp.maximum(i - down, 0)

    return pl.pallas_call(
        functools.partial(mlp_weights_body, down),
        grid=(down + halves * across,),
        in_specs=[
            pl.BlockSpec((rows, block), lambda i: (0, jnp.minimum(i, down - 1))),
            pl.BlockSpec((rows, width), lambda i: (0, 0)),
            pl.BlockSpec((rows, block), lambda i: (0, later(i) % across)),
            pl.BlockSpec((rows, width), lambda i: (0, later(i) // across)),
        ]
        + [pl.BlockSpec((block, width), lambda i: (i, 0)) for _ in before],
        out_specs=pl.BlockSpec((block, width), lambda i: (i, 0)),
        out_shape=pltpu.HBM((2 * units, width), LOW),
        input_output_aliases={4: 0} if before else {},
        compiler_params=pltpu.CompilerParams(vmem_limit_bytes=24 * MIB),
        cost_estimate=SHORT,
        name="mlp_weights",
    )(hidden, piece, normed, grad_pre, *before)


def heads_weights_body(steps, normed_ref, piece_ref, grad_joined_ref, attended_ref, out_ref):
    width = out_ref.shape[1]
    rest = grad_joined_ref.shape[1] - width

    block = out_ref.shape[0]
    lines = pl.ds(pl.multiple_of(pl.program_id(0) % steps * block, block), block)

    @pl.when(pl.program_id(0) < steps)
    def _():
        out_ref[...] = first_dims(normed_ref[:, lines], grad_joined_ref[:, 0:width]).astype(LOW)

    @pl.when(pl.program_id(0) >= steps)
    def _():
        out_ref[:, 0:rest] = first_dims(
            normed_ref[:, lines], grad_joined_ref[:, width:]
        ).astype(LOW)
        out_ref[:, rest:] = lax.dot_general(
            piece_ref[:, lines], attended_ref[...], (((0,), (1,)), ((), ())), preferred_element_type=WIDE
        ).astype(LOW)


def heads_weights(normed, grad_joined, piece, attended_t):
    rows, width = normed.shape
    block = 512
    steps = width // block
    return pl.pallas_call(
        functools.partial(heads_weights_body, steps),
        grid=(2 * steps,),
        in_specs=[
            pl.BlockSpec(normed.shape, lambda i: (0, 0)),
            pl.BlockSpec(piece.shape, lambda i: (0, 0)),
            pl.BlockSpec(grad_joined.shape, lambda i: (0, 0)),
            pl.BlockSpec(attended_t.shape, lambda i: (0, 0)),
        ],
        out_specs=pl.BlockSpec((block, width), lambda i: (i, 0)),
        out_shape=pltpu.HBM((2 * width, width), LOW),
        compiler_params=pltpu.CompilerParams(vmem_limit_bytes=20 * MIB),
        cost_estimate=SHORT,
        name="heads_weights",
    )(normed, piece, grad_joined, attended_t)


def spread_body(mlp_ref, left_ref, right_ref, down_ref, up_ref, qkv_ref, out_ref):
    step = pl.program_id(0)
    steps = pl.num_programs(0)

    @pl.when(step < steps // 2)
    def _():
        down_ref[...] = mlp_ref[...].astype(WIDE).reshape(down_ref.shape)

    @pl.when(step >= steps // 2)
    def _():
        up_ref[...] = mlp_ref[...].astype(WIDE).reshape(up_ref.shape)

    lines, columns = qkv_ref.shape
    width = left_ref.shape[-1]
    qkv_ref[:, 0:width] = left_ref[...].astype(WIDE).reshape(lines, width)
    right = right_ref[...].astype(WIDE).reshape(lines, width)
    qkv_ref[:, width:columns] = right[:, 0 : columns - width]
    out_ref[...] = jnp.transpose(right[:, columns - width :])


def spread(whole, n, units, columns):
    width = whole.shape[1]
    mlp_rows, heads_rows = 2 * units // n, 2 * width // n
    assert whole.shape[0] == n * (mlp_rows + heads_rows) and mlp_rows % heads_rows == 0
    lines = 256
    steps = width // lines
    block = 2 * units // steps
    inner = 2 * width - columns
    across = width // block
    skip = mlp_rows // heads_rows

    def later(i):
        return jnp.maximum(i - steps // 2, 0)

    by_rows = streamed(whole.reshape(n, -1, width))
    by_parts = streamed(whole.reshape(n, -1, heads_rows, width))
    part = (n // (2 * steps), 1, heads_rows, width)
    return pl.pallas_call(
        spread_body,
        grid=(steps,),
        in_specs=[
            pl.BlockSpec((n // steps, mlp_rows, width), lambda i: (i, 0, 0)),
            pl.BlockSpec(part, lambda i: (i, skip, 0, 0)),
            pl.BlockSpec(part, lambda i: (i + steps, skip, 0, 0)),
        ],
        out_specs=[
            pl.BlockSpec((block, width), lambda i: (jnp.minimum(i, steps // 2 - 1), 0)),
            pl.BlockSpec((block, width), lambda i: (later(i) % across, later(i) // across)),
            pl.BlockSpec((lines, columns), lambda i: (i, 0)),
            pl.BlockSpec((inner, lines), lambda i: (0, i)),
        ],
        out_shape=[
            jax.ShapeDtypeStruct((units, width), WIDE),
            jax.ShapeDtypeStruct((width, units), WIDE),
            jax.ShapeDtypeStruct((width, columns), WIDE),
            jax.ShapeDtypeStruct((inner, width), WIDE),
        ],
        compiler_params=pltpu.CompilerParams(vmem_limit_bytes=32 * MIB),
        cost_estimate=SHORT,
        name="spread",
    )(by_rows, by_parts, by_parts)


def output_body(count, side_ref, w_out_ref, hidden_ref, w_down_ref, *refs):
    attended_refs, (away_ref, kept_ref) = refs[:count], refs[count:]
    step = pl.program_id(0)
    attended = jnp.concatenate([ref[...] for ref in attended_refs], axis=0)
    total = jnp.dot(
        hidden_ref[...], w_down_ref[...], preferred_element_type=WIDE
    ) + first_dims(attended, w_out_ref[...])

    @pl.when(step == 0)
    def _():
        away_ref[...] = total.astype(LOW)

    @pl.when(step == 1)
    def _():
        kept_ref[...] = total


def output_terms(side, w_out, hidden, w_down, attended_t):
    rows, units = hidden.shape
    inner, width = w_out.shape
    half = width // 2

    def column(i, s):
        return (0, s[0] ^ (1 - i))

    def whole(i, s):
        return (0, 0)

    return pl.pallas_call(
        functools.partial(output_body, len(attended_t)),
        grid_spec=pltpu.PrefetchScalarGridSpec(
            num_scalar_prefetch=1,
            grid=(2,),
            in_specs=[
                pl.BlockSpec((inner, half), column),
                pl.BlockSpec((rows, units), whole),
                pl.BlockSpec((units, half), column),
            ]
            + [pl.BlockSpec(v.shape, whole) for v in attended_t],
            out_specs=[pl.BlockSpec((rows, half), whole)] * 2,
        ),
        out_shape=[
            jax.ShapeDtypeStruct((rows, half), LOW),
            jax.ShapeDtypeStruct((rows, half), WIDE),
        ],
        compiler_params=pltpu.CompilerParams(vmem_limit_bytes=24 * MIB),
        cost_estimate=SHORT,
        name="output_terms",
    )(side, w_out, hidden, w_down, *attended_t)


def second_dims(left, right):
    return lax.dot_general(left, right, (((1,), (1,)), ((), ())), preferred_element_type=WIDE)


def grad_in_body(count, side_ref, w_qkv_ref, grad_pre_ref, w_up_ref, *refs):
    away_ref, kept_ref = refs[count:]
    step = pl.program_id(0)
    grad_joined = jnp.concatenate([ref[...] for ref in refs[:count]], axis=1)
    total = second_dims(grad_joined, w_qkv_ref[...]) + second_dims(
        grad_pre_ref[...], w_up_ref[...]
    )

    @pl.when(step == 0)
    def _():
        away_ref[...] = total.astype(LOW)

    @pl.when(step == 1)
    def _():
        kept_ref[...] = total


def grad_in_terms(side, w_qkv, grad_pre, w_up, grad_joined):
    rows, units = grad_pre.shape
    width, columns = w_qkv.shape
    half = width // 2

    def picked(i, s):
        return (s[0] ^ (1 - i), 0)

    def whole(i, s):
        return (0, 0)

    return pl.pallas_call(
        functools.partial(grad_in_body, len(grad_joined)),
        grid_spec=pltpu.PrefetchScalarGridSpec(
            num_scalar_prefetch=1,
            grid=(2,),
            in_specs=[
                pl.BlockSpec((half, columns), picked),
                pl.BlockSpec((rows, units), whole),
                pl.BlockSpec((half, units), picked),
            ]
            + [pl.BlockSpec(v.shape, whole) for v in grad_joined],
            out_specs=[pl.BlockSpec((rows, half), whole)] * 2,
        ),
        out_shape=[
            jax.ShapeDtypeStruct((rows, half), LOW),
            jax.ShapeDtypeStruct((rows, half), WIDE),
        ],
        compiler_params=pltpu.CompilerParams(vmem_limit_bytes=24 * MIB),
        cost_estimate=SHORT,
        name="grad_in_terms",
    )(side, streamed(w_qkv), grad_pre, streamed(w_up), *grad_joined)


def hat_body(side_ref, kept_ref, arrived_ref, tokens_ref, stats_ref, gain_ref,
             hat_ref, sums_ref, gain_grad_ref):
    total = kept_ref[...] + arrived_ref[...].astype(WIDE)
    stats = stats_ref[...]
    x_hat = (tokens_ref[...].astype(WIDE) - stats[:, 0:1]) * stats[:, 1:2]
    grad_hat = total * gain_ref[...]
    hat_ref[...] = grad_hat
    lane = lax.broadcasted_iota(jnp.int32, stats.shape, 1)
    sums_ref[...] = jnp.where(
        lane == 0,
        jnp.sum(grad_hat, axis=1, keepdims=True),
        jnp.sum(grad_hat * x_hat, axis=1, keepdims=True),
    )

    @pl.when(pl.program_id(0) == 0)
    def _():
        gain_grad_ref[...] = jnp.zeros_like(gain_grad_ref)

    gain_grad_ref[...] += jnp.sum(total * x_hat, axis=0, keepdims=True)


def grad_in_hat(side, kept, arrived, tokens, stats, gain):
    rows, half = tokens.shape
    block = 448

    def rows_of(columns):
        return pl.BlockSpec((block, columns), lambda i, s: (i, 0))

    return pl.pallas_call(
        hat_body,
        grid_spec=pltpu.PrefetchScalarGridSpec(
            num_scalar_prefetch=1,
            grid=(rows // block,),
            in_specs=[rows_of(half), rows_of(half), rows_of(half), rows_of(128),
                      pl.BlockSpec((1, half), lambda i, s: (0, s[0]))],
            out_specs=[rows_of(half), rows_of(128), pl.BlockSpec((1, half), lambda i, s: (0, 0))],
        ),
        out_shape=[
            jax.ShapeDtypeStruct((rows, half), WIDE),
            jax.ShapeDtypeStruct((rows, 128), WIDE),
            jax.ShapeDtypeStruct((1, half), WIDE),
        ],
        cost_estimate=SHORT,
        name="grad_in_hat",
    )(side, kept, arrived, tokens, stats, gain)


def finish_body(cotangent_ref, tokens_ref, stats_ref, hat_ref, sums_ref, other_ref, out_ref):
    width = 2 * tokens_ref.shape[1]
    scaled = stats_ref[:, 1:2]
    x_hat = (tokens_ref[...].astype(WIDE) - stats_ref[:, 0:1]) * scaled
    sums = (sums_ref[:, 0:2] + other_ref[...]) / width
    out_ref[...] = (
        cotangent_ref[...].astype(WIDE)
        + scaled * (hat_ref[...] - sums[:, 0:1] - x_hat * sums[:, 1:2])
    ).astype(LOW)


def grad_in_finish(cotangent, tokens, stats, hat, sums, other):
    rows, half = tokens.shape
    block = 224

    def rows_of(columns):
        return pl.BlockSpec((block, columns), lambda i: (i, 0))

    return pl.pallas_call(
        finish_body,
        grid=(rows // block,),
        in_specs=[rows_of(c) for c in (half, half, 128, half, 128, 2)],
        out_specs=rows_of(half),
        out_shape=jax.ShapeDtypeStruct((rows, half), LOW),
        cost_estimate=SHORT,
        name="grad_in_finish",
    )(cotangent, tokens, stats, hat, sums, other)


def part_norm(values):
    center = jnp.mean(values, axis=0, keepdims=True)
    shifted = values - center
    scaled = lax.rsqrt(jnp.mean(shifted * shifted, axis=0, keepdims=True) + EPSILON)
    return shifted * scaled, scaled


def part_norm_back(grad, normal, scaled, gain):
    g = grad * gain
    inner = jnp.mean(g * normal, axis=0, keepdims=True)
    return scaled * (g - jnp.mean(g, axis=0, keepdims=True) - normal * inner)


def lane_fold(values):
    total = values[:, 0:128]
    for start in range(128, values.shape[1], 128):
        total = total + values[:, start : start + 128]
    return total


def attention_body(rows, tiles, count, *refs):
    joined_refs, grad_refs = refs[:count], refs[count : 2 * count]
    (gain_ref, query_mark_ref, key_mark_ref, attended_ref, grad_joined_ref, gain_grad_ref,
     key_grad, value_grad) = refs[2 * count :]

    def part(some, r0, r1):
        return jnp.concatenate([ref[r0:r1, :] for ref in some], axis=1)

    factor = float(HD) ** (-0.5)
    gain_query = gain_ref[0:HD, :]
    gain_key = gain_ref[HD : 2 * HD, :]
    pieces = []
    gain_sum_query = jnp.zeros((HD, 128), WIDE)
    gain_sum_key = jnp.zeros((HD, 128), WIDE)
    one_mark = jnp.where(lax.broadcasted_iota(jnp.int32, (HD, rows), 0) < 2, 1.0, 0.0).astype(LOW)
    for head in range(2):
        base = head * 3 * HD
        query_hat, query_scale = part_norm(part(joined_refs, base, base + HD))
        key_hat, key_scale = part_norm(part(joined_refs, base + HD, base + 2 * HD))
        value_t = part(joined_refs, base + 2 * HD, base + 3 * HD).astype(LOW)
        query_t = (query_hat * gain_query).astype(LOW)
        key_t = (key_hat * gain_key).astype(LOW)
        grad_t = part(grad_refs, head * HD, (head + 1) * HD)
        query_aug = jnp.concatenate([query_t * factor, query_mark_ref[...]], axis=0)
        key_aug = jnp.transpose(jnp.concatenate([key_t, key_mark_ref[...]], axis=0))
        value_aug_t = jnp.concatenate([value_t, one_mark], axis=0)
        value_aug = jnp.transpose(value_aug_t)
        query_grads = []
        for number, (q0, q1, k0, k1) in enumerate(tiles):
            scores = jnp.dot(key_aug[k0:k1], query_aug[:, q0:q1], preferred_element_type=WIDE)
            terms = jnp.exp(scores)
            terms_low = terms.astype(LOW)
            summed = jnp.dot(value_aug_t[:, k0:k1], terms_low, preferred_element_type=WIDE)
            inverse = 1.0 / summed[HD : HD + 1, :]
            attended = summed[0:HD, :] * inverse
            attended_ref[head * HD : (head + 1) * HD, q0:q1] = attended.astype(LOW)
            grad_tile = grad_t[:, q0:q1].astype(WIDE)
            row_inner = jnp.sum(grad_tile * attended, axis=0, keepdims=True)
            inner_high = row_inner.astype(LOW)
            inner_low = (row_inner - inner_high.astype(WIDE)).astype(LOW)
            place = lax.broadcasted_iota(jnp.int32, (HD, q1 - q0), 0)
            inner_mark = jnp.where(
                place == 0,
                -inner_high.astype(WIDE),
                jnp.where(place == 1, -inner_low.astype(WIDE), 0.0),
            ).astype(LOW)
            grad_aug = jnp.concatenate([grad_t[:, q0:q1], inner_mark], axis=0)
            shifted = jnp.dot(value_aug[k0:k1], grad_aug, preferred_element_type=WIDE)
            grad_scores = (terms * shifted).astype(LOW)
            query_grads.append(
                jnp.dot(key_t[:, k0:k1], grad_scores, preferred_element_type=WIDE)
                * (inverse * factor)
            )
            query_rows = jnp.transpose(
                jnp.concatenate(
                    [query_t[:, q0:q1].astype(WIDE) * (inverse * factor), grad_tile * inverse],
                    axis=0,
                ).astype(LOW)
            )
            key_term = jnp.dot(grad_scores, query_rows, preferred_element_type=WIDE)
            value_term = jnp.dot(terms_low, query_rows, preferred_element_type=WIDE)
            if number == 0:
                key_grad[k0:k1, :] = key_term
                value_grad[k0:k1, :] = value_term
                key_grad[k1:rows, :] = jnp.zeros((rows - k1, 2 * HD), WIDE)
                value_grad[k1:rows, :] = jnp.zeros((rows - k1, 2 * HD), WIDE)
            else:
                key_grad[k0:k1, :] += key_term
                value_grad[k0:k1, :] += value_term
        lane = lax.broadcasted_iota(jnp.int32, (rows, 2 * HD), 1)
        joint = jnp.transpose(jnp.where(lane < HD, key_grad[...], value_grad[...]))
        query_grad = jnp.concatenate(query_grads, axis=1)
        key_grad_t = joint[0:HD, :]
        gain_sum_query += lane_fold(query_grad * query_hat)
        gain_sum_key += lane_fold(key_grad_t * key_hat)
        pieces += [
            part_norm_back(query_grad, query_hat, query_scale, gain_query),
            part_norm_back(key_grad_t, key_hat, key_scale, gain_key),
            joint[HD : 2 * HD, :],
        ]
    grad_joined_ref[...] = jnp.transpose(jnp.concatenate(pieces, axis=0)).astype(LOW)

    @pl.when(pl.program_id(0) == 0)
    def _():
        gain_grad_ref[...] = jnp.zeros_like(gain_grad_ref)

    gain_grad_ref[...] += jnp.concatenate([gain_sum_query, gain_sum_key], axis=0)


def attention(joined_t, grad_t, gains, query_mark, key_mark, skip, pairs):
    rows = query_mark.shape[1]
    heads = 2 * pairs
    width = heads * 3 * HD
    far = 3 * (rows // 4)
    tiles = ((0, 512, 0, far), (512, 768, 0, rows), (768, rows, far, rows))

    def whole(i):
        return (0, 0)

    return pl.pallas_call(
        functools.partial(attention_body, rows, tiles, len(joined_t)),
        grid=(heads // 2,),
        in_specs=[pl.BlockSpec((6 * HD, v.shape[1]), lambda i: (i + skip, 0)) for v in joined_t]
        + [pl.BlockSpec((2 * HD, v.shape[1]), lambda i: (i + skip, 0)) for v in grad_t]
        + [
            pl.BlockSpec((2 * HD, 1), whole),
            pl.BlockSpec((HD, rows), whole),
            pl.BlockSpec((HD, rows), whole),
        ],
        out_specs=[
            pl.BlockSpec((2 * HD, rows), lambda i: (i, 0)),
            pl.BlockSpec((rows, 6 * HD), lambda i: (0, i)),
            pl.BlockSpec((2 * HD, 128), whole),
        ],
        out_shape=[
            jax.ShapeDtypeStruct((heads * HD, rows), LOW),
            jax.ShapeDtypeStruct((rows, width), LOW),
            jax.ShapeDtypeStruct((2 * HD, 128), WIDE),
        ],
        scratch_shapes=[
            pltpu.VMEM((rows, 2 * HD), WIDE),
            pltpu.VMEM((rows, 2 * HD), WIDE),
        ],
        compiler_params=pltpu.CompilerParams(vmem_limit_bytes=20 * MIB),
        cost_estimate=SHORT,
        name="attention_both",
    )(*joined_t, *grad_t, gains, query_mark, key_mark)


def ring_order(n):
    if n % 4:
        return list(range(n))
    up = [z * 4 + c for z in range(n // 4) for c in range(2)]
    down = [z * 4 + 2 + c for z in reversed(range(n // 4)) for c in range(2)]
    return up + down


def ring_scatter(values, n):
    return lax.psum_scatter(
        values, "batch", scatter_dimension=0, tiled=True, axis_index_groups=[ring_order(n)]
    )


def chips_scatter(values, n):
    order = ring_order(n)
    groups = [order[0::2], order[1::2]]
    return lax.psum_scatter(
        values, "batch", scatter_dimension=0, tiled=True, axis_index_groups=groups
    )


def ring_gather(own, n):
    return lax.all_gather(own, "batch", axis=0, tiled=True, axis_index_groups=[ring_order(n)])


def send(values, pairs):
    return lax.ppermute(values, "batch", pairs)


def exchange(values, bit, n):
    return send(values, [(i, i ^ bit) for i in range(n)])


def added(left, right):
    return (left.astype(WIDE) + right.astype(WIDE)).astype(LOW)


def then(done, *values):
    return lax.optimization_barrier((done, values))[1]


def ring_view(values, n):
    bits = max(n.bit_length() - 3, 0)
    return values.reshape((2,) + (2,) * bits + (2, values.shape[0] // n, values.shape[1]))


def ring_half(bit, place, n):
    dims = n.bit_length()
    mine = (place // bit) % 2
    if bit == 1:
        return dims - 2, mine
    if bit == 2:
        return 0, mine
    return dims - 1 - bit.bit_length() + 1, mine ^ ((place // 2) % 2)


def pair_send(values, bit, place, n):
    dim, mine = ring_half(bit, place, n)
    return exchange(lax.dynamic_slice_in_dim(values, 1 - mine, 1, dim), bit, n)


def pair_add(values, arrived, bit, place, n):
    dim, mine = ring_half(bit, place, n)
    return added(lax.dynamic_slice_in_dim(values, mine, 1, dim), arrived)


def pair_join(mine, other, bit, place, n):
    dim, half = ring_half(bit, place, n)
    return both_halves(mine, other, half == 0, dim)


def line_place(place, n):
    count = n // 4
    up = place // 4
    return jnp.where((place // 2) % 2 == 0, up, count - 1 - up), count


def line_send(values, place, n):
    mine, count = line_place(place, n)
    blocks = values.reshape(count, values.size // count // values.shape[-1], values.shape[-1])
    return blocks, [
        exchange(lax.dynamic_index_in_dim(blocks, mine ^ k, 0, False), 4 * k, n)
        for k in range(1, count)
    ]


def line_add(blocks, arrived, place, n):
    mine, _ = line_place(place, n)
    total = lax.dynamic_index_in_dim(blocks, mine, 0, False).astype(WIDE)
    for values in arrived:
        total = total + values.astype(WIDE)
    return total.astype(LOW)


def small_sums(values, n, afters):
    bit = 1
    while bit < n:
        bits = (bit, 2 * bit, 3 * bit) if bit * 4 <= n else (bit,)
        moved = [exchange(values, b, n) for b in bits]
        if afters:
            moved = then(afters.pop(0), *moved)
        values = values + moved[0]
        if len(bits) == 3:
            values = values + (moved[1] + moved[2])
        bit *= 4
    return values


def on_device(n_batch, tokens, ln_gain, w_qkv, qk_gain, w_out, w_up, b_up, w_down, b_out,
              cotangent, slot_image, token_valid):
    rows, half = tokens.shape
    width = 2 * half
    slots = slot_image.shape[0]
    slot_rows = rows // slots
    side = lax.axis_index("head")
    first = side == 0
    place = lax.axis_index("batch")
    sides = jnp.reshape(side, (1,)).astype(jnp.int32)
    bits = []
    while 4 * 2 ** len(bits) < n_batch:
        bits.append(4 * 2 ** len(bits))

    other_tokens = swap(tokens, "head")
    (held,) = then(tokens, cotangent)
    other_cotangent = swap(held, "head")

    token_image = jnp.repeat(slot_image, slot_rows, total_repeat_length=rows)
    ids = lax.broadcasted_iota(jnp.int32, (HD, rows), 0)
    same = token_image[None, :] == ids
    query_mark = jnp.where(same, 1.0, 0.0).astype(LOW)
    key_mark = jnp.where(same & (token_valid == 1)[None, :], 0.0, FAR)
    key_mark = jnp.where(ids < slots, key_mark, 0.0).astype(LOW)
    gains = qk_gain.reshape(-1, 1)
    grad_b_out = jnp.sum(cotangent.astype(WIDE), axis=0)
    (query_mark, key_mark, gains, grad_b_out), other_tokens = lax.optimization_barrier(
        ((query_mark, key_mark, gains, grad_b_out), other_tokens)
    )

    normed, stats = input_norm(sides, tokens, other_tokens, ln_gain)
    hidden, slope = mlp_forward(normed, w_up, b_up)
    grad_first, grad_b_up, piece_first, grad_pre, piece = mlp_slope(
        sides, cotangent, other_cotangent, w_down, slope
    )
    mlp_part = mlp_weights(hidden, piece_first, normed, grad_first)
    mlp_own = ring_scatter(mlp_part, n_batch)

    def sent(part, bit):
        return pair_send(part, bit, place, n_batch)

    def summed(after, part, arrived, bit):
        (arrived,) = then(after, arrived)
        return pair_add(part, arrived, bit, place, n_batch)

    part, some = then(mlp_part, piece, normed)
    joined_t = contract(w_qkv, some, 0, 1)
    grad_t = contract(w_out, part, 1, 1).astype(LOW)
    marks = (gains, query_mark, key_mark)
    pairs = w_out.shape[0] // (2 * HD)
    joined_t, grad_t = then((joined_t, grad_t), joined_t, grad_t)
    attended, grad_joined, gain_grad = attention([joined_t], [grad_t], *marks, 0, pairs)
    heads_part = heads_weights(normed, grad_joined, piece, attended)
    heads_part = ring_view(heads_part, n_batch)
    branch = (sides, w_out, hidden, w_down, [attended])
    back = (sides, w_qkv, grad_pre, w_up, [grad_joined])
    way = sent(heads_part, 1)
    heads_part = summed(heads_part, heads_part, way, 1)
    mlp_own, heads_part = then(heads_part, mlp_own, heads_part)
    heads_own = chips_scatter(heads_part.reshape(-1, width), n_batch)
    mlp_rows = mlp_own.shape[0]
    away_in, kept_in = grad_in_terms(*then(mlp_own, *back))
    arrived_in = swap(away_in, "head")
    (mlp_own,) = then(away_in, mlp_own)
    own = lax.dynamic_update_slice(
        jnp.zeros((mlp_rows + 2 * width // n_batch, width), LOW), mlp_own, (0, 0)
    )
    away_out, kept_out = output_terms(*then(away_in, *branch))
    arrived_out = swap(away_out, "head")
    own, heads_own = then((away_out, arrived_in), own, heads_own)
    own = lax.dynamic_update_slice(own, heads_own, (mlp_rows, 0))
    whole = ring_gather(own, n_batch)

    (arrived_in,) = then(own, arrived_in)
    hat, sums, grad_ln = grad_in_hat(
        sides, kept_in, arrived_in, tokens, stats, ln_gain.reshape(1, width)
    )
    gain_grad = jnp.sum(gain_grad, axis=1).reshape(2, HD)
    joint = jnp.concatenate([sums[:, 0:2].T, gain_grad], axis=1)
    joint_other = swap(joint, "head")
    (joint_other,) = then(hat, joint_other)
    sums_other = joint_other[:, 0:rows].T
    gain_grad = (gain_grad + joint_other[:, rows:]).reshape(-1)
    small = jnp.concatenate([grad_ln[0], grad_b_out, grad_b_up[0], gain_grad])
    grad_tokens = grad_in_finish(cotangent, tokens, stats, hat, sums, sums_other)
    (arrived_out,) = then(grad_tokens, arrived_out)
    output = (
        tokens.astype(WIDE) + (kept_out + arrived_out.astype(WIDE)) + b_out
    ).astype(LOW)
    small = small_sums(small, n_batch, [grad_tokens, output])
    units = b_up.shape[0]
    (whole,) = then((output, grad_tokens, small), whole)
    grad_wd, grad_wup, grad_wqkv, grad_wo = spread(whole, n_batch, units, w_qkv.shape[1])
    return (
        output,
        grad_tokens,
        small[0:half],
        grad_wqkv,
        small[2 * half + units :].reshape(qk_gain.shape),
        grad_wo,
        grad_wup,
        small[2 * half : 2 * half + units],
        grad_wd,
        small[half : 2 * half],
    )


def solution(mesh):
    placed = (
        P("batch", "head"),
        P(),
        P(None, "head"),
        P(),
        P("head", None),
        P(None, "head"),
        P("head"),
        P("head", None),
        P("head"),
        P("batch", "head"),
        P("batch"),
        P("batch"),
    )
    return jax.shard_map(
        functools.partial(on_device, mesh.shape["batch"]),
        mesh=mesh,
        in_specs=placed,
        out_specs=(
            P("batch", "head"),
            P("batch", "head"),
            P("head"),
            P(None, "head"),
            P(),
            P("head", None),
            P(None, "head"),
            P("head"),
            P("head", None),
            P("head"),
        ),
        check_vma=False,
    )
```
